32 devices in a mesh: tm: 8 (over y, x, core), space: 4 (over z).
Axes of the slice: x: 2, y: 2, z: 4, core: 2. Of those that a mesh axis runs over, the one named last changes fastest.
Arguments:
- node_fields: float32 [8, 5, 32, 128, 128], P('tm', None, 'space'), may hold values from -6 to 6
- region_label: int32 [32, 128, 128], P('space'), may hold values from 0 to 3
- sheet_shift: int32 [8, 128], P('tm'), may hold values from 0 to 1
- diffusivity: float32 [4], replicated, may hold values from 0.02 to 0.15
Outputs:
- updated_nodes: float32 [8, 5, 32, 128, 128], P('tm', None, 'space')
The draws below stay inside these ranges and needn't reach their ends.
All inputs are finite; a program needn't handle non-finite values.
Results may differ from the reference program's by a relative error of at most 0.00002.
Values sent between devices are 32-bit elements; how exact they have to be, the bound alone decides.
A program may use at most 64 MiB of HBM per device.

```python
import math
import jax
import jax.numpy as jnp
import numpy as np
from jax import lax

NX = 128
NY = 128
NODES = 5
REGIONS = 4
FINE_SWEEPS = 2
SLICES = 8
NZ = 32


def touch_ends(values, key, low, largest):
    dims = values.shape
    spot = [jax.random.randint(jax.random.fold_in(key, axis), (), 0, dims[axis]) for axis in range(len(dims))]
    values = values.at[tuple(spot)].set(low)
    longest = dims.index(max(dims))
    spot[longest] = (spot[longest] + 1) % dims[longest]
    return values.at[tuple(spot)].set(largest)


def level_of(rng, dims, cuts, low, top_value):
    gain, own = 1.0, jax.random.fold_in(rng, 6)
    for axis_at, blocks in cuts:
        steps = jnp.exp(jax.random.uniform(jax.random.fold_in(own, axis_at), (blocks,), jnp.float32, low / len(cuts), top_value / len(cuts)))
        gain = gain * jnp.repeat(steps, dims[axis_at] // blocks).reshape([-1 if axis == axis_at else 1 for axis in range(len(dims))])
    return gain


def gaussian(own_key, dims, scale, bound, shards=(), dtype=jnp.bfloat16):
    drawn = jax.random.normal(own_key, dims, jnp.float32) * scale
    if len(shards) > 0:
        drawn = level_of(own_key, dims, shards, -0.22, 0.18) * drawn
    return jnp.clip(drawn, min=-bound, max=bound).astype(dtype)


def setup_inputs(seed: int = 0) -> dict:
    arg_keys = jax.random.split(jax.random.key(seed), 5)
    node_fields = gaussian(arg_keys[0], (SLICES, NODES, NZ, NX, NY), 1.0, 6.0, ((0, 8), (2, 4)), jnp.float32)
    region_label = touch_ends(jax.random.randint(arg_keys[1], (NZ, NX, NY), 0, REGIONS), jax.random.fold_in(arg_keys[1], 1), 0, REGIONS - 1).astype(jnp.int32)
    sheet_shift = touch_ends(jax.random.randint(arg_keys[2], (SLICES, NY), 0, 2), jax.random.fold_in(arg_keys[2], 1), 0, 1).astype(jnp.int32)
    diffusivity = jnp.clip(jnp.exp(jax.random.uniform(arg_keys[3], (REGIONS,), jnp.float32, math.log(0.02), math.log(0.15))), 0.02, 0.15)
    return dict(node_fields=node_fields, region_label=region_label, sheet_shift=sheet_shift, diffusivity=diffusivity)


slice_length = 1.0

def node_tables():
    radius = math.sqrt(3.0 / 7.0)
    points = [0.0, (1.0 - radius) / 2.0, 0.5, (1.0 + radius) / 2.0, 1.0]
    integrals = np.zeros((4, 5))
    for column in range(5):
        coeffs = [1.0]
        divisor = 1.0
        for other in range(5):
            if other != column:
                anchor = points[other]
                product = [0.0] * (len(coeffs) + 1)
                for degree in range(len(coeffs)):
                    product[degree + 1] = product[degree + 1] + coeffs[degree]
                    product[degree] = product[degree] - anchor * coeffs[degree]
                coeffs = product
                divisor = divisor * (points[column] - anchor)
        for row in range(4):
            bottom = points[row]
            summit = points[row + 1]
            amount = 0.0
            for degree in range(len(coeffs)):
                amount = amount + coeffs[degree] / (degree + 1) * (summit ** (degree + 1) - bottom ** (degree + 1))
            integrals[row, column] = amount / divisor
    return (np.array(points), integrals)

def combine(coefficients, stack):
    total = float(coefficients[0]) * stack[0]
    for index in range(1, len(coefficients)):
        total = total + float(coefficients[index]) * stack[index]
    return total

def lookup(labels, table):
    result = jnp.zeros(labels.shape, jnp.float32)
    for region in range(table.shape[0]):
        result = result + jnp.where(labels == region, table[region], 0.0)
    return result

def restrict(field):
    shape = field.shape
    blocks = field.reshape(shape[:-3] + (shape[-3] // 4, 4, shape[-2] // 2, 2, shape[-1]))
    return lax.optimization_barrier(jnp.mean(blocks, axis=(-4, -2)))

def prolong(coarse):
    return jnp.repeat(jnp.repeat(coarse, 4, axis=-3), 2, axis=-2)

def pad_rows(field):
    return jnp.pad(field, [(0, 0)] * (field.ndim - 3) + [(1, 1), (0, 0), (0, 0)])

def neighbours(padded):
    center = padded[..., 1:-1, :, :]
    vertical = padded[..., 2:, :, :] + padded[..., :-2, :, :]
    across = jnp.roll(center, 1, -2) + jnp.roll(center, -1, -2)
    sideways = jnp.pad(center, [(0, 0)] * (center.ndim - 1) + [(1, 1)])
    lateral = sideways[..., 2:] + sideways[..., :-2]
    return (center, vertical, across, lateral)

def fine_rate(padded, kappa, advect):
    center, vertical, across, lateral = neighbours(padded)
    diffusion = kappa * (vertical + across + lateral - 6.0 * center)
    return diffusion - advect * (center - jnp.roll(center, 1, -2))

def coarse_rate(padded, kappa, advect):
    center, vertical, across, lateral = neighbours(padded)
    diffusion = kappa * ((vertical - 2.0 * center) / 16.0 + (across - 2.0 * center) / 4.0 + (lateral - 2.0 * center))
    return diffusion - 0.5 * advect * (center - jnp.roll(center, 1, -2))

def coarse_advance(initial, padded, kappa, advect, constant):
    return initial + slice_length * coarse_rate(padded, kappa, advect) + constant

def apply_correction(fields, delta_start, delta_end):
    times_table, integral_table = node_tables()
    pieces = []
    for node in range(NODES):
        weight = float(times_table[node])
        pieces.append(fields[node] + prolong((1.0 - weight) * delta_start + weight * delta_end))
    return jnp.stack(pieces)

def fine_sweeps(corrected, rates, kappa, advect, rims):
    times_table, integral_table = node_tables()
    old_values, old_rates = (corrected, rates)
    for sweep in range(FINE_SWEEPS):
        values = [old_values[0]]
        new_rates = [old_rates[0]]
        for node in range(NODES - 1):
            spacing = float(times_table[node + 1] - times_table[node]) * slice_length
            value = values[node] + spacing * (new_rates[node] - old_rates[node]) + slice_length * combine(integral_table[node], old_rates)
            values.append(value)
            if node < NODES - 2 or sweep < FINE_SWEEPS - 1:
                new_rates.append(fine_rate(rims(value[None]), kappa, advect)[0])
        old_values = jnp.stack(values)
        if sweep < FINE_SWEEPS - 1:
            old_rates = jnp.stack(new_rates)
    return old_values

def reference(node_fields, region_label, sheet_shift, diffusivity):
    times_table, integral_table = node_tables()
    weight_table = integral_table.sum(axis=0)
    kappa = lookup(region_label, diffusivity)
    kappa_coarse = restrict(kappa)
    advects = sheet_shift.astype(jnp.float32) / slice_length
    previous = jnp.concatenate([node_fields[0:1, 0], node_fields[:-1, NODES - 1]], 0)

    def prepare(inputs):
        fields, start, advect = inputs
        fields = jnp.concatenate([start[None], fields[1:]], 0)
        rates = fine_rate(pad_rows(fields), kappa, advect)
        coarse_start = restrict(start)
        moved = restrict(slice_length * combine(weight_table, rates))
        constant = moved - slice_length * coarse_rate(pad_rows(coarse_start), kappa_coarse, advect)
        return (coarse_start, constant)
    coarse_starts, constants = lax.map(prepare, (node_fields, previous, advects))

    def chain(carry, inputs):
        constant, advect = inputs
        ending = coarse_advance(carry, pad_rows(carry), kappa_coarse, advect, constant)
        return (ending, (carry, ending))
    finished, (begins, endings) = lax.scan(chain, coarse_starts[0], (constants, advects))

    def finish(inputs):
        fields, start, advect, begin, ending, coarse_start = inputs
        fields = jnp.concatenate([start[None], fields[1:]], 0)
        corrected = apply_correction(fields, begin - coarse_start, ending - restrict(fields[NODES - 1]))
        rates = fine_rate(pad_rows(corrected), kappa, advect)
        return fine_sweeps(corrected, rates, kappa, advect, pad_rows)
    return lax.map(finish, (node_fields, previous, advects, begins, endings, coarse_starts))
```

```python
import math

import jax
import jax.numpy as jnp
import numpy as np
from jax import lax
from jax.experimental import pallas as pl
from jax.experimental.pallas import tpu as pltpu
from jax.sharding import PartitionSpec as P

NODES = 5
FINE_SWEEPS = 2
BLOCK_Z = 4
BLOCK_X = 2
PAD = 8
PIECES = 4
MESH = pl.DeviceIdType.MESH

slice_length = 1.0


def node_tables():
    radius = math.sqrt(3.0 / 7.0)
    points = [0.0, (1.0 - radius) / 2.0, 0.5, (1.0 + radius) / 2.0, 1.0]
    integrals = np.zeros((4, 5))
    for column in range(5):
        coeffs = [1.0]
        divisor = 1.0
        for other in range(5):
            if other != column:
                anchor = points[other]
                product = [0.0] * (len(coeffs) + 1)
                for degree in range(len(coeffs)):
                    product[degree + 1] = product[degree + 1] + coeffs[degree]
                    product[degree] = product[degree] - anchor * coeffs[degree]
                coeffs = product
                divisor = divisor * (points[column] - anchor)
        for row in range(4):
            bottom = points[row]
            summit = points[row + 1]
            amount = 0.0
            for degree in range(len(coeffs)):
                amount = amount + coeffs[degree] / (degree + 1) * (
                    summit ** (degree + 1) - bottom ** (degree + 1)
                )
            integrals[row, column] = amount / divisor
    return (np.array(points), integrals)


TIMES, INTEGRALS = node_tables()
WEIGHTS = INTEGRALS.sum(axis=0)
STEPS = NODES - 1
REACH = FINE_SWEEPS * STEPS
EXCHANGES = 3 + REACH
FIRST = EXCHANGES - 1
GAPS = TIMES[1:] - TIMES[:-1]
LATE = (INTEGRALS * TIMES).sum(axis=1)
EARLY = INTEGRALS.sum(axis=1) - LATE
CHAIN_SLOTS = REACH - 1


class Transfer:
    def __init__(self, src, dst, send_sem, recv_sem, device, sends, receives):
        self.copy = pltpu.make_async_remote_copy(
            src_ref=src,
            dst_ref=dst,
            send_sem=send_sem,
            recv_sem=recv_sem,
            device_id=device,
            device_id_type=MESH,
        )
        self.sends, self.receives = sends, receives

    def start(self):
        pl.when(self.sends)(self.copy.start)

    def wait_recv(self):
        pl.when(self.receives)(self.copy.wait_recv)

    def wait_send(self):
        pl.when(self.sends)(self.copy.wait_send)


def kernel(
    fields_in, label_in, shift_in, table_in, out, fields, label, shift, table,
    kappa, kappa_c, start, rim, moved, shift_next, below, pads, mids, gain, lift, delta, fold,
    spread, base, grid, nodes, latest,
    halo_send, halo_recv, time_send, time_recv, wide_send, wide_recv, label_send, label_recv, load_sem,
):
    n, s = lax.axis_index("tm"), lax.axis_index("space")
    slices, slabs = lax.axis_size("tm"), lax.axis_size("space")
    depth, width, height = fields.shape[1:]
    rows_c = width // BLOCK_X
    depth_c = depth // BLOCK_Z
    near = -(-REACH // depth)
    own, own_c = near * depth, near * depth_c
    layers, layers_c = (2 * near + 1) * depth, (2 * near + 1) * depth_c
    chunk = min(64, width)
    piece = width // PIECES
    last = NODES - 1
    has_prev, has_next = n > 0, n < slices - 1
    has_low, has_high = s > 0, s < slabs - 1
    inner = pl.ds(PAD, width)
    here_c = pl.ds(own_c, depth_c)

    loads = [
        pltpu.make_async_copy(fields_in.at[node], fields.at[node], load_sem.at[node])
        for node in range(NODES)
    ]
    loads += [
        pltpu.make_async_copy(label_in, label.at[pl.ds(own, depth)], load_sem.at[NODES]),
        pltpu.make_async_copy(shift_in, shift, load_sem.at[NODES + 1]),
        pltpu.make_async_copy(table_in, table, load_sem.at[NODES + 2]),
    ]
    for load in loads:
        load.start()

    barrier = pltpu.get_barrier_semaphore()
    met = jnp.int32(0)
    for dn in (-1, 0, 1):
        span = near if dn == 0 else 1
        for ds in range(-span, span + 1):
            if dn == 0 and ds == 0:
                continue
            there = (n + dn >= 0) & (n + dn < slices) & (s + ds >= 0) & (s + ds < slabs)

            @pl.when(there)
            def _(dn=dn, ds=ds):
                pl.semaphore_signal(
                    barrier, inc=1, device_id={"tm": n + dn, "space": s + ds}, device_id_type=MESH
                )

            met = met + there.astype(jnp.int32)
    pl.semaphore_wait(barrier, met)

    shipped = []

    def send(transfer):
        transfer.start()
        shipped.append(transfer)
        return transfer

    def halo(index, source=None):
        buf = pads.at[index]
        pieces = []
        for k in range(PIECES):
            rows = pl.ds(PAD + k * piece, piece)
            if source is None:
                low, high = buf.at[1, rows], buf.at[depth, rows]
            else:
                low, high = (source.at[z, pl.ds(k * piece, piece)] for z in (0, depth - 1))
            sem = 2 * (index * PIECES + k)
            up = Transfer(
                high, buf.at[0, rows], halo_send.at[sem], halo_recv.at[sem],
                {"space": s + 1}, has_high, has_low,
            )
            down = Transfer(
                low, buf.at[depth + 1, rows], halo_send.at[sem + 1], halo_recv.at[sem + 1],
                {"space": s - 1}, has_low, has_high,
            )
            pieces.append((down, up))
        return pieces

    def arrive(pieces):
        for down, up in pieces:
            down.wait_recv()
            up.wait_recv()

    def time_hop(index, src, dst, ds=0):
        to = {"tm": n + 1} if ds == 0 else {"tm": n + 1, "space": s + ds}
        goes = has_next if ds == 0 else has_next & (s + ds >= 0) & (s + ds < slabs)
        comes = has_prev if ds == 0 else has_prev & (s - ds >= 0) & (s - ds < slabs)
        return Transfer(src, dst, time_send.at[index], time_recv.at[index], to, goes, comes)

    within = {
        distance: (s + distance >= 0) & (s + distance < slabs)
        for distance in range(-near, near + 1)
    }

    shift_hop = Transfer(
        shift_in, shift_next, time_send.at[0], time_recv.at[0], {"tm": n - 1}, has_prev, has_next
    )
    send(shift_hop)
    end_halo = halo(1, fields_in.at[last])
    for down, up in end_halo:
        send(down)
        send(up)
    rim_hops = [
        send(time_hop(6, fields_in.at[last, depth - 1], rim.at[0], 1)),
        send(time_hop(7, fields_in.at[last, 0], rim.at[1], -1)),
    ]
    start_hop = send(time_hop(1, fields_in.at[last], start))

    label_hops = []
    for distance in range(1, near + 1):
        for z in range(depth):
            for sign in (1, -1):
                there = own - sign * distance * depth + z
                sem = 2 * ((distance - 1) * depth + z) + (sign + 1) // 2
                label_hops.append(
                    Transfer(
                        label_in.at[z], label.at[there], label_send.at[sem], label_recv.at[sem],
                        {"space": s + sign * distance}, within[sign * distance], within[-sign * distance],
                    )
                )
    label_queue = list(label_hops)

    def send_labels(count):
        for transfer in label_queue[:count]:
            send(transfer)
        del label_queue[:count]

    wide_hops = []
    for field in range(2):
        for distance in range(1, near + 1):
            for sign in (1, -1):
                there = pl.ds(own_c - sign * distance * depth_c, depth_c)
                sem = 2 * (field * near + distance - 1) + (sign + 1) // 2
                wide_hops.append(
                    Transfer(
                        delta.at[field, here_c], delta.at[field, there], wide_send.at[sem], wide_recv.at[sem],
                        {"space": s + sign * distance}, within[sign * distance], within[-sign * distance],
                    )
                )

    first_slice = (n == 0).astype(jnp.float32)

    def sideways(center):
        lane = lax.broadcasted_iota(jnp.int32, center.shape, 1)
        return jnp.where(lane == height - 1, 0.0, pltpu.roll(center, height - 1, 1)) + jnp.where(
            lane == 0, 0.0, pltpu.roll(center, 1, 1)
        )

    def slope(buf, layer, r, advect, weight, rows):
        center = buf[layer, pl.ds(PAD + r, rows)]
        behind = buf[layer, pl.ds(PAD - 1 + r, rows)]
        total = buf[layer - 1, pl.ds(PAD + r, rows)] + buf[layer + 1, pl.ds(PAD + r, rows)]
        total = total + (behind + buf[layer, pl.ds(PAD + 1 + r, rows)])
        total = total + sideways(center) - 6.0 * center
        return weight * total - advect * (center - behind)

    def rate(index, z, r, advect, chunk=chunk):
        return slope(pads.at[index], z + 1, r, advect, kappa[own + z, pl.ds(r, chunk)], chunk)

    def place(buf, layer, r, value):
        rows = value.shape[0]
        buf[layer, pl.ds(PAD + r, rows)] = value
        if r == 0:
            buf[layer, pl.ds(PAD + width, 1)] = value[:1]
        if r + rows == width:
            buf[layer, pl.ds(PAD - 1, 1)] = value[rows - 1 :]

    def fill(index, z, r, value):
        place(pads.at[index], z + 1, r, value)

    def each(lo, hi, body):
        def turn(z, carry):
            for r in range(0, width, chunk):
                body(z, r, chunk)
            return carry

        lax.fori_loop(lo, hi, turn, 0)

    def edges(body, needs=None, gives=None):
        for k in range(PIECES):
            if needs is not None:
                arrive(needs[k : k + 1])
            body(0, k * piece, piece)
            body(depth - 1, k * piece, piece)
            if gives is not None:
                send(gives[k][0])
                send(gives[k][1])

    def interior(body):
        each(1, depth - 1, body)

    def combine(coefficients, first, z, r, chunk):
        at = pl.ds(r, chunk)
        total = (first_slice * float(coefficients[0])) * fields[0, z, at] if first is None else first
        for node in range(1, NODES):
            total = total + float(coefficients[node]) * fields[node, z, at]
        return total

    def weigh(z, r, chunk):
        fill(0, z, r, combine(slice_length * WEIGHTS, None, z, r, chunk))

    def foresee(z, r, chunk):
        fill(FIRST, z, r, combine(slice_length * INTEGRALS[0], None, z, r, chunk))

    for load in loads:
        load.wait()
    weighted_halo = halo(0)
    edges(weigh, None, weighted_halo)
    first_halo = halo(FIRST)
    edges(foresee, None, first_halo)
    interior(weigh)

    def look_up(layer, r, chunk):
        at = pl.ds(r, chunk)
        labels = label[layer, at]
        total = jnp.zeros((chunk, height), jnp.float32)
        for region in range(table.shape[0]):
            total = total + jnp.where(labels == region, table[region], 0.0)
        kappa[layer, at] = total

    def prepare(z, r, chunk):
        fill(1, z, r, fields[last, z, pl.ds(r, chunk)])
        look_up(own + z, r, chunk)

    each(0, depth, prepare)

    for index in range(EXCHANGES):

        @pl.when(jnp.logical_not(has_low))
        def _(index=index):
            pads[index, 0, inner] = jnp.zeros((width, height), jnp.float32)

        @pl.when(jnp.logical_not(has_high))
        def _(index=index):
            pads[index, depth + 1, inner] = jnp.zeros((width, height), jnp.float32)

    def restrict(target, layer_of):
        def turn(zc, carry):
            for r in range(0, width, chunk):
                total = layer_of(BLOCK_Z * zc, r)
                for k in range(1, BLOCK_Z):
                    total = total + layer_of(BLOCK_Z * zc + k, r)
                fold[pl.ds(r, chunk)] = total
            total = fold[pl.ds(0, rows_c, stride=BLOCK_X)]
            for k in range(1, BLOCK_X):
                total = total + fold[pl.ds(k, rows_c, stride=BLOCK_X)]
            target[zc] = total * (1.0 / (BLOCK_Z * BLOCK_X))
            return carry

        lax.fori_loop(0, depth_c, turn, 0)

    advect = shift[...].astype(jnp.float32) / slice_length

    arrive(weighted_halo)
    restrict(
        gain,
        lambda z, r: first_slice * fields[0, z, pl.ds(r, chunk)]
        - fields[last, z, pl.ds(r, chunk)]
        + slice_length * rate(0, z, r, advect),
    )
    restrict(kappa_c, lambda z, r: kappa[own + z, pl.ds(r, chunk)])

    @pl.when(jnp.logical_not(has_prev))
    def _():
        moved[...] = jnp.zeros_like(moved)
        delta[0, here_c] = jnp.zeros((depth_c, rows_c, height), jnp.float32)
        below[...] = jnp.zeros_like(below)

    @pl.when(has_prev & jnp.logical_not(has_low))
    def _():
        below[0] = jnp.zeros((rows_c, height), jnp.float32)

    @pl.when(has_prev & jnp.logical_not(has_high))
    def _():
        below[1] = jnp.zeros((rows_c, height), jnp.float32)

    for distance in range(1, near + 1):
        for sign in (1, -1):

            @pl.when(jnp.logical_not(within[sign * distance]))
            def _(distance=distance, sign=sign):
                there = own_c + sign * distance * depth_c
                delta[:, pl.ds(there, depth_c)] = jnp.zeros((2, depth_c, rows_c, height), jnp.float32)

    lift_hop = time_hop(2, lift, moved)
    body_hop = time_hop(3, delta.at[1, here_c], delta.at[0, here_c])
    up_hop = time_hop(4, delta.at[1, own_c + depth_c - 1], below.at[0], 1)
    down_hop = time_hop(5, delta.at[1, own_c], below.at[1], -1)
    shipped.extend([body_hop, up_hop, down_hop] + wide_hops)

    def chain():
        lift_hop.wait_recv()
        body_hop.wait_recv()
        up_hop.wait_recv()
        down_hop.wait_recv()
        for zc in range(depth_c):
            center = delta[0, own_c + zc]
            under = below[0] if zc == 0 else delta[0, own_c + zc - 1]
            over = below[1] if zc == depth_c - 1 else delta[0, own_c + zc + 1]
            behind = pltpu.roll(center, 1, 0)
            across = behind + pltpu.roll(center, rows_c - 1, 0)
            lateral = sideways(center)
            spreading = kappa_c[zc] * (
                (under + over - 2.0 * center) * (1.0 / (BLOCK_Z * BLOCK_Z))
                + (across - 2.0 * center) * (1.0 / (BLOCK_X * BLOCK_X))
                + (lateral - 2.0 * center)
            )
            flow = (1.0 / BLOCK_X) * advect * (center - behind)
            delta[1, own_c + zc] = center + slice_length * (spreading - flow) + (gain[zc] + moved[zc])
            if zc == 0:
                down_hop.start()
            if zc == depth_c - 1:
                up_hop.start()
        body_hop.start()
        for transfer in wide_hops:
            transfer.start()

    pl.when(n == 0)(chain)

    shift_hop.wait_recv()
    arrive(end_halo)
    advect_next = shift_next[...].astype(jnp.float32) / slice_length
    restrict(
        lift,
        lambda z, r: fields[last, z, pl.ds(r, chunk)]
        + (slice_length * float(WEIGHTS[0])) * rate(1, z, r, advect_next),
    )
    send(lift_hop)

    @pl.when(jnp.logical_not(has_prev))
    def _():
        def turn(z, carry):
            start[z] = fields[0, z]
            return carry

        lax.fori_loop(0, depth, turn, 0)
        rim[...] = jnp.zeros_like(rim)

    for end, there in enumerate((has_low, has_high)):

        @pl.when(has_prev & jnp.logical_not(there))
        def _(end=end):
            rim[end] = jnp.zeros((width, height), jnp.float32)

    start_hop.wait_recv()
    rim_hops[0].wait_recv()
    rim_hops[1].wait_recv()
    begin_weight = slice_length * float(INTEGRALS[0, 0])

    def combine_start(z, r, chunk):
        fill(2, z, r, combine(slice_length * INTEGRALS[0], begin_weight * start[z, pl.ds(r, chunk)], z, r, chunk))

    each(0, depth, combine_start)
    arrive(first_halo)
    for end, layer in ((0, 0), (1, depth + 1)):
        for r in range(0, width, chunk):
            at = pl.ds(PAD + r, chunk)
            pads[2, layer, at] = pads[FIRST, layer, at] + begin_weight * rim[end, pl.ds(r, chunk)]

    def fine_step(sweep, step, needs):
        old = fields if sweep == 0 else mids
        new = mids if sweep == 0 else None
        offset = 0 if sweep == 0 else -1
        index = 2 + sweep * STEPS + step
        final = sweep == FINE_SWEEPS - 1
        more = not (final and step == STEPS - 1)

        def advance(z, r, chunk):
            at = pl.ds(r, chunk)
            if step == 0:
                before = start[z, at]
            else:
                before = out[step, z, at] if final else new[step - 1, z, at]
            value = before + rate(index, z, r, advect, chunk)
            if final:
                out[step + 1, z, at] = value
            else:
                new[step, z, at] = value
            if not more:
                return
            if step < STEPS - 1:
                total = slice_length * float(GAPS[step + 1]) * (value - old[step + 1 + offset, z, at])
                row, source, shown, known = step + 1, old, offset, {}
            else:
                total, row, source, shown, known = None, 0, new, -1, {STEPS: value}
            for node in range(NODES):
                if node == 0:
                    part = start[z, at]
                else:
                    part = known[node] if node in known else source[node + shown, z, at]
                term = (slice_length * float(INTEGRALS[row, node])) * part
                total = term if total is None else total + term
            fill(index + 1, z, r, total)

        following = halo(index + 1) if more else None
        edges(advance, needs, following)
        return following, lambda: interior(advance)

    pair = None
    quota = -(-len(label_hops) // (2 * STEPS - 4))
    for stage in range(REACH - 2):
        if stage > 0:
            waiting = (n == stage) if stage < CHAIN_SLOTS else (n >= stage)
            pl.when(waiting)(chain)
        pair, rest = fine_step(stage // STEPS, stage % STEPS, pair)
        send_labels(quota)
        rest()

    for transfer in label_hops:
        transfer.wait_recv()
    for distance in range(1, near + 1):
        for sign in (1, -1):
            low = own + sign * distance * depth
            there = within[sign * distance]

            @pl.when(there)
            def _(low=low):
                each(low, low + depth, look_up)

            @pl.when(jnp.logical_not(there))
            def _(low=low):
                def turn(z, carry):
                    kappa[z] = jnp.zeros((width, height), jnp.float32)
                    return carry

                lax.fori_loop(low, low + depth, turn, 0)

    pl.when(n >= REACH - 2)(chain)
    pair, rest = fine_step(FINE_SWEEPS - 1, STEPS - 2, pair)
    rest()

    for transfer in wide_hops:
        transfer.wait_recv()

    def widen(c, carry):
        for field in range(2):
            for k in range(BLOCK_X):
                spread[field, c, pl.ds(k, rows_c, stride=BLOCK_X)] = delta[field, c]
        for r in range(0, width, chunk):
            at = pl.ds(r, chunk)
            place(base, c + 1, r, mix(EARLY[0], LATE[0], c, at))
        return carry

    def mix(early, late, c, at):
        return (slice_length * float(early)) * spread[0, c, at] + (slice_length * float(late)) * spread[1, c, at]

    lax.fori_loop(0, layers_c, widen, 0)
    base[0, inner] = jnp.zeros((width, height), jnp.float32)
    base[layers_c + 1, inner] = jnp.zeros((width, height), jnp.float32)

    def later(row, c, at):
        gap = float(GAPS[row])
        weight = float(TIMES[row])
        return mix(EARLY[row] - gap * (1.0 - weight), LATE[row] - gap * weight, c, at)

    def open_step(c, carry):
        for r in range(0, width, chunk):
            at, inside = pl.ds(r, chunk), pl.ds(PAD + r, chunk)
            center = base[c + 1, inside]
            behind = base[c + 1, pl.ds(PAD - 1 + r, chunk)]
            level = behind + base[c + 1, pl.ds(PAD + 1 + r, chunk)] + sideways(center)
            flow = advect * (center - behind)
            initial, following = spread[0, c, at], later(1, c, at)
            for k in range(BLOCK_Z):
                layer = BLOCK_Z * c + k
                total = level - (4.0 if 0 < k < BLOCK_Z - 1 else 5.0) * center
                if k == 0:
                    total = total + base[c, inside]
                if k == BLOCK_Z - 1:
                    total = total + base[c + 2, inside]
                value = initial + (kappa[layer, at] * total - flow)
                nodes[0, layer, at] = value
                place(grid.at[0], layer, r, float(GAPS[1]) * slice_length * value + following)
        return carry

    def wide_each(margin, body):
        def outer(i, carry):
            layer = own - margin + i + jnp.where(i >= margin, depth, 0)
            for r in range(0, width, chunk):
                body(layer, None, r)
            return carry

        def middle(z, carry):
            for r in range(0, width, chunk):
                body(own + z, z, r)
            return carry

        if margin > 0:
            lax.fori_loop(0, 2 * margin, outer, 0)
        lax.fori_loop(0, depth, middle, 0)

    def wide_step(stage):
        sweep, step = stage // STEPS, stage % STEPS
        source, target = grid.at[(stage - 1) % 2], grid.at[stage % 2]
        margin = REACH - 1 - stage
        final = sweep == FINE_SWEEPS - 1
        more = stage < REACH - 1

        def advance(layer, z, r):
            at, c = pl.ds(r, chunk), layer // BLOCK_Z
            initial = spread[0, c, at]
            if step == 0:
                before = initial
            else:
                before = latest[layer, at] if final else nodes[step - 1, layer, at]
            value = before + slope(source, layer, r, advect, kappa[layer, at], chunk)
            if final:
                if more:
                    latest[layer, at] = value
                if z is not None:
                    out[step + 1, z, at] = out[step + 1, z, at] + value
                    if step == 0:
                        out[0, z, at] = start[z, at] + initial
            else:
                nodes[step, layer, at] = value
            if not more:
                return
            if not final and step < STEPS - 1:
                total = slice_length * float(GAPS[step + 1]) * value + later(step + 1, c, at)
            else:
                if final:
                    row, known = step + 1, {}
                    total = slice_length * float(GAPS[row]) * (value - nodes[step, layer, at])
                else:
                    row, known = 0, {STEPS: value}
                    total = 0.0
                total = total + (slice_length * float(INTEGRALS[row, 0])) * initial
                for node in range(1, NODES):
                    part = known[node] if node in known else nodes[node - 1, layer, at]
                    total = total + (slice_length * float(INTEGRALS[row, node])) * part
            place(target, layer, r, total)

        wide_each(margin, advance)

    lax.fori_loop(0, layers_c, open_step, 0)
    for stage in range(1, STEPS):
        wide_step(stage)
    pair, rest = fine_step(FINE_SWEEPS - 1, STEPS - 1, pair)
    rest()
    for stage in range(STEPS, REACH):
        wide_step(stage)

    groups = {}
    for transfer in shipped:
        groups.setdefault(id(transfer.sends), []).append(transfer)
    for group in groups.values():

        @pl.when(group[0].sends)
        def _(group=group):
            for transfer in group:
                transfer.copy.wait_send()


def shards(node_fields, region_label, sheet_shift, diffusivity):
    fields = node_fields[0]
    nodes, depth, width, height = fields.shape
    depth_c, rows_c = depth // BLOCK_Z, width // BLOCK_X
    near = -(-REACH // depth)
    layers, layers_c = (2 * near + 1) * depth, (2 * near + 1) * depth_c
    f32 = jnp.float32
    fine, wide = (depth, width, height), (layers, width, height)
    coarse = (depth_c, rows_c, height)
    padded = width + 2 * PAD
    vmem, hbm = (pl.BlockSpec(memory_space=space) for space in (pltpu.VMEM, pltpu.HBM))
    result = pl.pallas_call(
        kernel,
        out_shape=jax.ShapeDtypeStruct(fields.shape, f32),
        in_specs=[hbm] * 4,
        out_specs=vmem,
        scratch_shapes=[
            pltpu.VMEM(fields.shape, f32),
            pltpu.VMEM(wide, jnp.int32),
            pltpu.VMEM(sheet_shift.shape, jnp.int32),
            pltpu.SMEM(diffusivity.shape, f32),
            pltpu.VMEM(wide, f32),
            pltpu.VMEM(coarse, f32),
            pltpu.VMEM(fine, f32),
            pltpu.VMEM((2, width, height), f32),
            pltpu.VMEM(coarse, f32),
            pltpu.VMEM(sheet_shift.shape, jnp.int32),
            pltpu.VMEM((2, rows_c, height), f32),
            pltpu.VMEM((EXCHANGES, depth + 2, padded, height), f32),
            pltpu.VMEM((STEPS,) + fine, f32),
            pltpu.VMEM(coarse, f32),
            pltpu.VMEM(coarse, f32),
            pltpu.VMEM((2, layers_c, rows_c, height), f32),
            pltpu.VMEM((width, height), f32),
            pltpu.VMEM((2, layers_c, width, height), f32),
            pltpu.VMEM((layers_c + 2, padded, height), f32),
            pltpu.VMEM((2, layers, padded, height), f32),
            pltpu.VMEM((STEPS,) + wide, f32),
            pltpu.VMEM(wide, f32),
            pltpu.SemaphoreType.DMA((2 * EXCHANGES * PIECES,)),
            pltpu.SemaphoreType.DMA((2 * EXCHANGES * PIECES,)),
            pltpu.SemaphoreType.DMA((8,)),
            pltpu.SemaphoreType.DMA((8,)),
            pltpu.SemaphoreType.DMA((4 * near,)),
            pltpu.SemaphoreType.DMA((4 * near,)),
            pltpu.SemaphoreType.DMA((2 * near * depth,)),
            pltpu.SemaphoreType.DMA((2 * near * depth,)),
            pltpu.SemaphoreType.DMA((NODES + 3,)),
        ],
        compiler_params=pltpu.CompilerParams(
            collective_id=0, has_side_effects=True, vmem_limit_bytes=48 * 1024 * 1024
        ),
    )(*(pltpu.with_memory_space_constraint(x, pltpu.HBM) for x in (fields, region_label, sheet_shift, diffusivity)))
    return result[None]


def solution(mesh):
    in_specs = (P("tm", None, "space", None, None), P("space", None, None), P("tm", None), P())
    out_specs = P("tm", None, "space", None, None)
    return jax.shard_map(shards, mesh=mesh, in_specs=in_specs, out_specs=out_specs, check_vma=False)
```

```python
import math

import jax
import jax.numpy as jnp
import numpy as np
from jax import lax
from jax.experimental import pallas as pl
from jax.experimental.pallas import tpu as pltpu
from jax.sharding import PartitionSpec as P

NODES = 5
FINE_SWEEPS = 2
BLOCK_Z = 4
BLOCK_X = 2
PAD = 8
PIECES = 4
MESH = pl.DeviceIdType.MESH

slice_length = 1.0


def node_tables():
    radius = math.sqrt(3.0 / 7.0)
    points = [0.0, (1.0 - radius) / 2.0, 0.5, (1.0 + radius) / 2.0, 1.0]
    integrals = np.zeros((4, 5))
    for column in range(5):
        coeffs = [1.0]
        divisor = 1.0
        for other in range(5):
            if other != column:
                anchor = points[other]
                product = [0.0] * (len(coeffs) + 1)
                for degree in range(len(coeffs)):
                    product[degree + 1] = product[degree + 1] + coeffs[degree]
                    product[degree] = product[degree] - anchor * coeffs[degree]
                coeffs = product
                divisor = divisor * (points[column] - anchor)
        for row in range(4):
            bottom = points[row]
            summit = points[row + 1]
            amount = 0.0
            for degree in range(len(coeffs)):
                amount = amount + coeffs[degree] / (degree + 1) * (
                    summit ** (degree + 1) - bottom ** (degree + 1)
                )
            integrals[row, column] = amount / divisor
    return (np.array(points), integrals)


TIMES, INTEGRALS = node_tables()
WEIGHTS = INTEGRALS.sum(axis=0)
STEPS = NODES - 1
REACH = FINE_SWEEPS * STEPS
EXCHANGES = 3 + REACH
FIRST = EXCHANGES - 1
GAPS = TIMES[1:] - TIMES[:-1]
LATE = (INTEGRALS * TIMES).sum(axis=1)
EARLY = INTEGRALS.sum(axis=1) - LATE
SLOTS = {1: 1, 2: 2, 3: 2, 4: 3, 5: 4, 6: 5}
LATE_SLICE = 7


class Transfer:
    def __init__(self, src, dst, send_sem, recv_sem, device, sends, receives):
        self.copy = pltpu.make_async_remote_copy(
            src_ref=src,
            dst_ref=dst,
            send_sem=send_sem,
            recv_sem=recv_sem,
            device_id=device,
            device_id_type=MESH,
        )
        self.sends, self.receives = sends, receives

    def start(self):
        pl.when(self.sends)(self.copy.start)

    def wait_recv(self):
        pl.when(self.receives)(self.copy.wait_recv)

    def wait_send(self):
        pl.when(self.sends)(self.copy.wait_send)


def kernel(
    fields_in, label_in, shift_in, table_in, out, fields, label, shift, table,
    kappa, inflow, decay, kappa_c, start, rim, moved, shift_next, pads, mids, gain, lift, delta, fold,
    spread, plan, base, grid, nodes, latest,
    halo_send, halo_recv, time_send, time_recv, start_send, start_recv, wide_send, wide_recv,
    label_send, label_recv, load_sem,
):
    n, s = lax.axis_index("tm"), lax.axis_index("space")
    slices, slabs = lax.axis_size("tm"), lax.axis_size("space")
    depth, width, height = fields.shape[1:]
    rows_c = width // BLOCK_X
    depth_c = depth // BLOCK_Z
    near = -(-REACH // depth)
    own, own_c = near * depth, near * depth_c
    layers, layers_c = (2 * near + 1) * depth, (2 * near + 1) * depth_c
    chunk = min(64, width)
    piece = width // PIECES
    last = NODES - 1
    has_prev, has_next = n > 0, n < slices - 1
    inner = pl.ds(PAD, width)
    here_c = pl.ds(own_c, depth_c)

    loads = [
        pltpu.make_async_copy(fields_in.at[node], fields.at[node], load_sem.at[node])
        for node in range(NODES)
    ]
    loads += [
        pltpu.make_async_copy(label_in, label.at[pl.ds(own, depth)], load_sem.at[NODES]),
        pltpu.make_async_copy(shift_in, shift, load_sem.at[NODES + 1]),
        pltpu.make_async_copy(table_in, table, load_sem.at[NODES + 2]),
    ]
    for load in loads:
        load.start()

    within = {
        distance: (s + distance >= 0) & (s + distance < slabs)
        for distance in range(-near, near + 1)
    }
    barrier = pltpu.get_barrier_semaphore()
    met = jnp.int32(0)
    for dn in (-1, 0, 1):
        for ds in range(-near, near + 1):
            if dn == 0 and ds == 0:
                continue
            there = (n + dn >= 0) & (n + dn < slices) & within[ds]

            @pl.when(there)
            def _(dn=dn, ds=ds):
                pl.semaphore_signal(
                    barrier, inc=1, device_id={"tm": n + dn, "space": s + ds}, device_id_type=MESH
                )

            met = met + there.astype(jnp.int32)

    drains = []

    def halo(index, source=None):
        buf = pads.at[index]
        pieces = []

        def pair(start, rows, low_sem, high_sem):
            here = pl.ds(PAD + start, rows)
            if source is None:
                low, high = buf.at[1, here], buf.at[depth, here]
            else:
                low, high = (source.at[z, pl.ds(start, rows)] for z in (0, depth - 1))
            up = Transfer(
                high, buf.at[0, here], halo_send.at[2 * index], halo_recv.at[high_sem],
                {"space": s + 1}, within[1], within[-1],
            )
            down = Transfer(
                low, buf.at[depth + 1, here], halo_send.at[2 * index + 1], halo_recv.at[low_sem],
                {"space": s - 1}, within[-1], within[1],
            )
            return down, up

        for k in range(PIECES):
            sem = 2 * (index * PIECES + k)
            pieces.append(pair(k * piece, piece, sem, sem + 1))
        drains.append(list(pair(0, width, 2 * index * PIECES, 2 * index * PIECES + 1)))
        return pieces

    def arrive(pieces):
        for down, up in pieces:
            down.wait_recv()
            up.wait_recv()

    def time_hop(index, src, dst, ds=0):
        goes = has_next if ds == 0 else has_next & within[ds]
        comes = has_prev if ds == 0 else has_prev & within[-ds]
        to = {"tm": n + 1} if ds == 0 else {"tm": n + 1, "space": s + ds}
        return Transfer(src, dst, time_send.at[index], time_recv.at[index], to, goes, comes)

    shift_hop = Transfer(
        shift_in, shift_next, time_send.at[0], time_recv.at[0], {"tm": n - 1}, has_prev, has_next
    )
    weighted_halo = halo(0)
    end_halo = halo(1, fields_in.at[last])
    first_halo = halo(FIRST)
    rim_hops = [
        time_hop(6, fields_in.at[last, depth - 1], rim.at[0], 1),
        time_hop(7, fields_in.at[last, 0], rim.at[1], -1),
    ]
    order = [z for k in range(depth // 2) for z in (k, depth - 1 - k)]
    start_hops = {
        z: Transfer(
            fields_in.at[last, z], start.at[z], start_send.at[z], start_recv.at[z],
            {"tm": n + 1}, has_next, has_prev,
        )
        for z in order
    }
    side = lax.rem(n, 2)
    label_hops = []
    for i in range(depth // 2):
        group = []
        for distance in range(1, near + 1):
            for sign in (1, -1):
                z = 2 * i + side
                sem = 4 * ((distance - 1) * (depth // 2) + i) + (sign + 1)
                there = own - sign * distance * depth + z
                first = Transfer(
                    label_in.at[z], label.at[there], label_send.at[sem], label_recv.at[sem],
                    {"space": s + sign * distance}, within[sign * distance], within[-sign * distance],
                )
                other = own - sign * distance * depth + z
                second = Transfer(
                    label.at[other], label.at[other], label_send.at[sem + 1], label_recv.at[sem + 1],
                    {"tm": n + 1 - 2 * side}, within[-sign * distance], within[-sign * distance],
                )
                group.append((first, second))
        label_hops.append(group)

    wide_hops, rest_hops = [], []
    edge_hops = [
        time_hop(4, delta.at[1, own_c + depth_c - 1], delta.at[0, own_c - 1], 1),
        time_hop(5, delta.at[1, own_c], delta.at[0, own_c + depth_c], -1),
    ]
    for distance in range(1, near + 1):
        for sign in (1, -1):
            sem = 2 * (distance - 1) + (sign + 1) // 2
            there = own_c - sign * distance * depth_c
            wide_hops.append(
                Transfer(
                    delta.at[1, here_c], delta.at[1, pl.ds(there, depth_c)],
                    wide_send.at[sem], wide_recv.at[sem],
                    {"space": s + sign * distance}, within[sign * distance], within[-sign * distance],
                )
            )
            skip = 1 if distance == 1 else 0
            if depth_c > skip:
                shown = skip if sign == -1 else 0
                rest_hops.append(
                    time_hop(
                        8 + sem,
                        delta.at[1, pl.ds(own_c + shown, depth_c - skip)],
                        delta.at[0, pl.ds(there + shown, depth_c - skip)],
                        sign * distance,
                    )
                )

    first_slice = (n == 0).astype(jnp.float32)

    def sideways(center):
        lane = lax.broadcasted_iota(jnp.int32, center.shape, 1)
        return jnp.where(lane == height - 1, 0.0, pltpu.roll(center, height - 1, 1)) + jnp.where(
            lane == 0, 0.0, pltpu.roll(center, 1, 1)
        )

    def slope(buf, layer, own_layer, r, rows):
        center = buf[layer, pl.ds(PAD + r, rows)]
        behind = buf[layer, pl.ds(PAD - 1 + r, rows)]
        total = buf[layer - 1, pl.ds(PAD + r, rows)] + buf[layer + 1, pl.ds(PAD + r, rows)]
        total = total + buf[layer, pl.ds(PAD + 1 + r, rows)]
        total = total + sideways(center)
        at = pl.ds(r, rows)
        return kappa[own_layer, at] * total + inflow[own_layer, at] * behind - decay[own_layer, at] * center

    def rate(index, z, r, chunk=chunk):
        return slope(pads.at[index], z + 1, own + z, r, chunk)

    def plain_rate(index, z, r, speed):
        buf = pads.at[index]
        center = buf[z + 1, pl.ds(PAD + r, chunk)]
        behind = buf[z + 1, pl.ds(PAD - 1 + r, chunk)]
        total = buf[z, pl.ds(PAD + r, chunk)] + buf[z + 2, pl.ds(PAD + r, chunk)]
        total = total + (behind + buf[z + 1, pl.ds(PAD + 1 + r, chunk)])
        total = total + sideways(center) - 6.0 * center
        return kappa[own + z, pl.ds(r, chunk)] * total - speed * (center - behind)

    def place(buf, layer, r, value):
        rows = value.shape[0]
        buf[layer, pl.ds(PAD + r, rows)] = value
        if r == 0:
            buf[layer, pl.ds(PAD + width, 1)] = value[:1]
        if r + rows == width:
            buf[layer, pl.ds(PAD - 1, 1)] = value[rows - 1 :]

    def fill(index, z, r, value):
        place(pads.at[index], z + 1, r, value)

    def each(lo, hi, body):
        def turn(z, carry):
            for r in range(0, width, chunk):
                body(z, r, chunk)
            return carry

        lax.fori_loop(lo, hi, turn, 0)

    def edges(body, needs=None, gives=None):
        for k in range(PIECES):
            if needs is not None:
                arrive(needs[k : k + 1])
            body(0, k * piece, piece)
            body(depth - 1, k * piece, piece)
            if gives is not None:
                gives[k][0].start()
                gives[k][1].start()

    def interior(body):
        each(1, depth - 1, body)

    def combine(coefficients, first, z, r, chunk):
        at = pl.ds(r, chunk)
        total = (first_slice * float(coefficients[0])) * fields[0, z, at] if first is None else first
        for node in range(1, NODES):
            total = total + float(coefficients[node]) * fields[node, z, at]
        return total

    def weigh(z, r, chunk):
        fill(0, z, r, combine(slice_length * WEIGHTS, None, z, r, chunk))

    def foresee(z, r, chunk):
        fill(FIRST, z, r, combine(slice_length * INTEGRALS[0], None, z, r, chunk))

    for load in loads:
        load.wait()
    edges(weigh)
    pl.semaphore_wait(barrier, met)
    for pieces in (weighted_halo, end_halo):
        for down, up in pieces:
            down.start()
            up.start()
    shift_hop.start()
    edges(foresee, None, first_halo)
    for transfer in rim_hops:
        transfer.start()
    for z in order:
        start_hops[z].start()
    interior(weigh)
    advect = shift[...].astype(jnp.float32) / slice_length

    def look_up(layer, r, chunk):
        at = pl.ds(r, chunk)
        labels = label[layer, at]
        total = jnp.zeros((chunk, height), jnp.float32)
        for region in range(table.shape[0]):
            total = total + jnp.where(labels == region, table[region], 0.0)
        kappa[layer, at] = total
        inflow[layer, at] = total + advect
        decay[layer, at] = 6.0 * total + advect

    def prepare(z, r, chunk):
        fill(1, z, r, fields[last, z, pl.ds(r, chunk)])
        look_up(own + z, r, chunk)

    each(0, depth, prepare)

    for index in range(EXCHANGES):

        @pl.when(jnp.logical_not(within[-1]))
        def _(index=index):
            pads[index, 0, inner] = jnp.zeros((width, height), jnp.float32)

        @pl.when(jnp.logical_not(within[1]))
        def _(index=index):
            pads[index, depth + 1, inner] = jnp.zeros((width, height), jnp.float32)

    def restrict(target, layer_of):
        def turn(zc, carry):
            for r in range(0, width, chunk):
                total = layer_of(BLOCK_Z * zc, r)
                for k in range(1, BLOCK_Z):
                    total = total + layer_of(BLOCK_Z * zc + k, r)
                fold[pl.ds(r, chunk)] = total
            total = fold[pl.ds(0, rows_c, stride=BLOCK_X)]
            for k in range(1, BLOCK_X):
                total = total + fold[pl.ds(k, rows_c, stride=BLOCK_X)]
            target[zc] = total * (1.0 / (BLOCK_Z * BLOCK_X))
            return carry

        lax.fori_loop(0, depth_c, turn, 0)

    arrive(weighted_halo)
    restrict(
        gain,
        lambda z, r: first_slice * fields[0, z, pl.ds(r, chunk)]
        - fields[last, z, pl.ds(r, chunk)]
        + slice_length * rate(0, z, r),
    )
    restrict(kappa_c, lambda z, r: kappa[own + z, pl.ds(r, chunk)])

    @pl.when(jnp.logical_not(has_prev))
    def _():
        moved[...] = jnp.zeros_like(moved)
        delta[0] = jnp.zeros((layers_c, rows_c, height), jnp.float32)

    for distance in range(1, near + 1):
        for sign in (1, -1):

            @pl.when(jnp.logical_not(within[sign * distance]))
            def _(distance=distance, sign=sign):
                there = own_c + sign * distance * depth_c
                delta[:, pl.ds(there, depth_c)] = jnp.zeros((2, depth_c, rows_c, height), jnp.float32)

    lift_hop = time_hop(2, lift, moved)
    body_hop = time_hop(3, delta.at[1, here_c], delta.at[0, here_c])

    def chain():
        lift_hop.wait_recv()
        for transfer in edge_hops:
            transfer.wait_recv()
        body_hop.wait_recv()
        for zc in range(depth_c):
            center = delta[0, own_c + zc]
            under, over = delta[0, own_c + zc - 1], delta[0, own_c + zc + 1]
            behind = pltpu.roll(center, 1, 0)
            across = behind + pltpu.roll(center, rows_c - 1, 0)
            lateral = sideways(center)
            spreading = kappa_c[zc] * (
                (under + over - 2.0 * center) * (1.0 / (BLOCK_Z * BLOCK_Z))
                + (across - 2.0 * center) * (1.0 / (BLOCK_X * BLOCK_X))
                + (lateral - 2.0 * center)
            )
            flow = (1.0 / BLOCK_X) * advect * (center - behind)
            delta[1, own_c + zc] = center + slice_length * (spreading - flow) + (gain[zc] + moved[zc])
            if zc == 0:
                edge_hops[1].start()
            if zc == depth_c - 1:
                edge_hops[0].start()
        body_hop.start()
        for transfer in rest_hops + wide_hops:
            transfer.start()

    pl.when(n == 0)(chain)

    shift_hop.wait_recv()
    arrive(end_halo)
    advect_next = shift_next[...].astype(jnp.float32) / slice_length
    restrict(
        lift,
        lambda z, r: fields[last, z, pl.ds(r, chunk)]
        + (slice_length * float(WEIGHTS[0])) * plain_rate(1, z, r, advect_next),
    )
    lift_hop.start()

    @pl.when(jnp.logical_not(has_prev))
    def _():
        def turn(z, carry):
            start[z] = fields[0, z]
            return carry

        lax.fori_loop(0, depth, turn, 0)
        rim[...] = jnp.zeros_like(rim)

    for end, there in enumerate((within[-1], within[1])):

        @pl.when(has_prev & jnp.logical_not(there))
        def _(end=end):
            rim[end] = jnp.zeros((width, height), jnp.float32)

    begin_weight = slice_length * float(INTEGRALS[0, 0])

    def combine_start(z, r, chunk):
        fill(2, z, r, combine(slice_length * INTEGRALS[0], begin_weight * start[z, pl.ds(r, chunk)], z, r, chunk))

    def open_layers(which):
        for z in which:
            start_hops[z].wait_recv()
            for r in range(0, width, chunk):
                combine_start(z, r, chunk)

    rim_hops[0].wait_recv()
    rim_hops[1].wait_recv()
    arrive(first_halo)
    for end, layer in ((0, 0), (1, depth + 1)):
        for r in range(0, width, chunk):
            at = pl.ds(PAD + r, chunk)
            pads[2, layer, at] = pads[FIRST, layer, at] + begin_weight * rim[end, pl.ds(r, chunk)]
    open_layers(order[:4])

    def fine_step(sweep, step, needs):
        old = fields if sweep == 0 else mids
        new = mids if sweep == 0 else None
        offset = 0 if sweep == 0 else -1
        index = 2 + sweep * STEPS + step
        final = sweep == FINE_SWEEPS - 1
        more = not (final and step == STEPS - 1)

        def advance(z, r, chunk):
            at = pl.ds(r, chunk)
            if step == 0:
                before = start[z, at]
            else:
                before = out[step, z, at] if final else new[step - 1, z, at]
            value = before + rate(index, z, r, chunk)
            if final:
                out[step + 1, z, at] = value
            else:
                new[step, z, at] = value
            if not more:
                return
            weights = slice_length * INTEGRALS[(step + 1) % STEPS]
            if step < STEPS - 1:
                total = slice_length * float(GAPS[step + 1]) * value
                weights[step + 1] -= slice_length * GAPS[step + 1]
                source, shown, known = old, offset, {}
            else:
                total, source, shown, known = None, new, -1, {STEPS: value}
            for node in range(NODES):
                if node == 0:
                    part = start[z, at]
                else:
                    part = known[node] if node in known else source[node + shown, z, at]
                term = float(weights[node]) * part
                total = term if total is None else total + term
            fill(index + 1, z, r, total)

        following = halo(index + 1) if more else None
        edges(advance, needs, following)
        return following, lambda: interior(advance)

    def forward(group):
        for first, second in group:
            first.wait_recv()
            second.start()

    def drain(count):
        for group in drains[:count]:
            for transfer in group:
                transfer.wait_send()
        del drains[:count]

    shares = -(-len(label_hops) // (REACH - 4))
    sent = []
    pair = None
    for stage in range(REACH - 2):
        for slice_at, slot in SLOTS.items():
            if slot == stage:
                pl.when(n == slice_at)(chain)
        pair, rest = fine_step(stage // STEPS, stage % STEPS, pair)
        passing = sent
        sent = label_hops[stage * shares : (stage + 1) * shares]
        for group in sent:
            for first, second in group:
                first.start()
        if stage == 0:
            open_layers(order[4:])
        rest()
        for group in passing:
            forward(group)
        drain(len(drains) - 2)

    for group in label_hops:
        for first, second in group:
            second.wait_recv()
    for distance in range(1, near + 1):
        for sign in (1, -1):
            low = own + sign * distance * depth
            there = within[sign * distance]

            @pl.when(there)
            def _(low=low):
                each(low, low + depth, look_up)

            @pl.when(jnp.logical_not(there))
            def _(low=low):
                def turn(z, carry):
                    kappa[z] = jnp.zeros((width, height), jnp.float32)
                    inflow[z] = jnp.zeros((width, height), jnp.float32)
                    decay[z] = jnp.zeros((width, height), jnp.float32)
                    return carry

                lax.fori_loop(low, low + depth, turn, 0)

    pl.when(n >= LATE_SLICE)(chain)
    pair, rest = fine_step(FINE_SWEEPS - 1, STEPS - 2, pair)
    rest()

    drain(len(drains) - 2)
    lift_hop.wait_send()
    shift_hop.wait_send()
    for transfer in rim_hops + list(start_hops.values()):
        transfer.wait_send()
    for transfer in wide_hops + rest_hops:
        transfer.wait_recv()

    def mix(early, late, begin, finish):
        return (slice_length * float(early)) * begin + (slice_length * float(late)) * finish

    def widen(c, carry):
        for field in range(2):
            for k in range(BLOCK_X):
                spread[field, c, pl.ds(k, rows_c, stride=BLOCK_X)] = delta[field, c]
        for r in range(0, width, chunk):
            at = pl.ds(r, chunk)
            begin, finish = spread[0, c, at], spread[1, c, at]
            place(base, c + 1, r, mix(EARLY[0], LATE[0], begin, finish))
            for row in range(1, STEPS):
                gap, weight = float(GAPS[row]), float(TIMES[row])
                plan[row - 1, c, at] = mix(
                    EARLY[row] - gap * (1.0 - weight), LATE[row] - gap * weight, begin, finish
                )
        return carry

    lax.fori_loop(0, layers_c, widen, 0)
    base[0, inner] = jnp.zeros((width, height), jnp.float32)
    base[layers_c + 1, inner] = jnp.zeros((width, height), jnp.float32)

    def open_step(c, carry):
        for r in range(0, width, chunk):
            at, inside = pl.ds(r, chunk), pl.ds(PAD + r, chunk)
            center = base[c + 1, inside]
            behind = base[c + 1, pl.ds(PAD - 1 + r, chunk)]
            level = base[c + 1, pl.ds(PAD + 1 + r, chunk)] + sideways(center)
            initial, following = spread[0, c, at], plan[0, c, at]
            for k in range(BLOCK_Z):
                layer = BLOCK_Z * c + k
                under = base[c, inside] if k == 0 else center
                over = base[c + 2, inside] if k == BLOCK_Z - 1 else center
                total = level + (under + over)
                value = initial + (kappa[layer, at] * total + inflow[layer, at] * behind - decay[layer, at] * center)
                nodes[0, layer, at] = value
                place(grid.at[0], layer, r, float(GAPS[1]) * slice_length * value + following)
        return carry

    def wide_each(margin, body):
        def outer(i, carry):
            layer = own - margin + i + jnp.where(i >= margin, depth, 0)
            for r in range(0, width, chunk):
                body(layer, None, r)
            return carry

        def middle(z, carry):
            for r in range(0, width, chunk):
                body(own + z, z, r)
            return carry

        if margin > 0:
            lax.fori_loop(0, 2 * margin, outer, 0)
        lax.fori_loop(0, depth, middle, 0)

    def wide_step(stage):
        sweep, step = stage // STEPS, stage % STEPS
        source, target = grid.at[(stage - 1) % 2], grid.at[stage % 2]
        margin = REACH - 1 - stage
        final = sweep == FINE_SWEEPS - 1
        more = stage < REACH - 1

        def advance(layer, z, r):
            at, c = pl.ds(r, chunk), layer // BLOCK_Z
            if step == 0 or final:
                initial = spread[0, c, at]
            if step == 0:
                before = initial
            else:
                before = latest[layer, at] if final else nodes[step - 1, layer, at]
            value = before + slope(source, layer, layer, r, chunk)
            if final:
                if more:
                    latest[layer, at] = value
                if z is not None:
                    out[step + 1, z, at] = out[step + 1, z, at] + value
                    if step == 0:
                        out[0, z, at] = start[z, at] + initial
            else:
                nodes[step, layer, at] = value
            if not more:
                return
            if not final and step < STEPS - 1:
                total = slice_length * float(GAPS[step + 1]) * value + plan[step, c, at]
            else:
                weights = slice_length * INTEGRALS[(step + 1) % STEPS]
                known = {}
                if final:
                    total = slice_length * float(GAPS[step + 1]) * value + float(weights[0]) * initial
                    weights[step + 1] -= slice_length * GAPS[step + 1]
                else:
                    total = float(weights[0]) * spread[0, c, at]
                    known = {STEPS: value}
                for node in range(1, NODES):
                    part = known[node] if node in known else nodes[node - 1, layer, at]
                    total = total + float(weights[node]) * part
            place(target, layer, r, total)

        wide_each(margin, advance)

    lax.fori_loop(0, layers_c, open_step, 0)
    for stage in range(1, STEPS):
        wide_step(stage)
    pair, rest = fine_step(FINE_SWEEPS - 1, STEPS - 1, pair)
    rest()
    for stage in range(STEPS, REACH):
        wide_step(stage)

    drain(len(drains))
    for group in label_hops:
        for first, second in group:
            first.wait_send()
            second.wait_send()
    for transfer in edge_hops + [body_hop] + rest_hops + wide_hops:
        transfer.wait_send()


def shards(node_fields, region_label, sheet_shift, diffusivity):
    fields = node_fields[0]
    nodes, depth, width, height = fields.shape
    depth_c, rows_c = depth // BLOCK_Z, width // BLOCK_X
    near = -(-REACH // depth)
    layers, layers_c = (2 * near + 1) * depth, (2 * near + 1) * depth_c
    f32 = jnp.float32
    fine, wide = (depth, width, height), (layers, width, height)
    coarse = (depth_c, rows_c, height)
    padded = width + 2 * PAD
    vmem, hbm = (pl.BlockSpec(memory_space=space) for space in (pltpu.VMEM, pltpu.HBM))
    result = pl.pallas_call(
        kernel,
        out_shape=jax.ShapeDtypeStruct(fields.shape, f32),
        in_specs=[hbm] * 4,
        out_specs=vmem,
        scratch_shapes=[
            pltpu.VMEM(fields.shape, f32),
            pltpu.VMEM(wide, jnp.int32),
            pltpu.VMEM(sheet_shift.shape, jnp.int32),
            pltpu.SMEM(diffusivity.shape, f32),
            pltpu.VMEM(wide, f32),
            pltpu.VMEM(wide, f32),
            pltpu.VMEM(wide, f32),
            pltpu.VMEM(coarse, f32),
            pltpu.VMEM(fine, f32),
            pltpu.VMEM((2, width, height), f32),
            pltpu.VMEM(coarse, f32),
            pltpu.VMEM(sheet_shift.shape, jnp.int32),
            pltpu.VMEM((EXCHANGES, depth + 2, padded, height), f32),
            pltpu.VMEM((STEPS,) + fine, f32),
            pltpu.VMEM(coarse, f32),
            pltpu.VMEM(coarse, f32),
            pltpu.VMEM((2, layers_c, rows_c, height), f32),
            pltpu.VMEM((width, height), f32),
            pltpu.VMEM((2, layers_c, width, height), f32),
            pltpu.VMEM((STEPS - 1, layers_c, width, height), f32),
            pltpu.VMEM((layers_c + 2, padded, height), f32),
            pltpu.VMEM((2, layers, padded, height), f32),
            pltpu.VMEM((STEPS,) + wide, f32),
            pltpu.VMEM(wide, f32),
            pltpu.SemaphoreType.DMA((2 * EXCHANGES,)),
            pltpu.SemaphoreType.DMA((2 * EXCHANGES * PIECES,)),
            pltpu.SemaphoreType.DMA((8 + 2 * near,)),
            pltpu.SemaphoreType.DMA((8 + 2 * near,)),
            pltpu.SemaphoreType.DMA((depth,)),
            pltpu.SemaphoreType.DMA((depth,)),
            pltpu.SemaphoreType.DMA((2 * near,)),
            pltpu.SemaphoreType.DMA((2 * near,)),
            pltpu.SemaphoreType.DMA((2 * near * depth,)),
            pltpu.SemaphoreType.DMA((2 * near * depth,)),
            pltpu.SemaphoreType.DMA((NODES + 3,)),
        ],
        compiler_params=pltpu.CompilerParams(
            collective_id=0, has_side_effects=True, vmem_limit_bytes=56 * 1024 * 1024,
        ),
    )(*(pltpu.with_memory_space_constraint(x, pltpu.HBM) for x in (fields, region_label, sheet_shift, diffusivity)))
    return result[None]


def solution(mesh):
    in_specs = (P("tm", None, "space", None, None), P("space", None, None), P("tm", None), P())
    out_specs = P("tm", None, "space", None, None)
    return jax.shard_map(shards, mesh=mesh, in_specs=in_specs, out_specs=out_specs, check_vma=False)
```

```python
import math

import jax
import jax.numpy as jnp
import numpy as np
from jax import lax
from jax.experimental import pallas as pl
from jax.experimental.pallas import tpu as pltpu
from jax.sharding import PartitionSpec as P

NODES = 5
FINE_SWEEPS = 2
BLOCK_Z = 4
BLOCK_X = 2
PAD = 8
PIECES = 4
MESH = pl.DeviceIdType.MESH

slice_length = 1.0


def node_tables():
    radius = math.sqrt(3.0 / 7.0)
    points = [0.0, (1.0 - radius) / 2.0, 0.5, (1.0 + radius) / 2.0, 1.0]
    integrals = np.zeros((4, 5))
    for column in range(5):
        coeffs = [1.0]
        divisor = 1.0
        for other in range(5):
            if other != column:
                anchor = points[other]
                product = [0.0] * (len(coeffs) + 1)
                for degree in range(len(coeffs)):
                    product[degree + 1] = product[degree + 1] + coeffs[degree]
                    product[degree] = product[degree] - anchor * coeffs[degree]
                coeffs = product
                divisor = divisor * (points[column] - anchor)
        for row in range(4):
            bottom = points[row]
            summit = points[row + 1]
            amount = 0.0
            for degree in range(len(coeffs)):
                amount = amount + coeffs[degree] / (degree + 1) * (
                    summit ** (degree + 1) - bottom ** (degree + 1)
                )
            integrals[row, column] = amount / divisor
    return (np.array(points), integrals)


TIMES, INTEGRALS = node_tables()
WEIGHTS = INTEGRALS.sum(axis=0)
STEPS = NODES - 1
REACH = FINE_SWEEPS * STEPS
EXCHANGES = 3 + REACH
FIRST = EXCHANGES - 1
GAPS = TIMES[1:] - TIMES[:-1]
LATE = (INTEGRALS * TIMES).sum(axis=1)
EARLY = INTEGRALS.sum(axis=1) - LATE
SLOTS = {1: 0, 2: 1, 3: 2, 4: 3, 5: 4, 6: 5}
LATE_SLICE = 7


class Transfer:
    def __init__(self, src, dst, send_sem, recv_sem, device, sends, receives):
        self.copy = pltpu.make_async_remote_copy(
            src_ref=src,
            dst_ref=dst,
            send_sem=send_sem,
            recv_sem=recv_sem,
            device_id=device,
            device_id_type=MESH,
        )
        self.sends, self.receives = sends, receives

    def start(self):
        pl.when(self.sends)(self.copy.start)

    def wait_recv(self):
        pl.when(self.receives)(self.copy.wait_recv)

    def wait_send(self):
        pl.when(self.sends)(self.copy.wait_send)


def kernel(
    fields_in, label_in, shift_in, table_in, out, fields, label, shift, table,
    kappa, inflow, decay, kappa_c, start, rim, moved, shift_next, pads, mids, gain, lift, delta, fold,
    spread, plan, base, grid, nodes, latest,
    halo_send, halo_recv, time_send, time_recv, start_send, start_recv, wide_send, wide_recv,
    label_send, label_recv, load_sem,
):
    n, s = lax.axis_index("tm"), lax.axis_index("space")
    slices, slabs = lax.axis_size("tm"), lax.axis_size("space")
    depth, width, height = fields.shape[1:]
    rows_c = width // BLOCK_X
    depth_c = depth // BLOCK_Z
    near = -(-REACH // depth)
    own, own_c = near * depth, near * depth_c
    layers, layers_c = (2 * near + 1) * depth, (2 * near + 1) * depth_c
    chunk = min(64, width)
    piece = width // PIECES
    last = NODES - 1
    has_prev, has_next = n > 0, n < slices - 1
    inner = pl.ds(PAD, width)
    here_c = pl.ds(own_c, depth_c)

    loads = [
        pltpu.make_async_copy(fields_in.at[node], fields.at[node], load_sem.at[node])
        for node in range(NODES)
    ]
    loads += [
        pltpu.make_async_copy(label_in, label.at[pl.ds(own, depth)], load_sem.at[NODES]),
        pltpu.make_async_copy(shift_in, shift, load_sem.at[NODES + 1]),
        pltpu.make_async_copy(table_in, table, load_sem.at[NODES + 2]),
    ]
    for load in loads:
        load.start()

    within = {
        distance: (s + distance >= 0) & (s + distance < slabs)
        for distance in range(-near, near + 1)
    }
    barrier = pltpu.get_barrier_semaphore()
    met = jnp.int32(0)
    for dn in (-1, 0, 1):
        for ds in range(-near, near + 1):
            if dn == 0 and ds == 0:
                continue
            there = (n + dn >= 0) & (n + dn < slices) & within[ds]

            @pl.when(there)
            def _(dn=dn, ds=ds):
                pl.semaphore_signal(
                    barrier, inc=1, device_id={"tm": n + dn, "space": s + ds}, device_id_type=MESH
                )

            met = met + there.astype(jnp.int32)

    drains = []

    def halo(index, source=None):
        buf = pads.at[index]
        pieces = []

        def pair(start, rows, low_sem, high_sem):
            here = pl.ds(PAD + start, rows)
            if source is None:
                low, high = buf.at[1, here], buf.at[depth, here]
            else:
                low, high = (source.at[z, pl.ds(start, rows)] for z in (0, depth - 1))
            up = Transfer(
                high, buf.at[0, here], halo_send.at[2 * index], halo_recv.at[high_sem],
                {"space": s + 1}, within[1], within[-1],
            )
            down = Transfer(
                low, buf.at[depth + 1, here], halo_send.at[2 * index + 1], halo_recv.at[low_sem],
                {"space": s - 1}, within[-1], within[1],
            )
            return down, up

        for k in range(PIECES):
            sem = 2 * (index * PIECES + k)
            pieces.append(pair(k * piece, piece, sem, sem + 1))
        drains.append(list(pair(0, width, 2 * index * PIECES, 2 * index * PIECES + 1)))
        return pieces

    def arrive(pieces):
        for down, up in pieces:
            down.wait_recv()
            up.wait_recv()

    def time_hop(index, src, dst, ds=0):
        goes = has_next if ds == 0 else has_next & within[ds]
        comes = has_prev if ds == 0 else has_prev & within[-ds]
        to = {"tm": n + 1} if ds == 0 else {"tm": n + 1, "space": s + ds}
        return Transfer(src, dst, time_send.at[index], time_recv.at[index], to, goes, comes)

    shift_hop = Transfer(
        shift_in, shift_next, time_send.at[0], time_recv.at[0], {"tm": n - 1}, has_prev, has_next
    )
    weighted_halo = halo(0)
    end_halo = halo(1, fields_in.at[last])
    first_halo = halo(FIRST)
    rim_hops = [
        time_hop(6, fields_in.at[last, depth - 1], rim.at[0], 1),
        time_hop(7, fields_in.at[last, 0], rim.at[1], -1),
    ]
    order = [z for k in range(depth // 2) for z in (k, depth - 1 - k)]
    start_hops = {
        z: Transfer(
            fields_in.at[last, z], start.at[z], start_send.at[z], start_recv.at[z],
            {"tm": n + 1}, has_next, has_prev,
        )
        for z in order
    }
    side = lax.rem(n, 2)
    label_hops = []
    for i in range(depth // 2):
        group = []
        for distance in range(1, near + 1):
            for sign in (1, -1):
                z = 2 * i + side
                sem = 4 * ((distance - 1) * (depth // 2) + i) + (sign + 1)
                there = own - sign * distance * depth + z
                first = Transfer(
                    label_in.at[z], label.at[there], label_send.at[sem], label_recv.at[sem],
                    {"space": s + sign * distance}, within[sign * distance], within[-sign * distance],
                )
                other = own - sign * distance * depth + z
                second = Transfer(
                    label.at[other], label.at[other], label_send.at[sem + 1], label_recv.at[sem + 1],
                    {"tm": n + 1 - 2 * side}, within[-sign * distance], within[-sign * distance],
                )
                group.append((first, second))
        label_hops.append(group)

    wide_hops, rest_hops = [], []
    edge_hops = [
        time_hop(4, delta.at[1, own_c + depth_c - 1], delta.at[0, own_c - 1], 1),
        time_hop(5, delta.at[1, own_c], delta.at[0, own_c + depth_c], -1),
    ]
    for distance in range(1, near + 1):
        for sign in (1, -1):
            sem = 2 * (distance - 1) + (sign + 1) // 2
            there = own_c - sign * distance * depth_c
            wide_hops.append(
                Transfer(
                    delta.at[1, here_c], delta.at[1, pl.ds(there, depth_c)],
                    wide_send.at[sem], wide_recv.at[sem],
                    {"space": s + sign * distance}, within[sign * distance], within[-sign * distance],
                )
            )
            skip = 1 if distance == 1 else 0
            if depth_c > skip:
                shown = skip if sign == -1 else 0
                rest_hops.append(
                    time_hop(
                        8 + sem,
                        delta.at[1, pl.ds(own_c + shown, depth_c - skip)],
                        delta.at[0, pl.ds(there + shown, depth_c - skip)],
                        sign * distance,
                    )
                )

    first_slice = (n == 0).astype(jnp.float32)

    def sideways(center):
        lane = lax.broadcasted_iota(jnp.int32, center.shape, 1)
        return jnp.where(lane == height - 1, 0.0, pltpu.roll(center, height - 1, 1)) + jnp.where(
            lane == 0, 0.0, pltpu.roll(center, 1, 1)
        )

    def slope(buf, layer, own_layer, r, rows):
        center = buf[layer, pl.ds(PAD + r, rows)]
        behind = buf[layer, pl.ds(PAD - 1 + r, rows)]
        total = buf[layer - 1, pl.ds(PAD + r, rows)] + buf[layer + 1, pl.ds(PAD + r, rows)]
        total = total + buf[layer, pl.ds(PAD + 1 + r, rows)]
        total = total + sideways(center)
        at = pl.ds(r, rows)
        return kappa[own_layer, at] * total + inflow[own_layer, at] * behind - decay[own_layer, at] * center

    def rate(index, z, r, chunk=chunk):
        return slope(pads.at[index], z + 1, own + z, r, chunk)

    def plain_rate(index, z, r, speed):
        buf = pads.at[index]
        center = buf[z + 1, pl.ds(PAD + r, chunk)]
        behind = buf[z + 1, pl.ds(PAD - 1 + r, chunk)]
        total = buf[z, pl.ds(PAD + r, chunk)] + buf[z + 2, pl.ds(PAD + r, chunk)]
        total = total + (behind + buf[z + 1, pl.ds(PAD + 1 + r, chunk)])
        total = total + sideways(center) - 6.0 * center
        return kappa[own + z, pl.ds(r, chunk)] * total - speed * (center - behind)

    def place(buf, layer, r, value):
        rows = value.shape[0]
        buf[layer, pl.ds(PAD + r, rows)] = value
        if r == 0:
            buf[layer, pl.ds(PAD + width, 1)] = value[:1]
        if r + rows == width:
            buf[layer, pl.ds(PAD - 1, 1)] = value[rows - 1 :]

    def fill(index, z, r, value):
        place(pads.at[index], z + 1, r, value)

    def each(lo, hi, body, unroll=1):
        def turn(z, carry):
            for r in range(0, width, chunk):
                body(z, r, chunk)
            return carry

        lax.fori_loop(lo, hi, turn, 0, unroll=unroll)

    def edges(body, needs=None, gives=None):
        for k in range(PIECES):
            if needs is not None:
                arrive(needs[k : k + 1])
            body(0, k * piece, piece)
            body(depth - 1, k * piece, piece)
            if gives is not None:
                gives[k][0].start()
                gives[k][1].start()

    def interior(body):
        each(1, depth - 1, body, 2)

    def combine(coefficients, first, z, r, chunk):
        at = pl.ds(r, chunk)
        total = (first_slice * float(coefficients[0])) * fields[0, z, at] if first is None else first
        for node in range(1, NODES):
            total = total + float(coefficients[node]) * fields[node, z, at]
        return total

    def weigh(z, r, chunk):
        fill(0, z, r, combine(slice_length * WEIGHTS, None, z, r, chunk))

    def foresee(z, r, chunk):
        fill(FIRST, z, r, combine(slice_length * INTEGRALS[0], None, z, r, chunk))

    for load in loads:
        load.wait()
    edges(weigh)
    pl.semaphore_wait(barrier, met)
    for pieces in (weighted_halo, end_halo):
        for down, up in pieces:
            down.start()
            up.start()
    shift_hop.start()
    edges(foresee, None, first_halo)
    for transfer in rim_hops:
        transfer.start()
    for z in order:
        start_hops[z].start()
    interior(weigh)
    advect = shift[...].astype(jnp.float32) / slice_length

    def look_up(layer, r, chunk):
        at = pl.ds(r, chunk)
        labels = label[layer, at]
        total = jnp.zeros((chunk, height), jnp.float32)
        for region in range(table.shape[0]):
            total = total + jnp.where(labels == region, table[region], 0.0)
        kappa[layer, at] = total
        inflow[layer, at] = total + advect
        decay[layer, at] = 6.0 * total + advect

    def prepare(z, r, chunk):
        fill(1, z, r, fields[last, z, pl.ds(r, chunk)])
        look_up(own + z, r, chunk)

    each(0, depth, prepare)

    for index in range(EXCHANGES):

        @pl.when(jnp.logical_not(within[-1]))
        def _(index=index):
            pads[index, 0, inner] = jnp.zeros((width, height), jnp.float32)

        @pl.when(jnp.logical_not(within[1]))
        def _(index=index):
            pads[index, depth + 1, inner] = jnp.zeros((width, height), jnp.float32)

    def restrict(target, layer_of):
        def turn(zc, carry):
            for r in range(0, width, chunk):
                total = layer_of(BLOCK_Z * zc, r)
                for k in range(1, BLOCK_Z):
                    total = total + layer_of(BLOCK_Z * zc + k, r)
                fold[pl.ds(r, chunk)] = total
            total = fold[pl.ds(0, rows_c, stride=BLOCK_X)]
            for k in range(1, BLOCK_X):
                total = total + fold[pl.ds(k, rows_c, stride=BLOCK_X)]
            target[zc] = total * (1.0 / (BLOCK_Z * BLOCK_X))
            return carry

        lax.fori_loop(0, depth_c, turn, 0)

    arrive(weighted_halo)
    restrict(
        gain,
        lambda z, r: first_slice * fields[0, z, pl.ds(r, chunk)]
        - fields[last, z, pl.ds(r, chunk)]
        + slice_length * rate(0, z, r),
    )
    restrict(kappa_c, lambda z, r: kappa[own + z, pl.ds(r, chunk)])

    @pl.when(jnp.logical_not(has_prev))
    def _():
        moved[...] = jnp.zeros_like(moved)
        delta[0] = jnp.zeros((layers_c, rows_c, height), jnp.float32)

    for distance in range(1, near + 1):
        for sign in (1, -1):

            @pl.when(jnp.logical_not(within[sign * distance]))
            def _(distance=distance, sign=sign):
                there = own_c + sign * distance * depth_c
                delta[:, pl.ds(there, depth_c)] = jnp.zeros((2, depth_c, rows_c, height), jnp.float32)

    lift_hop = time_hop(2, lift, moved)
    body_hop = time_hop(3, delta.at[1, here_c], delta.at[0, here_c])

    def chain():
        lift_hop.wait_recv()
        for transfer in edge_hops:
            transfer.wait_recv()
        body_hop.wait_recv()
        for zc in range(depth_c):
            center = delta[0, own_c + zc]
            under, over = delta[0, own_c + zc - 1], delta[0, own_c + zc + 1]
            behind = pltpu.roll(center, 1, 0)
            across = behind + pltpu.roll(center, rows_c - 1, 0)
            lateral = sideways(center)
            spreading = kappa_c[zc] * (
                (under + over - 2.0 * center) * (1.0 / (BLOCK_Z * BLOCK_Z))
                + (across - 2.0 * center) * (1.0 / (BLOCK_X * BLOCK_X))
                + (lateral - 2.0 * center)
            )
            flow = (1.0 / BLOCK_X) * advect * (center - behind)
            delta[1, own_c + zc] = center + slice_length * (spreading - flow) + (gain[zc] + moved[zc])
            if zc == 0:
                edge_hops[1].start()
            if zc == depth_c - 1:
                edge_hops[0].start()
        body_hop.start()
        for transfer in rest_hops + wide_hops:
            transfer.start()

    pl.when(n == 0)(chain)

    shift_hop.wait_recv()
    arrive(end_halo)
    advect_next = shift_next[...].astype(jnp.float32) / slice_length
    restrict(
        lift,
        lambda z, r: fields[last, z, pl.ds(r, chunk)]
        + (slice_length * float(WEIGHTS[0])) * plain_rate(1, z, r, advect_next),
    )
    lift_hop.start()

    @pl.when(jnp.logical_not(has_prev))
    def _():
        def turn(z, carry):
            start[z] = fields[0, z]
            return carry

        lax.fori_loop(0, depth, turn, 0)
        rim[...] = jnp.zeros_like(rim)

    for end, there in enumerate((within[-1], within[1])):

        @pl.when(has_prev & jnp.logical_not(there))
        def _(end=end):
            rim[end] = jnp.zeros((width, height), jnp.float32)

    begin_weight = slice_length * float(INTEGRALS[0, 0])

    def combine_start(z, r, chunk):
        fill(2, z, r, combine(slice_length * INTEGRALS[0], begin_weight * start[z, pl.ds(r, chunk)], z, r, chunk))

    def open_layers(which):
        for z in which:
            start_hops[z].wait_recv()
            for r in range(0, width, chunk):
                combine_start(z, r, chunk)

    rim_hops[0].wait_recv()
    rim_hops[1].wait_recv()
    arrive(first_halo)
    for end, layer in ((0, 0), (1, depth + 1)):
        for r in range(0, width, chunk):
            at = pl.ds(PAD + r, chunk)
            pads[2, layer, at] = pads[FIRST, layer, at] + begin_weight * rim[end, pl.ds(r, chunk)]
    open_layers(order[:4])

    def fine_step(sweep, step, needs):
        old = fields if sweep == 0 else mids
        new = mids if sweep == 0 else None
        offset = 0 if sweep == 0 else -1
        index = 2 + sweep * STEPS + step
        final = sweep == FINE_SWEEPS - 1
        more = not (final and step == STEPS - 1)

        def advance(z, r, chunk):
            at = pl.ds(r, chunk)
            if step == 0:
                before = start[z, at]
            else:
                before = out[step, z, at] if final else new[step - 1, z, at]
            value = before + rate(index, z, r, chunk)
            if final:
                out[step + 1, z, at] = value
            else:
                new[step, z, at] = value
            if not more:
                return
            weights = slice_length * INTEGRALS[(step + 1) % STEPS]
            if step < STEPS - 1:
                total = slice_length * float(GAPS[step + 1]) * value
                weights[step + 1] -= slice_length * GAPS[step + 1]
                source, shown, known = old, offset, {}
            else:
                total, source, shown, known = None, new, -1, {STEPS: value}
            for node in range(NODES):
                if node == 0:
                    part = start[z, at]
                else:
                    part = known[node] if node in known else source[node + shown, z, at]
                term = float(weights[node]) * part
                total = term if total is None else total + term
            fill(index + 1, z, r, total)

        following = halo(index + 1) if more else None
        edges(advance, needs, following)
        return following, lambda: interior(advance)

    def forward(group):
        for first, second in group:
            first.wait_recv()
            second.start()

    def drain(count):
        for group in drains[:count]:
            for transfer in group:
                transfer.wait_send()
        del drains[:count]

    shares = -(-len(label_hops) // (REACH - 4))
    sent = []
    pair = None
    for stage in range(REACH - 2):
        for slice_at, slot in SLOTS.items():
            if slot == stage:
                pl.when(n == slice_at)(chain)
        pair, rest = fine_step(stage // STEPS, stage % STEPS, pair)
        passing = sent
        sent = label_hops[stage * shares : (stage + 1) * shares]
        for group in sent:
            for first, second in group:
                first.start()
        if stage == 0:
            open_layers(order[4:])
        rest()
        for group in passing:
            forward(group)
        drain(len(drains) - 2)

    for group in label_hops:
        for first, second in group:
            second.wait_recv()
    for distance in range(1, near + 1):
        for sign in (1, -1):
            low = own + sign * distance * depth
            there = within[sign * distance]

            @pl.when(there)
            def _(low=low):
                each(low, low + depth, look_up)

            @pl.when(jnp.logical_not(there))
            def _(low=low):
                def turn(z, carry):
                    kappa[z] = jnp.zeros((width, height), jnp.float32)
                    inflow[z] = jnp.zeros((width, height), jnp.float32)
                    decay[z] = jnp.zeros((width, height), jnp.float32)
                    return carry

                lax.fori_loop(low, low + depth, turn, 0)

    pl.when(n >= LATE_SLICE)(chain)
    pair, rest = fine_step(FINE_SWEEPS - 1, STEPS - 2, pair)
    rest()

    drain(len(drains) - 2)
    lift_hop.wait_send()
    shift_hop.wait_send()
    for transfer in rim_hops + list(start_hops.values()):
        transfer.wait_send()
    for transfer in wide_hops + rest_hops:
        transfer.wait_recv()

    def mix(early, late, begin, finish):
        return (slice_length * float(early)) * begin + (slice_length * float(late)) * finish

    def widen(c, carry):
        for field in range(2):
            for k in range(BLOCK_X):
                spread[field, c, pl.ds(k, rows_c, stride=BLOCK_X)] = delta[field, c]
        for r in range(0, width, chunk):
            at = pl.ds(r, chunk)
            begin, finish = spread[0, c, at], spread[1, c, at]
            place(base, c + 1, r, mix(EARLY[0], LATE[0], begin, finish))
            for row in range(1, STEPS):
                gap, weight = float(GAPS[row]), float(TIMES[row])
                plan[row - 1, c, at] = mix(
                    EARLY[row] - gap * (1.0 - weight), LATE[row] - gap * weight, begin, finish
                )
        return carry

    lax.fori_loop(0, layers_c, widen, 0)
    base[0, inner] = jnp.zeros((width, height), jnp.float32)
    base[layers_c + 1, inner] = jnp.zeros((width, height), jnp.float32)

    def open_step(c, carry):
        for r in range(0, width, chunk):
            at, inside = pl.ds(r, chunk), pl.ds(PAD + r, chunk)
            center = base[c + 1, inside]
            behind = base[c + 1, pl.ds(PAD - 1 + r, chunk)]
            level = base[c + 1, pl.ds(PAD + 1 + r, chunk)] + sideways(center)
            initial, following = spread[0, c, at], plan[0, c, at]
            for k in range(BLOCK_Z):
                layer = BLOCK_Z * c + k
                under = base[c, inside] if k == 0 else center
                over = base[c + 2, inside] if k == BLOCK_Z - 1 else center
                total = level + (under + over)
                value = initial + (kappa[layer, at] * total + inflow[layer, at] * behind - decay[layer, at] * center)
                nodes[0, layer, at] = value
                place(grid.at[0], layer, r, float(GAPS[1]) * slice_length * value + following)
        return carry

    def wide_each(margin, body):
        def outer(i, carry):
            layer = own - margin + i + jnp.where(i >= margin, depth, 0)
            for r in range(0, width, chunk):
                body(layer, None, r)
            return carry

        def middle(z, carry):
            for r in range(0, width, chunk):
                body(own + z, z, r)
            return carry

        if margin > 0:
            lax.fori_loop(0, 2 * margin, outer, 0, unroll=min(4, 2 * margin))
        lax.fori_loop(0, depth, middle, 0, unroll=4)

    def wide_step(stage):
        sweep, step = stage // STEPS, stage % STEPS
        source, target = grid.at[(stage - 1) % 2], grid.at[stage % 2]
        margin = REACH - 1 - stage
        final = sweep == FINE_SWEEPS - 1
        more = stage < REACH - 1

        def advance(layer, z, r):
            at, c = pl.ds(r, chunk), layer // BLOCK_Z
            if step == 0 or final:
                initial = spread[0, c, at]
            if step == 0:
                before = initial
            else:
                before = latest[layer, at] if final else nodes[step - 1, layer, at]
            value = before + slope(source, layer, layer, r, chunk)
            if final:
                if more:
                    latest[layer, at] = value
                if z is not None:
                    out[step + 1, z, at] = out[step + 1, z, at] + value
                    if step == 0:
                        out[0, z, at] = start[z, at] + initial
            else:
                nodes[step, layer, at] = value
            if not more:
                return
            if not final and step < STEPS - 1:
                total = slice_length * float(GAPS[step + 1]) * value + plan[step, c, at]
            else:
                weights = slice_length * INTEGRALS[(step + 1) % STEPS]
                known = {}
                if final:
                    total = slice_length * float(GAPS[step + 1]) * value + float(weights[0]) * initial
                    weights[step + 1] -= slice_length * GAPS[step + 1]
                else:
                    total = float(weights[0]) * spread[0, c, at]
                    known = {STEPS: value}
                for node in range(1, NODES):
                    part = known[node] if node in known else nodes[node - 1, layer, at]
                    total = total + float(weights[node]) * part
            place(target, layer, r, total)

        wide_each(margin, advance)

    lax.fori_loop(0, layers_c, open_step, 0)
    for stage in range(1, STEPS):
        wide_step(stage)
    pair, rest = fine_step(FINE_SWEEPS - 1, STEPS - 1, pair)
    rest()
    for stage in range(STEPS, REACH):
        wide_step(stage)

    drain(len(drains))
    for group in label_hops:
        for first, second in group:
            first.wait_send()
            second.wait_send()
    for transfer in edge_hops + [body_hop] + rest_hops + wide_hops:
        transfer.wait_send()


def shards(node_fields, region_label, sheet_shift, diffusivity):
    fields = node_fields[0]
    nodes, depth, width, height = fields.shape
    depth_c, rows_c = depth // BLOCK_Z, width // BLOCK_X
    near = -(-REACH // depth)
    layers, layers_c = (2 * near + 1) * depth, (2 * near + 1) * depth_c
    f32 = jnp.float32
    fine, wide = (depth, width, height), (layers, width, height)
    coarse = (depth_c, rows_c, height)
    padded = width + 2 * PAD
    vmem, hbm = (pl.BlockSpec(memory_space=space) for space in (pltpu.VMEM, pltpu.HBM))
    result = pl.pallas_call(
        kernel,
        out_shape=jax.ShapeDtypeStruct(fields.shape, f32),
        in_specs=[hbm] * 4,
        out_specs=vmem,
        scratch_shapes=[
            pltpu.VMEM(fields.shape, f32),
            pltpu.VMEM(wide, jnp.int32),
            pltpu.VMEM(sheet_shift.shape, jnp.int32),
            pltpu.SMEM(diffusivity.shape, f32),
            pltpu.VMEM(wide, f32),
            pltpu.VMEM(wide, f32),
            pltpu.VMEM(wide, f32),
            pltpu.VMEM(coarse, f32),
            pltpu.VMEM(fine, f32),
            pltpu.VMEM((2, width, height), f32),
            pltpu.VMEM(coarse, f32),
            pltpu.VMEM(sheet_shift.shape, jnp.int32),
            pltpu.VMEM((EXCHANGES, depth + 2, padded, height), f32),
            pltpu.VMEM((STEPS,) + fine, f32),
            pltpu.VMEM(coarse, f32),
            pltpu.VMEM(coarse, f32),
            pltpu.VMEM((2, layers_c, rows_c, height), f32),
            pltpu.VMEM((width, height), f32),
            pltpu.VMEM((2, layers_c, width, height), f32),
            pltpu.VMEM((STEPS - 1, layers_c, width, height), f32),
            pltpu.VMEM((layers_c + 2, padded, height), f32),
            pltpu.VMEM((2, layers, padded, height), f32),
            pltpu.VMEM((STEPS,) + wide, f32),
            pltpu.VMEM(wide, f32),
            pltpu.SemaphoreType.DMA((2 * EXCHANGES,)),
            pltpu.SemaphoreType.DMA((2 * EXCHANGES * PIECES,)),
            pltpu.SemaphoreType.DMA((8 + 2 * near,)),
            pltpu.SemaphoreType.DMA((8 + 2 * near,)),
            pltpu.SemaphoreType.DMA((depth,)),
            pltpu.SemaphoreType.DMA((depth,)),
            pltpu.SemaphoreType.DMA((2 * near,)),
            pltpu.SemaphoreType.DMA((2 * near,)),
            pltpu.SemaphoreType.DMA((2 * near * depth,)),
            pltpu.SemaphoreType.DMA((2 * near * depth,)),
            pltpu.SemaphoreType.DMA((NODES + 3,)),
        ],
        compiler_params=pltpu.CompilerParams(
            collective_id=0, has_side_effects=True, vmem_limit_bytes=48 * 1024 * 1024,
        ),
    )(*(pltpu.with_memory_space_constraint(x, pltpu.HBM) for x in (fields, region_label, sheet_shift, diffusivity)))
    return result[None]


def solution(mesh):
    in_specs = (P("tm", None, "space", None, None), P("space", None, None), P("tm", None), P())
    out_specs = P("tm", None, "space", None, None)
    return jax.shard_map(shards, mesh=mesh, in_specs=in_specs, out_specs=out_specs, check_vma=False)
```

```python
import math

import jax
import jax.numpy as jnp
import numpy as np
from jax import lax
from jax.experimental import pallas as pl
from jax.experimental.pallas import tpu as pltpu
from jax.sharding import PartitionSpec as P

NODES = 5
FINE_SWEEPS = 2
BLOCK_Z = 4
BLOCK_X = 2
PAD = 8
PIECES = 4
MESH = pl.DeviceIdType.MESH

slice_length = 1.0


def node_tables():
    radius = math.sqrt(3.0 / 7.0)
    points = [0.0, (1.0 - radius) / 2.0, 0.5, (1.0 + radius) / 2.0, 1.0]
    integrals = np.zeros((4, 5))
    for column in range(5):
        coeffs = [1.0]
        divisor = 1.0
        for other in range(5):
            if other != column:
                anchor = points[other]
                product = [0.0] * (len(coeffs) + 1)
                for degree in range(len(coeffs)):
                    product[degree + 1] = product[degree + 1] + coeffs[degree]
                    product[degree] = product[degree] - anchor * coeffs[degree]
                coeffs = product
                divisor = divisor * (points[column] - anchor)
        for row in range(4):
            bottom = points[row]
            summit = points[row + 1]
            amount = 0.0
            for degree in range(len(coeffs)):
                amount = amount + coeffs[degree] / (degree + 1) * (
                    summit ** (degree + 1) - bottom ** (degree + 1)
                )
            integrals[row, column] = amount / divisor
    return (np.array(points), integrals)


TIMES, INTEGRALS = node_tables()
WEIGHTS = INTEGRALS.sum(axis=0)
STEPS = NODES - 1
REACH = FINE_SWEEPS * STEPS
EXCHANGES = 3 + REACH
FIRST = EXCHANGES - 1
GAPS = TIMES[1:] - TIMES[:-1]
LATE = (INTEGRALS * TIMES).sum(axis=1)
EARLY = INTEGRALS.sum(axis=1) - LATE
SLOTS = {1: 0, 2: 1, 3: 2, 4: 3, 5: 4, 6: 5}
LATE_SLICE = 7


class Transfer:
    def __init__(self, src, dst, send_sem, recv_sem, device, sends, receives):
        self.copy = pltpu.make_async_remote_copy(
            src_ref=src,
            dst_ref=dst,
            send_sem=send_sem,
            recv_sem=recv_sem,
            device_id=device,
            device_id_type=MESH,
        )
        self.sends, self.receives = sends, receives

    def start(self):
        pl.when(self.sends)(self.copy.start)

    def wait_recv(self):
        pl.when(self.receives)(self.copy.wait_recv)

    def wait_send(self):
        pl.when(self.sends)(self.copy.wait_send)


def kernel(
    fields_in, label_in, shift_in, table_in, out, fields, label, shift, table,
    kappa, inflow, decay, kappa_c, start, rim, moved, shift_next, pads, mids, gain, lift, delta, front, fold,
    spread, plan, base, grid, nodes, latest,
    halo_send, halo_recv, time_send, time_recv, start_send, start_recv, wide_send, wide_recv, edge_send, edge_recv,
    label_send, label_recv, load_sem,
):
    n, s = lax.axis_index("tm"), lax.axis_index("space")
    slices, slabs = lax.axis_size("tm"), lax.axis_size("space")
    depth, width, height = fields.shape[1:]
    rows_c = width // BLOCK_X
    depth_c = depth // BLOCK_Z
    near = -(-REACH // depth)
    own, own_c = near * depth, near * depth_c
    layers, layers_c = (2 * near + 1) * depth, (2 * near + 1) * depth_c
    chunk = min(64, width)
    piece = width // PIECES
    last = NODES - 1
    has_prev, has_next = n > 0, n < slices - 1
    inner = pl.ds(PAD, width)
    here_c = pl.ds(own_c, depth_c)

    loads = [
        pltpu.make_async_copy(fields_in.at[node], fields.at[node], load_sem.at[node])
        for node in range(NODES)
    ]
    loads += [
        pltpu.make_async_copy(label_in, label.at[pl.ds(own, depth)], load_sem.at[NODES]),
        pltpu.make_async_copy(shift_in, shift, load_sem.at[NODES + 1]),
        pltpu.make_async_copy(table_in, table, load_sem.at[NODES + 2]),
    ]
    for load in loads:
        load.start()

    within = {
        distance: (s + distance >= 0) & (s + distance < slabs)
        for distance in range(-near, near + 1)
    }
    for distance in range(1, near + 1):
        for sign in (1, -1):

            @pl.when(jnp.logical_not(within[sign * distance]))
            def _(distance=distance, sign=sign):
                there = own_c + sign * distance * depth_c
                delta[:, pl.ds(there, depth_c)] = jnp.zeros((2, depth_c, rows_c, height), jnp.float32)
                if distance == 1:
                    edge = depth_c + 1 if sign == 1 else 0
                    for ref in (gain, moved, kappa_c):
                        ref[edge] = jnp.zeros((rows_c, height), jnp.float32)

    @pl.when(jnp.logical_not(has_prev))
    def _():
        moved[...] = jnp.zeros_like(moved)
        delta[0] = jnp.zeros((layers_c, rows_c, height), jnp.float32)

    barrier = pltpu.get_barrier_semaphore()
    met = jnp.int32(0)
    for dn in (-1, 0, 1):
        for ds in range(-near, near + 1):
            if dn == 0 and ds == 0:
                continue
            there = (n + dn >= 0) & (n + dn < slices) & within[ds]

            @pl.when(there)
            def _(dn=dn, ds=ds):
                pl.semaphore_signal(
                    barrier, inc=1, device_id={"tm": n + dn, "space": s + ds}, device_id_type=MESH
                )

            met = met + there.astype(jnp.int32)

    drains = []

    def halo(index, source=None):
        buf = pads.at[index]
        pieces = []

        def pair(start, rows, low_sem, high_sem):
            here = pl.ds(PAD + start, rows)
            if source is None:
                low, high = buf.at[1, here], buf.at[depth, here]
            else:
                low, high = (source.at[z, pl.ds(start, rows)] for z in (0, depth - 1))
            up = Transfer(
                high, buf.at[0, here], halo_send.at[2 * index], halo_recv.at[high_sem],
                {"space": s + 1}, within[1], within[-1],
            )
            down = Transfer(
                low, buf.at[depth + 1, here], halo_send.at[2 * index + 1], halo_recv.at[low_sem],
                {"space": s - 1}, within[-1], within[1],
            )
            return down, up

        for k in range(PIECES):
            sem = 2 * (index * PIECES + k)
            pieces.append(pair(k * piece, piece, sem, sem + 1))
        drains.append(list(pair(0, width, 2 * index * PIECES, 2 * index * PIECES + 1)))
        return pieces

    def arrive(pieces):
        for down, up in pieces:
            down.wait_recv()
            up.wait_recv()

    side = lax.rem(n, 2)
    beyond = (side == 0) & has_prev
    always = n >= 0

    def time_hop(index, src, dst, ds=0, sends=always, receives=always):
        goes = has_next & sends if ds == 0 else has_next & sends & within[ds]
        comes = has_prev & receives if ds == 0 else has_prev & receives & within[-ds]
        to = {"tm": n + 1} if ds == 0 else {"tm": n + 1, "space": s + ds}
        return Transfer(src, dst, time_send.at[index], time_recv.at[index], to, goes, comes)

    shift_hop = Transfer(
        shift_in, shift_next, time_send.at[0], time_recv.at[0], {"tm": n - 1}, has_prev, has_next
    )
    weighted_halo = halo(0)
    end_halo = halo(1, fields_in.at[last])
    first_halo = halo(FIRST)
    rim_hops = [
        time_hop(6, fields_in.at[last, depth - 1], rim.at[0], 1),
        time_hop(7, fields_in.at[last, 0], rim.at[1], -1),
    ]
    order = [z for k in range(depth // 2) for z in (k, depth - 1 - k)]
    start_hops = {
        z: Transfer(
            fields_in.at[last, z], start.at[z], start_send.at[z], start_recv.at[z],
            {"tm": n + 1}, has_next, has_prev,
        )
        for z in order
    }
    label_hops = []
    for i in range(depth // 2):
        group = []
        for distance in range(1, near + 1):
            for sign in (1, -1):
                z = 2 * i + side
                sem = 4 * ((distance - 1) * (depth // 2) + i) + (sign + 1)
                there = own - sign * distance * depth + z
                first = Transfer(
                    label_in.at[z], label.at[there], label_send.at[sem], label_recv.at[sem],
                    {"space": s + sign * distance}, within[sign * distance], within[-sign * distance],
                )
                other = own - sign * distance * depth + z
                second = Transfer(
                    label.at[other], label.at[other], label_send.at[sem + 1], label_recv.at[sem + 1],
                    {"tm": n + 1 - 2 * side}, within[-sign * distance], within[-sign * distance],
                )
                group.append((first, second))
        label_hops.append(group)

    own_layers = pl.ds(1, depth_c)
    whole = jnp.logical_not(beyond)
    from_beyond = (side == 1) & (n > 1)
    from_whole = jnp.logical_not(from_beyond)
    lift_hops = [
        time_hop(2, lift, moved.at[own_layers]),
        time_hop(4, lift.at[depth_c - 1], moved.at[0], 1, side == 1, beyond),
        time_hop(5, lift.at[0], moved.at[depth_c + 1], -1, side == 1, beyond),
    ]
    edge_hops = []
    for k, ref in enumerate((kappa_c, gain)):
        edge_hops.append(
            Transfer(
                ref.at[depth_c], ref.at[0], edge_send.at[2 * k], edge_recv.at[2 * k],
                {"space": s + 1}, beyond & within[1], beyond & within[-1],
            )
        )
        edge_hops.append(
            Transfer(
                ref.at[1], ref.at[depth_c + 1], edge_send.at[2 * k + 1], edge_recv.at[2 * k + 1],
                {"space": s - 1}, beyond & within[-1], beyond & within[1],
            )
        )
    front_hop = time_hop(
        1, front, delta.at[0, pl.ds(own_c - 1, depth_c + 2)], 0, beyond, from_beyond
    )
    body_hop = time_hop(3, delta.at[1, here_c], delta.at[0, here_c], 0, whole, from_whole)
    wide_hops, rest_hops, slab_hops = [], [], []
    for distance in range(1, near + 1):
        for sign in (1, -1):
            sem = 2 * (distance - 1) + (sign + 1) // 2
            there = own_c - sign * distance * depth_c
            wide_hops.append(
                Transfer(
                    delta.at[1, here_c], delta.at[1, pl.ds(there, depth_c)],
                    wide_send.at[sem], wide_recv.at[sem],
                    {"space": s + sign * distance}, within[sign * distance], within[-sign * distance],
                )
            )
            slab_hops.append(
                time_hop(
                    8 + 2 * near + sem, delta.at[1, here_c], delta.at[0, pl.ds(there, depth_c)],
                    sign * distance, whole, from_whole,
                )
            )
            skip = 1 if distance == 1 else 0
            if depth_c > skip:
                shown = skip if sign == -1 else 0
                rest_hops.append(
                    time_hop(
                        8 + sem,
                        delta.at[1, pl.ds(own_c + shown, depth_c - skip)],
                        delta.at[0, pl.ds(there + shown, depth_c - skip)],
                        sign * distance, beyond, from_beyond,
                    )
                )

    first_slice = (n == 0).astype(jnp.float32)

    def sideways(center):
        lane = lax.broadcasted_iota(jnp.int32, center.shape, 1)
        return jnp.where(lane == height - 1, 0.0, pltpu.roll(center, height - 1, 1)) + jnp.where(
            lane == 0, 0.0, pltpu.roll(center, 1, 1)
        )

    def slope(buf, layer, own_layer, r, rows):
        center = buf[layer, pl.ds(PAD + r, rows)]
        behind = buf[layer, pl.ds(PAD - 1 + r, rows)]
        total = buf[layer - 1, pl.ds(PAD + r, rows)] + buf[layer + 1, pl.ds(PAD + r, rows)]
        total = total + buf[layer, pl.ds(PAD + 1 + r, rows)]
        total = total + sideways(center)
        at = pl.ds(r, rows)
        return kappa[own_layer, at] * total + inflow[own_layer, at] * behind - decay[own_layer, at] * center

    def rate(index, z, r, chunk=chunk):
        return slope(pads.at[index], z + 1, own + z, r, chunk)

    def plain_rate(index, z, r, speed):
        buf = pads.at[index]
        center = buf[z + 1, pl.ds(PAD + r, chunk)]
        behind = buf[z + 1, pl.ds(PAD - 1 + r, chunk)]
        total = buf[z, pl.ds(PAD + r, chunk)] + buf[z + 2, pl.ds(PAD + r, chunk)]
        total = total + (behind + buf[z + 1, pl.ds(PAD + 1 + r, chunk)])
        total = total + sideways(center) - 6.0 * center
        return kappa[own + z, pl.ds(r, chunk)] * total - speed * (center - behind)

    def place(buf, layer, r, value):
        rows = value.shape[0]
        buf[layer, pl.ds(PAD + r, rows)] = value
        if r == 0:
            buf[layer, pl.ds(PAD + width, 1)] = value[:1]
        if r + rows == width:
            buf[layer, pl.ds(PAD - 1, 1)] = value[rows - 1 :]

    def fill(index, z, r, value):
        place(pads.at[index], z + 1, r, value)

    def each(lo, hi, body, unroll=1):
        def turn(z, carry):
            for r in range(0, width, chunk):
                body(z, r, chunk)
            return carry

        lax.fori_loop(lo, hi, turn, 0, unroll=unroll)

    def edges(body, needs=None, gives=None):
        for k in range(PIECES):
            if needs is not None:
                arrive(needs[k : k + 1])
            body(0, k * piece, piece)
            body(depth - 1, k * piece, piece)
            if gives is not None:
                gives[k][0].start()
                gives[k][1].start()

    def interior(body):
        each(1, depth - 1, body, 2)

    def combine(coefficients, first, z, r, chunk):
        at = pl.ds(r, chunk)
        total = (first_slice * float(coefficients[0])) * fields[0, z, at] if first is None else first
        for node in range(1, NODES):
            total = total + float(coefficients[node]) * fields[node, z, at]
        return total

    def weigh(z, r, chunk):
        fill(0, z, r, combine(slice_length * WEIGHTS, None, z, r, chunk))

    def foresee(z, r, chunk):
        fill(FIRST, z, r, combine(slice_length * INTEGRALS[0], None, z, r, chunk))

    for load in loads:
        load.wait()
    edges(weigh)
    pl.semaphore_wait(barrier, met)
    for pieces in (weighted_halo, end_halo):
        for down, up in pieces:
            down.start()
            up.start()
    shift_hop.start()
    edges(foresee, None, first_halo)
    for transfer in rim_hops:
        transfer.start()
    for z in order:
        start_hops[z].start()
    interior(weigh)
    advect = shift[...].astype(jnp.float32) / slice_length

    def look_up(layer, r, chunk):
        at = pl.ds(r, chunk)
        labels = label[layer, at]
        total = jnp.zeros((chunk, height), jnp.float32)
        for region in range(table.shape[0]):
            total = total + jnp.where(labels == region, table[region], 0.0)
        kappa[layer, at] = total
        inflow[layer, at] = total + advect
        decay[layer, at] = 6.0 * total + advect

    def prepare(z, r, chunk):
        fill(1, z, r, fields[last, z, pl.ds(r, chunk)])
        look_up(own + z, r, chunk)

    each(0, depth, prepare)

    for index in range(EXCHANGES):

        @pl.when(jnp.logical_not(within[-1]))
        def _(index=index):
            pads[index, 0, inner] = jnp.zeros((width, height), jnp.float32)

        @pl.when(jnp.logical_not(within[1]))
        def _(index=index):
            pads[index, depth + 1, inner] = jnp.zeros((width, height), jnp.float32)

    def restrict(target, layer_of):
        def turn(zc, carry):
            for r in range(0, width, chunk):
                total = layer_of(BLOCK_Z * zc, r)
                for k in range(1, BLOCK_Z):
                    total = total + layer_of(BLOCK_Z * zc + k, r)
                fold[pl.ds(r, chunk)] = total
            total = fold[pl.ds(0, rows_c, stride=BLOCK_X)]
            for k in range(1, BLOCK_X):
                total = total + fold[pl.ds(k, rows_c, stride=BLOCK_X)]
            target[zc] = total * (1.0 / (BLOCK_Z * BLOCK_X))
            return carry

        lax.fori_loop(0, depth_c, turn, 0)

    arrive(weighted_halo)
    restrict(
        gain.at[own_layers],
        lambda z, r: first_slice * fields[0, z, pl.ds(r, chunk)]
        - fields[last, z, pl.ds(r, chunk)]
        + slice_length * rate(0, z, r),
    )
    edge_hops[2].start()
    edge_hops[3].start()
    restrict(kappa_c.at[own_layers], lambda z, r: kappa[own + z, pl.ds(r, chunk)])
    edge_hops[0].start()
    edge_hops[1].start()

    def chain(wider):
        for transfer in lift_hops + edge_hops + [body_hop] + slab_hops + [front_hop]:
            transfer.wait_recv()
        for zc in range(-1, depth_c + 1) if wider else range(depth_c):
            center = delta[0, own_c + zc]
            under, over = delta[0, own_c + zc - 1], delta[0, own_c + zc + 1]
            behind = pltpu.roll(center, 1, 0)
            across = behind + pltpu.roll(center, rows_c - 1, 0)
            lateral = sideways(center)
            spreading = kappa_c[zc + 1] * (
                (under + over - 2.0 * center) * (1.0 / (BLOCK_Z * BLOCK_Z))
                + (across - 2.0 * center) * (1.0 / (BLOCK_X * BLOCK_X))
                + (lateral - 2.0 * center)
            )
            flow = (1.0 / BLOCK_X) * advect * (center - behind)
            value = center + slice_length * (spreading - flow) + (gain[zc + 1] + moved[zc + 1])
            if 0 <= zc < depth_c:
                delta[1, own_c + zc] = value
            if wider:
                front[zc + 1] = value
        for transfer in [front_hop] + rest_hops if wider else slab_hops + [body_hop]:
            transfer.start()
        for transfer in wide_hops:
            transfer.start()

    pl.when(n == 0)(lambda: chain(False))

    shift_hop.wait_recv()
    arrive(end_halo)
    advect_next = shift_next[...].astype(jnp.float32) / slice_length
    restrict(
        lift,
        lambda z, r: fields[last, z, pl.ds(r, chunk)]
        + (slice_length * float(WEIGHTS[0])) * plain_rate(1, z, r, advect_next),
    )
    for transfer in lift_hops:
        transfer.start()

    @pl.when(jnp.logical_not(has_prev))
    def _():
        def turn(z, carry):
            start[z] = fields[0, z]
            return carry

        lax.fori_loop(0, depth, turn, 0)
        rim[...] = jnp.zeros_like(rim)

    for end, there in enumerate((within[-1], within[1])):

        @pl.when(has_prev & jnp.logical_not(there))
        def _(end=end):
            rim[end] = jnp.zeros((width, height), jnp.float32)

    begin_weight = slice_length * float(INTEGRALS[0, 0])

    def combine_start(z, r, chunk):
        fill(2, z, r, combine(slice_length * INTEGRALS[0], begin_weight * start[z, pl.ds(r, chunk)], z, r, chunk))

    def open_layers(which):
        for z in which:
            start_hops[z].wait_recv()
            for r in range(0, width, chunk):
                combine_start(z, r, chunk)

    rim_hops[0].wait_recv()
    rim_hops[1].wait_recv()
    arrive(first_halo)
    for end, layer in ((0, 0), (1, depth + 1)):
        for r in range(0, width, chunk):
            at = pl.ds(PAD + r, chunk)
            pads[2, layer, at] = pads[FIRST, layer, at] + begin_weight * rim[end, pl.ds(r, chunk)]
    open_layers(order[:4])

    def fine_step(sweep, step, needs):
        old = fields if sweep == 0 else mids
        new = mids if sweep == 0 else None
        offset = 0 if sweep == 0 else -1
        index = 2 + sweep * STEPS + step
        final = sweep == FINE_SWEEPS - 1
        more = not (final and step == STEPS - 1)

        def advance(z, r, chunk):
            at = pl.ds(r, chunk)
            if step == 0:
                before = start[z, at]
            else:
                before = out[step, z, at] if final else new[step - 1, z, at]
            value = before + rate(index, z, r, chunk)
            if final:
                out[step + 1, z, at] = value
            else:
                new[step, z, at] = value
            if not more:
                return
            weights = slice_length * INTEGRALS[(step + 1) % STEPS]
            if step < STEPS - 1:
                total = slice_length * float(GAPS[step + 1]) * value
                weights[step + 1] -= slice_length * GAPS[step + 1]
                source, shown, known = old, offset, {}
            else:
                total, source, shown, known = None, new, -1, {STEPS: value}
            for node in range(NODES):
                if node == 0:
                    part = start[z, at]
                else:
                    part = known[node] if node in known else source[node + shown, z, at]
                term = float(weights[node]) * part
                total = term if total is None else total + term
            fill(index + 1, z, r, total)

        following = halo(index + 1) if more else None
        edges(advance, needs, following)
        return following, lambda: interior(advance)

    def forward(group):
        for first, second in group:
            first.wait_recv()
            second.start()

    def drain(count):
        for group in drains[:count]:
            for transfer in group:
                transfer.wait_send()
        del drains[:count]

    shares = -(-len(label_hops) // (REACH - 4))
    sent = []
    pair = None
    for stage in range(REACH - 2):
        for slice_at, slot in SLOTS.items():
            if slot == stage:
                pl.when(n == slice_at)(lambda wider=slice_at % 2 == 0: chain(wider))
        pair, rest = fine_step(stage // STEPS, stage % STEPS, pair)
        passing = sent
        sent = label_hops[stage * shares : (stage + 1) * shares]
        for group in sent:
            for first, second in group:
                first.start()
        if stage == 0:
            open_layers(order[4:])
        rest()
        for group in passing:
            forward(group)
        drain(len(drains) - 2)

    for group in label_hops:
        for first, second in group:
            second.wait_recv()
    for distance in range(1, near + 1):
        for sign in (1, -1):
            low = own + sign * distance * depth
            there = within[sign * distance]

            @pl.when(there)
            def _(low=low):
                each(low, low + depth, look_up)

            @pl.when(jnp.logical_not(there))
            def _(low=low):
                def turn(z, carry):
                    kappa[z] = jnp.zeros((width, height), jnp.float32)
                    inflow[z] = jnp.zeros((width, height), jnp.float32)
                    decay[z] = jnp.zeros((width, height), jnp.float32)
                    return carry

                lax.fori_loop(low, low + depth, turn, 0)

    pl.when((n >= LATE_SLICE) & (side == 1))(lambda: chain(False))
    if slices > LATE_SLICE + 1:
        pl.when((n >= LATE_SLICE) & (side == 0))(lambda: chain(True))
    pair, rest = fine_step(FINE_SWEEPS - 1, STEPS - 2, pair)
    rest()

    drain(len(drains) - 2)
    for group in label_hops:
        for first, second in group:
            first.wait_send()
            second.wait_send()
    for transfer in [shift_hop, front_hop, body_hop] + lift_hops + edge_hops + rim_hops + list(start_hops.values()):
        transfer.wait_send()
    for transfer in slab_hops + rest_hops + wide_hops:
        transfer.wait_send()
    for transfer in wide_hops + rest_hops:
        transfer.wait_recv()

    def mix(early, late, begin, finish):
        return (slice_length * float(early)) * begin + (slice_length * float(late)) * finish

    def widen(c, carry):
        for field in range(2):
            for k in range(BLOCK_X):
                spread[field, c, pl.ds(k, rows_c, stride=BLOCK_X)] = delta[field, c]
        for r in range(0, width, chunk):
            at = pl.ds(r, chunk)
            begin, finish = spread[0, c, at], spread[1, c, at]
            place(base, c + 1, r, mix(EARLY[0], LATE[0], begin, finish))
            for row in range(1, STEPS):
                gap, weight = float(GAPS[row]), float(TIMES[row])
                plan[row - 1, c, at] = mix(
                    EARLY[row] - gap * (1.0 - weight), LATE[row] - gap * weight, begin, finish
                )
        return carry

    lax.fori_loop(0, layers_c, widen, 0)
    base[0, inner] = jnp.zeros((width, height), jnp.float32)
    base[layers_c + 1, inner] = jnp.zeros((width, height), jnp.float32)

    def open_step(c, carry):
        for r in range(0, width, chunk):
            at, inside = pl.ds(r, chunk), pl.ds(PAD + r, chunk)
            center = base[c + 1, inside]
            behind = base[c + 1, pl.ds(PAD - 1 + r, chunk)]
            level = base[c + 1, pl.ds(PAD + 1 + r, chunk)] + sideways(center)
            initial, following = spread[0, c, at], plan[0, c, at]
            for k in range(BLOCK_Z):
                layer = BLOCK_Z * c + k
                under = base[c, inside] if k == 0 else center
                over = base[c + 2, inside] if k == BLOCK_Z - 1 else center
                total = level + (under + over)
                value = initial + (kappa[layer, at] * total + inflow[layer, at] * behind - decay[layer, at] * center)
                nodes[0, layer, at] = value
                place(grid.at[0], layer, r, float(GAPS[1]) * slice_length * value + following)
        return carry

    def wide_each(margin, body):
        def outer(i, carry):
            layer = own - margin + i + jnp.where(i >= margin, depth, 0)
            for r in range(0, width, chunk):
                body(layer, None, r)
            return carry

        def middle(z, carry):
            for r in range(0, width, chunk):
                body(own + z, z, r)
            return carry

        if margin > 0:
            lax.fori_loop(0, 2 * margin, outer, 0, unroll=min(4, 2 * margin))
        lax.fori_loop(0, depth, middle, 0, unroll=4)

    def wide_step(stage):
        sweep, step = stage // STEPS, stage % STEPS
        source, target = grid.at[(stage - 1) % 2], grid.at[stage % 2]
        margin = REACH - 1 - stage
        final = sweep == FINE_SWEEPS - 1
        more = stage < REACH - 1

        def advance(layer, z, r):
            at, c = pl.ds(r, chunk), layer // BLOCK_Z
            if step == 0 or final:
                initial = spread[0, c, at]
            if step == 0:
                before = initial
            else:
                before = latest[layer, at] if final else nodes[step - 1, layer, at]
            value = before + slope(source, layer, layer, r, chunk)
            if final:
                if more:
                    latest[layer, at] = value
                if z is not None:
                    out[step + 1, z, at] = out[step + 1, z, at] + value
                    if step == 0:
                        out[0, z, at] = start[z, at] + initial
            else:
                nodes[step, layer, at] = value
            if not more:
                return
            if not final and step < STEPS - 1:
                total = slice_length * float(GAPS[step + 1]) * value + plan[step, c, at]
            else:
                weights = slice_length * INTEGRALS[(step + 1) % STEPS]
                known = {}
                if final:
                    total = slice_length * float(GAPS[step + 1]) * value + float(weights[0]) * initial
                    weights[step + 1] -= slice_length * GAPS[step + 1]
                else:
                    total = float(weights[0]) * spread[0, c, at]
                    known = {STEPS: value}
                for node in range(1, NODES):
                    part = known[node] if node in known else nodes[node - 1, layer, at]
                    total = total + float(weights[node]) * part
            place(target, layer, r, total)

        wide_each(margin, advance)

    lax.fori_loop(0, layers_c, open_step, 0)
    for stage in range(1, STEPS):
        wide_step(stage)
    pair, rest = fine_step(FINE_SWEEPS - 1, STEPS - 1, pair)
    rest()
    drain(len(drains))
    for stage in range(STEPS, REACH):
        wide_step(stage)


def shards(node_fields, region_label, sheet_shift, diffusivity):
    fields = node_fields[0]
    nodes, depth, width, height = fields.shape
    depth_c, rows_c = depth // BLOCK_Z, width // BLOCK_X
    near = -(-REACH // depth)
    layers, layers_c = (2 * near + 1) * depth, (2 * near + 1) * depth_c
    f32 = jnp.float32
    fine, wide = (depth, width, height), (layers, width, height)
    coarse = (depth_c, rows_c, height)
    ringed = (depth_c + 2, rows_c, height)
    padded = width + 2 * PAD
    vmem, hbm = (pl.BlockSpec(memory_space=space) for space in (pltpu.VMEM, pltpu.HBM))
    result = pl.pallas_call(
        kernel,
        out_shape=jax.ShapeDtypeStruct(fields.shape, f32),
        in_specs=[hbm] * 4,
        out_specs=vmem,
        scratch_shapes=[
            pltpu.VMEM(fields.shape, f32),
            pltpu.VMEM(wide, jnp.int32),
            pltpu.VMEM(sheet_shift.shape, jnp.int32),
            pltpu.SMEM(diffusivity.shape, f32),
            pltpu.VMEM(wide, f32),
            pltpu.VMEM(wide, f32),
            pltpu.VMEM(wide, f32),
            pltpu.VMEM(ringed, f32),
            pltpu.VMEM(fine, f32),
            pltpu.VMEM((2, width, height), f32),
            pltpu.VMEM(ringed, f32),
            pltpu.VMEM(sheet_shift.shape, jnp.int32),
            pltpu.VMEM((EXCHANGES, depth + 2, padded, height), f32),
            pltpu.VMEM((STEPS,) + fine, f32),
            pltpu.VMEM(ringed, f32),
            pltpu.VMEM(coarse, f32),
            pltpu.VMEM((2, layers_c, rows_c, height), f32),
            pltpu.VMEM(ringed, f32),
            pltpu.VMEM((width, height), f32),
            pltpu.VMEM((2, layers_c, width, height), f32),
            pltpu.VMEM((STEPS - 1, layers_c, width, height), f32),
            pltpu.VMEM((layers_c + 2, padded, height), f32),
            pltpu.VMEM((2, layers, padded, height), f32),
            pltpu.VMEM((STEPS,) + wide, f32),
            pltpu.VMEM(wide, f32),
            pltpu.SemaphoreType.DMA((2 * EXCHANGES,)),
            pltpu.SemaphoreType.DMA((2 * EXCHANGES * PIECES,)),
            pltpu.SemaphoreType.DMA((8 + 4 * near,)),
            pltpu.SemaphoreType.DMA((8 + 4 * near,)),
            pltpu.SemaphoreType.DMA((depth,)),
            pltpu.SemaphoreType.DMA((depth,)),
            pltpu.SemaphoreType.DMA((2 * near,)),
            pltpu.SemaphoreType.DMA((2 * near,)),
            pltpu.SemaphoreType.DMA((4,)),
            pltpu.SemaphoreType.DMA((4,)),
            pltpu.SemaphoreType.DMA((2 * near * depth,)),
            pltpu.SemaphoreType.DMA((2 * near * depth,)),
            pltpu.SemaphoreType.DMA((NODES + 3,)),
        ],
        compiler_params=pltpu.CompilerParams(
            collective_id=0, has_side_effects=True, vmem_limit_bytes=48 * 1024 * 1024,
        ),
    )(*(pltpu.with_memory_space_constraint(x, pltpu.HBM) for x in (fields, region_label, sheet_shift, diffusivity)))
    return result[None]


def solution(mesh):
    in_specs = (P("tm", None, "space", None, None), P("space", None, None), P("tm", None), P())
    out_specs = P("tm", None, "space", None, None)
    return jax.shard_map(shards, mesh=mesh, in_specs=in_specs, out_specs=out_specs, check_vma=False)
```

```python
import math

import jax
import jax.numpy as jnp
import numpy as np
from jax import lax
from jax.experimental import pallas as pl
from jax.experimental.pallas import tpu as pltpu
from jax.sharding import PartitionSpec as P

NODES = 5
FINE_SWEEPS = 2
BLOCK_Z = 4
BLOCK_X = 2
PAD = 8
PIECES = 4
MESH = pl.DeviceIdType.MESH

slice_length = 1.0


def node_tables():
    radius = math.sqrt(3.0 / 7.0)
    points = [0.0, (1.0 - radius) / 2.0, 0.5, (1.0 + radius) / 2.0, 1.0]
    integrals = np.zeros((4, 5))
    for column in range(5):
        coeffs = [1.0]
        divisor = 1.0
        for other in range(5):
            if other != column:
                anchor = points[other]
                product = [0.0] * (len(coeffs) + 1)
                for degree in range(len(coeffs)):
                    product[degree + 1] = product[degree + 1] + coeffs[degree]
                    product[degree] = product[degree] - anchor * coeffs[degree]
                coeffs = product
                divisor = divisor * (points[column] - anchor)
        for row in range(4):
            bottom = points[row]
            summit = points[row + 1]
            amount = 0.0
            for degree in range(len(coeffs)):
                amount = amount + coeffs[degree] / (degree + 1) * (
                    summit ** (degree + 1) - bottom ** (degree + 1)
                )
            integrals[row, column] = amount / divisor
    return (np.array(points), integrals)


TIMES, INTEGRALS = node_tables()
WEIGHTS = INTEGRALS.sum(axis=0)
STEPS = NODES - 1
REACH = FINE_SWEEPS * STEPS
EXCHANGES = 3 + REACH
FIRST = EXCHANGES - 1
OPENING = {0: 0, 1: 1, FIRST: 2}
GAPS = TIMES[1:] - TIMES[:-1]
LATE = (INTEGRALS * TIMES).sum(axis=1)
EARLY = INTEGRALS.sum(axis=1) - LATE
SLOTS = {1: 0, 2: 1, 3: 2, 4: 3, 5: 4, 6: 5}
LATE_SLICE = 7


class Transfer:
    def __init__(self, src, dst, send_sem, recv_sem, device, sends, receives):
        self.copy = pltpu.make_async_remote_copy(
            src_ref=src,
            dst_ref=dst,
            send_sem=send_sem,
            recv_sem=recv_sem,
            device_id=device,
            device_id_type=MESH,
        )
        self.sends, self.receives = sends, receives

    def start(self):
        pl.when(self.sends)(self.copy.start)

    def wait_recv(self):
        pl.when(self.receives)(self.copy.wait_recv)

    def wait_send(self):
        pl.when(self.sends)(self.copy.wait_send)


def kernel(
    fields_in, label_in, shift_in, table_in, out, fields, label, shift, table,
    kappa, inflow, decay, kappa_c, start, rim, moved, shift_next, pads, mids, gain, lift, delta, front, sums, fold,
    spread, plan, base, grid, nodes, latest,
    halo_send, halo_recv, time_send, time_recv, start_send, start_recv, wide_send, wide_recv, edge_send, edge_recv,
    label_send, label_recv, load_sem,
):
    n, s = lax.axis_index("tm"), lax.axis_index("space")
    slices, slabs = lax.axis_size("tm"), lax.axis_size("space")
    depth, width, height = fields.shape[1:]
    rows_c = width // BLOCK_X
    depth_c = depth // BLOCK_Z
    near = -(-REACH // depth)
    own, own_c = near * depth, near * depth_c
    layers, layers_c = (2 * near + 1) * depth, (2 * near + 1) * depth_c
    chunk = min(64, width)
    piece = width // PIECES
    last = NODES - 1
    has_prev, has_next = n > 0, n < slices - 1
    inner = pl.ds(PAD, width)
    here_c = pl.ds(own_c, depth_c)

    loads = [
        pltpu.make_async_copy(fields_in, fields, load_sem.at[0]),
        pltpu.make_async_copy(label_in, label.at[pl.ds(own, depth)], load_sem.at[1]),
        pltpu.make_async_copy(shift_in, shift, load_sem.at[2]),
        pltpu.make_async_copy(table_in, table, load_sem.at[3]),
    ]
    for load in loads:
        load.start()

    within = {
        distance: (s + distance >= 0) & (s + distance < slabs)
        for distance in range(-near, near + 1)
    }
    for distance in range(1, near + 1):
        for sign in (1, -1):

            @pl.when(jnp.logical_not(within[sign * distance]))
            def _(distance=distance, sign=sign):
                there = own_c + sign * distance * depth_c
                delta[:, pl.ds(there, depth_c)] = jnp.zeros((2, depth_c, rows_c, height), jnp.float32)
                if distance == 1:
                    edge = depth_c + 1 if sign == 1 else 0
                    for ref in (gain, moved, kappa_c):
                        ref[edge] = jnp.zeros((rows_c, height), jnp.float32)

    @pl.when(jnp.logical_not(has_prev))
    def _():
        moved[...] = jnp.zeros_like(moved)
        delta[0] = jnp.zeros((layers_c, rows_c, height), jnp.float32)

    barrier = pltpu.get_barrier_semaphore()
    met = jnp.int32(0)
    for dn in (-1, 0, 1):
        for ds in range(-near, near + 1):
            if dn == 0 and ds == 0:
                continue
            there = (n + dn >= 0) & (n + dn < slices) & within[ds]

            @pl.when(there)
            def _(dn=dn, ds=ds):
                pl.semaphore_signal(
                    barrier, inc=1, device_id={"tm": n + dn, "space": s + ds}, device_id_type=MESH
                )

            met = met + there.astype(jnp.int32)

    drains = []

    def halo(index, source=None):
        buf = pads.at[index]
        if index in OPENING:
            count, gone, come = 1, 2 * OPENING[index], 2 * OPENING[index]
        else:
            count = PIECES
            gone = 2 * (len(OPENING) + index % 2)
            come = 2 * (len(OPENING) + (index % 2) * PIECES)
        share = width // count

        def pair(start, rows, sem):
            here = pl.ds(PAD + start, rows)
            if source is None:
                low, high = buf.at[1, here], buf.at[depth, here]
            else:
                low, high = (source.at[z, pl.ds(start, rows)] for z in (0, depth - 1))
            up = Transfer(
                high, buf.at[0, here], halo_send.at[gone], halo_recv.at[sem + 1],
                {"space": s + 1}, within[1], within[-1],
            )
            down = Transfer(
                low, buf.at[depth + 1, here], halo_send.at[gone + 1], halo_recv.at[sem],
                {"space": s - 1}, within[-1], within[1],
            )
            return down, up

        drains.append(list(pair(0, width, come)))
        return [pair(k * share, share, come + 2 * k) for k in range(count)]

    def arrive(pieces):
        for down, up in pieces:
            down.wait_recv()
            up.wait_recv()

    side = lax.rem(n, 2)
    beyond = (side == 0) & has_prev
    always = n >= 0

    def time_hop(index, src, dst, ds=0, sends=always, receives=always):
        goes = has_next & sends if ds == 0 else has_next & sends & within[ds]
        comes = has_prev & receives if ds == 0 else has_prev & receives & within[-ds]
        to = {"tm": n + 1} if ds == 0 else {"tm": n + 1, "space": s + ds}
        return Transfer(src, dst, time_send.at[index], time_recv.at[index], to, goes, comes)

    shift_hop = Transfer(
        shift_in, shift_next, time_send.at[0], time_recv.at[0], {"tm": n - 1}, has_prev, has_next
    )
    weighted_halo = halo(0)
    end_halo = halo(1, fields_in.at[last])
    first_halo = halo(FIRST)
    rim_hops = [
        time_hop(6, fields_in.at[last, depth - 1], rim.at[0], 1),
        time_hop(7, fields_in.at[last, 0], rim.at[1], -1),
    ]
    rim_depth = min(2, depth // 2)
    spans = [(0, rim_depth), (depth - rim_depth, rim_depth), (rim_depth, depth - 2 * rim_depth)]
    start_hops = [
        Transfer(
            fields_in.at[last, pl.ds(low, count)], start.at[pl.ds(low, count)],
            start_send.at[k], start_recv.at[k], {"tm": n + 1}, has_next, has_prev,
        )
        for k, (low, count) in enumerate(spans)
        if count
    ]
    half = depth // 2
    label_parts = [[] for _ in range(half)]
    label_hops, label_forwards = [], []
    for distance in range(1, near + 1):
        for sign in (1, -1):
            sem = 2 * (distance - 1) + (sign + 1) // 2
            to, sends, receives = {"space": s + sign * distance}, within[sign * distance], within[-sign * distance]
            low = side * half
            there = own - sign * distance * depth + low
            sems = label_send.at[sem], label_recv.at[sem]
            for i in range(half):
                label_parts[i].append(
                    Transfer(label_in.at[low + i], label.at[there + i], *sems, to, sends, receives)
                )
            there = pl.ds(there, half)
            label_hops.append(
                Transfer(label_in.at[pl.ds(low, half)], label.at[there], *sems, to, sends, receives)
            )
            label_forwards.append(
                Transfer(
                    label.at[there], label.at[there],
                    label_send.at[2 * near + sem], label_recv.at[2 * near + sem],
                    {"tm": n + 1 - 2 * side}, receives, receives,
                )
            )

    own_layers = pl.ds(1, depth_c)
    whole = jnp.logical_not(beyond)
    from_beyond = (side == 1) & (n > 1)
    from_whole = jnp.logical_not(from_beyond)
    lift_hops = [
        time_hop(2, lift, moved.at[own_layers]),
        time_hop(4, lift.at[depth_c - 1], moved.at[0], 1, side == 1, beyond),
        time_hop(5, lift.at[0], moved.at[depth_c + 1], -1, side == 1, beyond),
    ]
    edge_hops = []
    for k, ref in enumerate((kappa_c, gain)):
        edge_hops.append(
            Transfer(
                ref.at[depth_c], ref.at[0], edge_send.at[2 * k], edge_recv.at[2 * k],
                {"space": s + 1}, beyond & within[1], beyond & within[-1],
            )
        )
        edge_hops.append(
            Transfer(
                ref.at[1], ref.at[depth_c + 1], edge_send.at[2 * k + 1], edge_recv.at[2 * k + 1],
                {"space": s - 1}, beyond & within[-1], beyond & within[1],
            )
        )
    front_hop = time_hop(
        1, front, delta.at[0, pl.ds(own_c - 1, depth_c + 2)], 0, beyond, from_beyond
    )
    body_hop = time_hop(3, delta.at[1, here_c], delta.at[0, here_c], 0, whole, from_whole)
    wide_hops, rest_hops, slab_hops = [], [], []
    for distance in range(1, near + 1):
        for sign in (1, -1):
            sem = 2 * (distance - 1) + (sign + 1) // 2
            there = own_c - sign * distance * depth_c
            wide_hops.append(
                Transfer(
                    delta.at[1, here_c], delta.at[1, pl.ds(there, depth_c)],
                    wide_send.at[sem], wide_recv.at[sem],
                    {"space": s + sign * distance}, within[sign * distance], within[-sign * distance],
                )
            )
            slab_hops.append(
                time_hop(
                    8 + 2 * near + sem, delta.at[1, here_c], delta.at[0, pl.ds(there, depth_c)],
                    sign * distance, whole, from_whole,
                )
            )
            skip = 1 if distance == 1 else 0
            if depth_c > skip:
                shown = skip if sign == -1 else 0
                rest_hops.append(
                    time_hop(
                        8 + sem,
                        delta.at[1, pl.ds(own_c + shown, depth_c - skip)],
                        delta.at[0, pl.ds(there + shown, depth_c - skip)],
                        sign * distance, beyond, from_beyond,
                    )
                )

    first_slice = (n == 0).astype(jnp.float32)

    def sideways(center):
        lane = lax.broadcasted_iota(jnp.int32, center.shape, 1)
        return jnp.where(lane == height - 1, 0.0, pltpu.roll(center, height - 1, 1)) + jnp.where(
            lane == 0, 0.0, pltpu.roll(center, 1, 1)
        )

    def slope(buf, layer, own_layer, r, rows):
        center = buf[layer, pl.ds(PAD + r, rows)]
        behind = buf[layer, pl.ds(PAD - 1 + r, rows)]
        total = buf[layer - 1, pl.ds(PAD + r, rows)] + buf[layer + 1, pl.ds(PAD + r, rows)]
        total = total + buf[layer, pl.ds(PAD + 1 + r, rows)]
        total = total + sideways(center)
        at = pl.ds(r, rows)
        return kappa[own_layer, at] * total + inflow[own_layer, at] * behind - decay[own_layer, at] * center

    def rate(index, z, r, chunk=chunk):
        return slope(pads.at[index], z + 1, own + z, r, chunk)

    def plain_rate(index, z, r, speed):
        buf = pads.at[index]
        center = buf[z + 1, pl.ds(PAD + r, chunk)]
        behind = buf[z + 1, pl.ds(PAD - 1 + r, chunk)]
        total = buf[z, pl.ds(PAD + r, chunk)] + buf[z + 2, pl.ds(PAD + r, chunk)]
        total = total + (behind + buf[z + 1, pl.ds(PAD + 1 + r, chunk)])
        total = total + sideways(center) - 6.0 * center
        return kappa[own + z, pl.ds(r, chunk)] * total - speed * (center - behind)

    def place(buf, layer, r, value):
        rows = value.shape[0]
        buf[layer, pl.ds(PAD + r, rows)] = value
        if r == 0:
            buf[layer, pl.ds(PAD + width, 1)] = value[:1]
        if r + rows == width:
            buf[layer, pl.ds(PAD - 1, 1)] = value[rows - 1 :]

    def fill(index, z, r, value):
        place(pads.at[index], z + 1, r, value)

    def each(lo, hi, body, unroll=1):
        def turn(z, carry):
            for r in range(0, width, chunk):
                body(z, r, chunk)
            return carry

        lax.fori_loop(lo, hi, turn, 0, unroll=unroll)

    def edges(body, needs=None, gives=None):
        count = PIECES if gives is None else len(gives)
        rows = width // count
        for k in range(count):
            if needs is not None:
                arrive(needs[k : k + 1])
            body(0, k * rows, rows)
            body(depth - 1, k * rows, rows)
            if gives is not None:
                gives[k][0].start()
                gives[k][1].start()

    def interior(body):
        each(1, depth - 1, body, 2)

    def combine(coefficients, first, z, r, chunk):
        at = pl.ds(r, chunk)
        total = (first_slice * float(coefficients[0])) * fields[0, z, at] if first is None else first
        for node in range(1, NODES):
            total = total + float(coefficients[node]) * fields[node, z, at]
        return total

    def weigh(z, r, chunk):
        fill(0, z, r, combine(slice_length * WEIGHTS, None, z, r, chunk))

    def foresee(z, r, chunk):
        fill(FIRST, z, r, combine(slice_length * INTEGRALS[0], None, z, r, chunk))

    for load in loads:
        load.wait()
    edges(weigh)
    pl.semaphore_wait(barrier, met)
    for pieces in (weighted_halo, end_halo):
        for down, up in pieces:
            down.start()
            up.start()
    shift_hop.start()
    edges(foresee, None, first_halo)
    for transfer in rim_hops:
        transfer.start()
    for transfer in start_hops:
        transfer.start()
    interior(weigh)
    advect = shift[...].astype(jnp.float32) / slice_length

    def look_up(layer, r, chunk):
        at = pl.ds(r, chunk)
        labels = label[layer, at]
        total = jnp.zeros((chunk, height), jnp.float32)
        for region in range(table.shape[0]):
            total = total + jnp.where(labels == region, table[region], 0.0)
        kappa[layer, at] = total
        inflow[layer, at] = total + advect
        decay[layer, at] = 6.0 * total + advect

    def prepare(z, r, chunk):
        fill(1, z, r, fields[last, z, pl.ds(r, chunk)])
        look_up(own + z, r, chunk)

    each(0, depth, prepare)

    for index in range(EXCHANGES):

        @pl.when(jnp.logical_not(within[-1]))
        def _(index=index):
            pads[index, 0, inner] = jnp.zeros((width, height), jnp.float32)

        @pl.when(jnp.logical_not(within[1]))
        def _(index=index):
            pads[index, depth + 1, inner] = jnp.zeros((width, height), jnp.float32)

    def restrict(target, layer_of):
        def turn(zc, carry):
            for r in range(0, width, chunk):
                total = layer_of(BLOCK_Z * zc, r)
                for k in range(1, BLOCK_Z):
                    total = total + layer_of(BLOCK_Z * zc + k, r)
                fold[pl.ds(r, chunk)] = total
            total = fold[pl.ds(0, rows_c, stride=BLOCK_X)]
            for k in range(1, BLOCK_X):
                total = total + fold[pl.ds(k, rows_c, stride=BLOCK_X)]
            target[zc] = total * (1.0 / (BLOCK_Z * BLOCK_X))
            return carry

        lax.fori_loop(0, depth_c, turn, 0)

    def block_sums(index, layer_of):
        for zc in range(depth_c):
            inside = [z for z in range(BLOCK_Z * zc, BLOCK_Z * (zc + 1)) if 0 < z < depth - 1]
            for r in range(0, width, chunk):
                total = layer_of(inside[0], r)
                for z in inside[1:]:
                    total = total + layer_of(z, r)
                sums[index, zc, pl.ds(r, chunk)] = total

    def close(index, target, layer_of):
        for zc in range(depth_c):
            for r in range(0, width, chunk):
                total = sums[index, zc, pl.ds(r, chunk)]
                if zc == 0:
                    total = total + layer_of(0, r)
                if zc == depth_c - 1:
                    total = total + layer_of(depth - 1, r)
                fold[pl.ds(r, chunk)] = total
            total = fold[pl.ds(0, rows_c, stride=BLOCK_X)]
            for k in range(1, BLOCK_X):
                total = total + fold[pl.ds(k, rows_c, stride=BLOCK_X)]
            target[zc] = total * (1.0 / (BLOCK_Z * BLOCK_X))

    def gain_layer(z, r):
        at = pl.ds(r, chunk)
        return first_slice * fields[0, z, at] - fields[last, z, at] + slice_length * rate(0, z, r)

    def lift_layer(z, r):
        weight = slice_length * float(WEIGHTS[0])
        return fields[last, z, pl.ds(r, chunk)] + weight * plain_rate(1, z, r, advect_next)

    restrict(kappa_c.at[own_layers], lambda z, r: kappa[own + z, pl.ds(r, chunk)])
    edge_hops[0].start()
    edge_hops[1].start()
    block_sums(0, gain_layer)
    shift_hop.wait_recv()
    advect_next = shift_next[...].astype(jnp.float32) / slice_length
    block_sums(1, lift_layer)
    arrive(weighted_halo)
    close(0, gain.at[own_layers], gain_layer)
    edge_hops[2].start()
    edge_hops[3].start()

    def chain(wider):
        for transfer in lift_hops + edge_hops + [body_hop] + slab_hops + [front_hop]:
            transfer.wait_recv()
        for zc in range(-1, depth_c + 1) if wider else range(depth_c):
            center = delta[0, own_c + zc]
            under, over = delta[0, own_c + zc - 1], delta[0, own_c + zc + 1]
            behind = pltpu.roll(center, 1, 0)
            across = behind + pltpu.roll(center, rows_c - 1, 0)
            lateral = sideways(center)
            spreading = kappa_c[zc + 1] * (
                (under + over - 2.0 * center) * (1.0 / (BLOCK_Z * BLOCK_Z))
                + (across - 2.0 * center) * (1.0 / (BLOCK_X * BLOCK_X))
                + (lateral - 2.0 * center)
            )
            flow = (1.0 / BLOCK_X) * advect * (center - behind)
            value = center + slice_length * (spreading - flow) + (gain[zc + 1] + moved[zc + 1])
            if 0 <= zc < depth_c:
                delta[1, own_c + zc] = value
            if wider:
                front[zc + 1] = value
        for transfer in [front_hop] if wider else slab_hops + [body_hop]:
            transfer.start()

    def spread_ends():
        for transfer in rest_hops + wide_hops:
            transfer.start()

    pl.when(n == 0)(lambda: chain(False))

    arrive(end_halo)
    close(1, lift, lift_layer)
    for transfer in lift_hops:
        transfer.start()

    @pl.when(jnp.logical_not(has_prev))
    def _():
        def turn(z, carry):
            start[z] = fields[0, z]
            return carry

        lax.fori_loop(0, depth, turn, 0)
        rim[...] = jnp.zeros_like(rim)

    for end, there in enumerate((within[-1], within[1])):

        @pl.when(has_prev & jnp.logical_not(there))
        def _(end=end):
            rim[end] = jnp.zeros((width, height), jnp.float32)

    begin_weight = slice_length * float(INTEGRALS[0, 0])

    def combine_start(z, r, chunk):
        fill(2, z, r, combine(slice_length * INTEGRALS[0], begin_weight * start[z, pl.ds(r, chunk)], z, r, chunk))

    def open_layers(which):
        for k in which:
            start_hops[k].wait_recv()
            low, count = spans[k]
            for z in range(low, low + count):
                for r in range(0, width, chunk):
                    combine_start(z, r, chunk)

    rim_hops[0].wait_recv()
    rim_hops[1].wait_recv()
    arrive(first_halo)
    for end, layer in ((0, 0), (1, depth + 1)):
        for r in range(0, width, chunk):
            at = pl.ds(PAD + r, chunk)
            pads[2, layer, at] = pads[FIRST, layer, at] + begin_weight * rim[end, pl.ds(r, chunk)]
    open_layers((0, 1))

    def fine_step(sweep, step, needs):
        old = fields if sweep == 0 else mids
        new = mids if sweep == 0 else None
        offset = 0 if sweep == 0 else -1
        index = 2 + sweep * STEPS + step
        final = sweep == FINE_SWEEPS - 1
        more = not (final and step == STEPS - 1)

        def advance(z, r, chunk):
            at = pl.ds(r, chunk)
            if step == 0:
                before = start[z, at]
            else:
                before = out[step, z, at] if final else new[step - 1, z, at]
            value = before + rate(index, z, r, chunk)
            if final:
                out[step + 1, z, at] = value
            else:
                new[step, z, at] = value
            if not more:
                return
            weights = slice_length * INTEGRALS[(step + 1) % STEPS]
            if step < STEPS - 1:
                total = slice_length * float(GAPS[step + 1]) * value
                weights[step + 1] -= slice_length * GAPS[step + 1]
                source, shown, known = old, offset, {}
            else:
                total, source, shown, known = None, new, -1, {STEPS: value}
            for node in range(NODES):
                if node == 0:
                    part = start[z, at]
                else:
                    part = known[node] if node in known else source[node + shown, z, at]
                term = float(weights[node]) * part
                total = term if total is None else total + term
            fill(index + 1, z, r, total)

        following = halo(index + 1) if more else None
        edges(advance, needs, following)
        return following, lambda: interior(advance)

    def drain(count):
        for group in drains[:count]:
            for transfer in group:
                transfer.wait_send()
        del drains[:count]

    pair = None
    for stage in range(REACH - 2):
        turns = [slice_at for slice_at, slot in SLOTS.items() if slot == stage]
        for slice_at in turns:
            pl.when(n == slice_at)(lambda wider=slice_at % 2 == 0: chain(wider))
        pair, rest = fine_step(stage // STEPS, stage % STEPS, pair)
        if stage < half:
            for transfer in label_parts[stage]:
                transfer.start()
        for slice_at in turns + ([0] if stage == 0 else []):
            pl.when(n == slice_at)(spread_ends)
        if stage == 0:
            open_layers(range(2, len(start_hops)))
        rest()
        if stage == half:
            for first, second in zip(label_hops, label_forwards):
                first.wait_recv()
                second.start()
        drain(len(drains) - 1)

    for transfer in label_forwards:
        transfer.wait_recv()
    for distance in range(1, near + 1):
        for sign in (1, -1):
            low = own + sign * distance * depth
            there = within[sign * distance]

            @pl.when(there)
            def _(low=low):
                each(low, low + depth, look_up)

            @pl.when(jnp.logical_not(there))
            def _(low=low):
                def turn(z, carry):
                    kappa[z] = jnp.zeros((width, height), jnp.float32)
                    inflow[z] = jnp.zeros((width, height), jnp.float32)
                    decay[z] = jnp.zeros((width, height), jnp.float32)
                    return carry

                lax.fori_loop(low, low + depth, turn, 0)

    pl.when((n >= LATE_SLICE) & (side == 1))(lambda: chain(False))
    if slices > LATE_SLICE + 1:
        pl.when((n >= LATE_SLICE) & (side == 0))(lambda: chain(True))
    pl.when(n >= LATE_SLICE)(spread_ends)
    pair, rest = fine_step(FINE_SWEEPS - 1, STEPS - 2, pair)
    rest()

    drain(len(drains) - 1)
    for transfer in label_hops + label_forwards + lift_hops + edge_hops + rim_hops + start_hops:
        transfer.wait_send()
    for transfer in [shift_hop, front_hop, body_hop] + slab_hops + rest_hops + wide_hops:
        transfer.wait_send()
    for transfer in wide_hops + rest_hops:
        transfer.wait_recv()

    def mix(early, late, begin, finish):
        return (slice_length * float(early)) * begin + (slice_length * float(late)) * finish

    def widen(c, carry):
        for field in range(2):
            for k in range(BLOCK_X):
                spread[field, c, pl.ds(k, rows_c, stride=BLOCK_X)] = delta[field, c]
        for r in range(0, width, chunk):
            at = pl.ds(r, chunk)
            begin, finish = spread[0, c, at], spread[1, c, at]
            place(base, c + 1, r, mix(EARLY[0], LATE[0], begin, finish))
            for row in range(1, STEPS):
                gap, weight = float(GAPS[row]), float(TIMES[row])
                plan[row - 1, c, at] = mix(
                    EARLY[row] - gap * (1.0 - weight), LATE[row] - gap * weight, begin, finish
                )
        return carry

    lax.fori_loop(0, layers_c, widen, 0)
    base[0, inner] = jnp.zeros((width, height), jnp.float32)
    base[layers_c + 1, inner] = jnp.zeros((width, height), jnp.float32)

    def open_step(c, carry):
        for r in range(0, width, chunk):
            at, inside = pl.ds(r, chunk), pl.ds(PAD + r, chunk)
            center = base[c + 1, inside]
            behind = base[c + 1, pl.ds(PAD - 1 + r, chunk)]
            level = base[c + 1, pl.ds(PAD + 1 + r, chunk)] + sideways(center)
            initial, following = spread[0, c, at], plan[0, c, at]
            for k in range(BLOCK_Z):
                layer = BLOCK_Z * c + k
                under = base[c, inside] if k == 0 else center
                over = base[c + 2, inside] if k == BLOCK_Z - 1 else center
                total = level + (under + over)
                value = initial + (kappa[layer, at] * total + inflow[layer, at] * behind - decay[layer, at] * center)
                nodes[0, layer, at] = value
                place(grid.at[0], layer, r, float(GAPS[1]) * slice_length * value + following)
        return carry

    def wide_each(margin, body, apart):
        if not apart:

            def through(i, carry):
                for r in range(0, width, chunk):
                    body(own - margin + i, None, r)
                return carry

            lax.fori_loop(0, depth + 2 * margin, through, 0, unroll=4)
            return

        def outer(i, carry):
            layer = own - margin + i + jnp.where(i >= margin, depth, 0)
            for r in range(0, width, chunk):
                body(layer, None, r)
            return carry

        def middle(z, carry):
            for r in range(0, width, chunk):
                body(own + z, z, r)
            return carry

        if margin > 0:
            lax.fori_loop(0, 2 * margin, outer, 0, unroll=min(4, 2 * margin))
        lax.fori_loop(0, depth, middle, 0, unroll=4)

    def wide_step(stage):
        sweep, step = stage // STEPS, stage % STEPS
        source, target = grid.at[(stage - 1) % 2], grid.at[stage % 2]
        margin = REACH - 1 - stage
        final = sweep == FINE_SWEEPS - 1
        more = stage < REACH - 1

        def advance(layer, z, r):
            at, c = pl.ds(r, chunk), layer // BLOCK_Z
            if step == 0 or final:
                initial = spread[0, c, at]
            if step == 0:
                before = initial
            else:
                before = latest[layer, at] if final else nodes[step - 1, layer, at]
            value = before + slope(source, layer, layer, r, chunk)
            if final:
                if more:
                    latest[layer, at] = value
                if z is not None:
                    out[step + 1, z, at] = out[step + 1, z, at] + value
                    if step == 0:
                        out[0, z, at] = start[z, at] + initial
            else:
                nodes[step, layer, at] = value
            if not more:
                return
            if not final and step < STEPS - 1:
                total = slice_length * float(GAPS[step + 1]) * value + plan[step, c, at]
            else:
                weights = slice_length * INTEGRALS[(step + 1) % STEPS]
                known = {}
                if final:
                    total = slice_length * float(GAPS[step + 1]) * value + float(weights[0]) * initial
                    weights[step + 1] -= slice_length * GAPS[step + 1]
                else:
                    total = float(weights[0]) * spread[0, c, at]
                    known = {STEPS: value}
                for node in range(1, NODES):
                    part = known[node] if node in known else nodes[node - 1, layer, at]
                    total = total + float(weights[node]) * part
            place(target, layer, r, total)

        wide_each(margin, advance, final)

    lax.fori_loop(0, layers_c, open_step, 0)
    for stage in range(1, STEPS):
        wide_step(stage)
    pair, rest = fine_step(FINE_SWEEPS - 1, STEPS - 1, pair)
    rest()
    drain(len(drains))
    for stage in range(STEPS, REACH):
        wide_step(stage)


def shards(node_fields, region_label, sheet_shift, diffusivity):
    fields = node_fields[0]
    nodes, depth, width, height = fields.shape
    depth_c, rows_c = depth // BLOCK_Z, width // BLOCK_X
    near = -(-REACH // depth)
    layers, layers_c = (2 * near + 1) * depth, (2 * near + 1) * depth_c
    f32 = jnp.float32
    fine, wide = (depth, width, height), (layers, width, height)
    coarse = (depth_c, rows_c, height)
    ringed = (depth_c + 2, rows_c, height)
    padded = width + 2 * PAD
    vmem, hbm = (pl.BlockSpec(memory_space=space) for space in (pltpu.VMEM, pltpu.HBM))
    result = pl.pallas_call(
        kernel,
        out_shape=jax.ShapeDtypeStruct(fields.shape, f32),
        in_specs=[hbm] * 4,
        out_specs=vmem,
        scratch_shapes=[
            pltpu.VMEM(fields.shape, f32),
            pltpu.VMEM(wide, jnp.int32),
            pltpu.VMEM(sheet_shift.shape, jnp.int32),
            pltpu.SMEM(diffusivity.shape, f32),
            pltpu.VMEM(wide, f32),
            pltpu.VMEM(wide, f32),
            pltpu.VMEM(wide, f32),
            pltpu.VMEM(ringed, f32),
            pltpu.VMEM(fine, f32),
            pltpu.VMEM((2, width, height), f32),
            pltpu.VMEM(ringed, f32),
            pltpu.VMEM(sheet_shift.shape, jnp.int32),
            pltpu.VMEM((EXCHANGES, depth + 2, padded, height), f32),
            pltpu.VMEM((STEPS,) + fine, f32),
            pltpu.VMEM(ringed, f32),
            pltpu.VMEM(coarse, f32),
            pltpu.VMEM((2, layers_c, rows_c, height), f32),
            pltpu.VMEM(ringed, f32),
            pltpu.VMEM((2, depth_c, width, height), f32),
            pltpu.VMEM((width, height), f32),
            pltpu.VMEM((2, layers_c, width, height), f32),
            pltpu.VMEM((STEPS - 1, layers_c, width, height), f32),
            pltpu.VMEM((layers_c + 2, padded, height), f32),
            pltpu.VMEM((2, layers, padded, height), f32),
            pltpu.VMEM((STEPS,) + wide, f32),
            pltpu.VMEM(wide, f32),
            pltpu.SemaphoreType.DMA((2 * len(OPENING) + 4,)),
            pltpu.SemaphoreType.DMA((2 * len(OPENING) + 4 * PIECES,)),
            pltpu.SemaphoreType.DMA((8 + 4 * near,)),
            pltpu.SemaphoreType.DMA((8 + 4 * near,)),
            pltpu.SemaphoreType.DMA((3,)),
            pltpu.SemaphoreType.DMA((3,)),
            pltpu.SemaphoreType.DMA((2 * near,)),
            pltpu.SemaphoreType.DMA((2 * near,)),
            pltpu.SemaphoreType.DMA((4,)),
            pltpu.SemaphoreType.DMA((4,)),
            pltpu.SemaphoreType.DMA((4 * near,)),
            pltpu.SemaphoreType.DMA((4 * near,)),
            pltpu.SemaphoreType.DMA((4,)),
        ],
        compiler_params=pltpu.CompilerParams(
            collective_id=0, has_side_effects=True, vmem_limit_bytes=48 * 1024 * 1024,
        ),
    )(*(pltpu.with_memory_space_constraint(x, pltpu.HBM) for x in (fields, region_label, sheet_shift, diffusivity)))
    return result[None]


def solution(mesh):
    in_specs = (P("tm", None, "space", None, None), P("space", None, None), P("tm", None), P())
    out_specs = P("tm", None, "space", None, None)
    return jax.shard_map(shards, mesh=mesh, in_specs=in_specs, out_specs=out_specs, check_vma=False)
```

```python
import math

import jax
import jax.numpy as jnp
import numpy as np
from jax import lax
from jax.experimental import pallas as pl
from jax.experimental.pallas import tpu as pltpu
from jax.sharding import PartitionSpec as P

NODES = 5
FINE_SWEEPS = 2
BLOCK_Z = 4
BLOCK_X = 2
PAD = 8
PIECES = 4
MESH = pl.DeviceIdType.MESH

slice_length = 1.0


def node_tables():
    radius = math.sqrt(3.0 / 7.0)
    points = [0.0, (1.0 - radius) / 2.0, 0.5, (1.0 + radius) / 2.0, 1.0]
    integrals = np.zeros((4, 5))
    for column in range(5):
        coeffs = [1.0]
        divisor = 1.0
        for other in range(5):
            if other != column:
                anchor = points[other]
                product = [0.0] * (len(coeffs) + 1)
                for degree in range(len(coeffs)):
                    product[degree + 1] = product[degree + 1] + coeffs[degree]
                    product[degree] = product[degree] - anchor * coeffs[degree]
                coeffs = product
                divisor = divisor * (points[column] - anchor)
        for row in range(4):
            bottom = points[row]
            summit = points[row + 1]
            amount = 0.0
            for degree in range(len(coeffs)):
                amount = amount + coeffs[degree] / (degree + 1) * (
                    summit ** (degree + 1) - bottom ** (degree + 1)
                )
            integrals[row, column] = amount / divisor
    return (np.array(points), integrals)


TIMES, INTEGRALS = node_tables()
WEIGHTS = INTEGRALS.sum(axis=0)
STEPS = NODES - 1
REACH = FINE_SWEEPS * STEPS
EXCHANGES = 3 + REACH
FIRST = EXCHANGES - 1
OPENING = {0: 0, 1: 1, FIRST: 2}
GAPS = TIMES[1:] - TIMES[:-1]
LATE = (INTEGRALS * TIMES).sum(axis=1)
EARLY = INTEGRALS.sum(axis=1) - LATE
SLOTS = {1: 0, 2: 2, 3: 2, 4: 4, 5: 4, 6: 5}
LATE_SLICE = 7


class Transfer:
    def __init__(self, src, dst, send_sem, recv_sem, device, sends, receives):
        self.copy = pltpu.make_async_remote_copy(
            src_ref=src,
            dst_ref=dst,
            send_sem=send_sem,
            recv_sem=recv_sem,
            device_id=device,
            device_id_type=MESH,
        )
        self.sends, self.receives = sends, receives

    def start(self):
        pl.when(self.sends)(self.copy.start)

    def wait_recv(self):
        pl.when(self.receives)(self.copy.wait_recv)

    def wait_send(self):
        pl.when(self.sends)(self.copy.wait_send)


def kernel(
    fields_in, label_in, shift_in, table_in, out, fields, label, shift, table,
    kappa, inflow, decay, kappa_c, start, rim, moved, shift_next, pads, mids, gain, lift, delta, front, sums, fold,
    spread, plan, base, grid, nodes, latest,
    halo_send, halo_recv, time_send, time_recv, start_send, start_recv, wide_send, wide_recv, edge_send, edge_recv,
    label_send, label_recv, load_sem,
):
    n, s = lax.axis_index("tm"), lax.axis_index("space")
    slices, slabs = lax.axis_size("tm"), lax.axis_size("space")
    depth, width, height = fields.shape[1:]
    rows_c = width // BLOCK_X
    depth_c = depth // BLOCK_Z
    near = -(-REACH // depth)
    own, own_c = near * depth, near * depth_c
    layers, layers_c = (2 * near + 1) * depth, (2 * near + 1) * depth_c
    chunk = min(64, width)
    piece = width // PIECES
    last = NODES - 1
    has_prev, has_next = n > 0, n < slices - 1
    inner = pl.ds(PAD, width)
    here_c = pl.ds(own_c, depth_c)

    loads = [
        pltpu.make_async_copy(fields_in, fields, load_sem.at[0]),
        pltpu.make_async_copy(label_in, label.at[pl.ds(own, depth)], load_sem.at[1]),
        pltpu.make_async_copy(shift_in, shift, load_sem.at[2]),
        pltpu.make_async_copy(table_in, table, load_sem.at[3]),
    ]
    for load in loads:
        load.start()

    within = {
        distance: (s + distance >= 0) & (s + distance < slabs)
        for distance in range(-near, near + 1)
    }
    for distance in range(1, near + 1):
        for sign in (1, -1):

            @pl.when(jnp.logical_not(within[sign * distance]))
            def _(distance=distance, sign=sign):
                there = own_c + sign * distance * depth_c
                delta[:, pl.ds(there, depth_c)] = jnp.zeros((2, depth_c, rows_c, height), jnp.float32)
                if distance == 1:
                    edge = depth_c + 1 if sign == 1 else 0
                    for ref in (gain, moved, kappa_c):
                        ref[edge] = jnp.zeros((rows_c, height), jnp.float32)

    @pl.when(jnp.logical_not(has_prev))
    def _():
        moved[...] = jnp.zeros_like(moved)
        delta[0] = jnp.zeros((layers_c, rows_c, height), jnp.float32)

    barrier = pltpu.get_barrier_semaphore()
    met = jnp.int32(0)
    for dn in (-1, 0, 1):
        for ds in range(-near, near + 1):
            if dn == 0 and ds == 0:
                continue
            there = (n + dn >= 0) & (n + dn < slices) & within[ds]

            @pl.when(there)
            def _(dn=dn, ds=ds):
                pl.semaphore_signal(
                    barrier, inc=1, device_id={"tm": n + dn, "space": s + ds}, device_id_type=MESH
                )

            met = met + there.astype(jnp.int32)

    drains = []

    def halo(index, source=None):
        buf = pads.at[index]
        if index in OPENING:
            count, gone, come = 1, 2 * OPENING[index], 2 * OPENING[index]
        else:
            count = PIECES
            gone = 2 * (len(OPENING) + index % 2)
            come = 2 * (len(OPENING) + (index % 2) * PIECES)
        share = width // count

        def pair(start, rows, sem):
            here = pl.ds(PAD + start, rows)
            if source is None:
                low, high = buf.at[1, here], buf.at[depth, here]
            else:
                low, high = (source.at[z, pl.ds(start, rows)] for z in (0, depth - 1))
            up = Transfer(
                high, buf.at[0, here], halo_send.at[gone], halo_recv.at[sem + 1],
                {"space": s + 1}, within[1], within[-1],
            )
            down = Transfer(
                low, buf.at[depth + 1, here], halo_send.at[gone + 1], halo_recv.at[sem],
                {"space": s - 1}, within[-1], within[1],
            )
            return down, up

        drains.append(list(pair(0, width, come)))
        return [pair(k * share, share, come + 2 * k) for k in range(count)]

    def arrive(pieces):
        for down, up in pieces:
            down.wait_recv()
            up.wait_recv()

    side = lax.rem(n, 2)
    beyond = (side == 0) & has_prev
    always = n >= 0

    def time_hop(index, src, dst, ds=0, sends=always, receives=always):
        goes = has_next & sends if ds == 0 else has_next & sends & within[ds]
        comes = has_prev & receives if ds == 0 else has_prev & receives & within[-ds]
        to = {"tm": n + 1} if ds == 0 else {"tm": n + 1, "space": s + ds}
        return Transfer(src, dst, time_send.at[index], time_recv.at[index], to, goes, comes)

    shift_hop = Transfer(
        shift_in, shift_next, time_send.at[0], time_recv.at[0], {"tm": n - 1}, has_prev, has_next
    )
    weighted_halo = halo(0)
    end_halo = halo(1, fields_in.at[last])
    first_halo = halo(FIRST)
    rim_hops = [
        time_hop(6, fields_in.at[last, depth - 1], rim.at[0], 1),
        time_hop(7, fields_in.at[last, 0], rim.at[1], -1),
    ]
    rim_depth = min(2, depth // 2)
    spans = [(0, rim_depth), (depth - rim_depth, rim_depth), (rim_depth, depth - 2 * rim_depth)]
    start_hops = [
        Transfer(
            fields_in.at[last, pl.ds(low, count)], start.at[pl.ds(low, count)],
            start_send.at[k], start_recv.at[k], {"tm": n + 1}, has_next, has_prev,
        )
        for k, (low, count) in enumerate(spans)
        if count
    ]
    half = depth // 2
    label_parts = [[] for _ in range(half)]
    label_hops, label_forwards = [], []
    for distance in range(1, near + 1):
        for sign in (1, -1):
            sem = 2 * (distance - 1) + (sign + 1) // 2
            to, sends, receives = {"space": s + sign * distance}, within[sign * distance], within[-sign * distance]
            low = side * half
            there = own - sign * distance * depth + low
            sems = label_send.at[sem], label_recv.at[sem]
            for i in range(half):
                label_parts[i].append(
                    Transfer(label_in.at[low + i], label.at[there + i], *sems, to, sends, receives)
                )
            there = pl.ds(there, half)
            label_hops.append(
                Transfer(label_in.at[pl.ds(low, half)], label.at[there], *sems, to, sends, receives)
            )
            label_forwards.append(
                Transfer(
                    label.at[there], label.at[there],
                    label_send.at[2 * near + sem], label_recv.at[2 * near + sem],
                    {"tm": n + 1 - 2 * side}, receives, receives,
                )
            )

    own_layers = pl.ds(1, depth_c)
    whole = jnp.logical_not(beyond)
    from_beyond = (side == 1) & (n > 1)
    from_whole = jnp.logical_not(from_beyond)
    lift_hops = [
        time_hop(2, lift, moved.at[own_layers]),
        time_hop(4, lift.at[depth_c - 1], moved.at[0], 1, side == 1, beyond),
        time_hop(5, lift.at[0], moved.at[depth_c + 1], -1, side == 1, beyond),
    ]
    edge_hops = []
    for k, ref in enumerate((kappa_c, gain)):
        edge_hops.append(
            Transfer(
                ref.at[depth_c], ref.at[0], edge_send.at[2 * k], edge_recv.at[2 * k],
                {"space": s + 1}, beyond & within[1], beyond & within[-1],
            )
        )
        edge_hops.append(
            Transfer(
                ref.at[1], ref.at[depth_c + 1], edge_send.at[2 * k + 1], edge_recv.at[2 * k + 1],
                {"space": s - 1}, beyond & within[-1], beyond & within[1],
            )
        )
    front_hop = time_hop(
        1, front, delta.at[0, pl.ds(own_c - 1, depth_c + 2)], 0, beyond, from_beyond
    )
    body_hop = time_hop(3, delta.at[1, here_c], delta.at[0, here_c], 0, whole, from_whole)
    wide_hops, rest_hops, slab_hops = [], [], []
    for distance in range(1, near + 1):
        for sign in (1, -1):
            sem = 2 * (distance - 1) + (sign + 1) // 2
            there = own_c - sign * distance * depth_c
            wide_hops.append(
                Transfer(
                    delta.at[1, here_c], delta.at[1, pl.ds(there, depth_c)],
                    wide_send.at[sem], wide_recv.at[sem],
                    {"space": s + sign * distance}, within[sign * distance], within[-sign * distance],
                )
            )
            slab_hops.append(
                time_hop(
                    8 + 2 * near + sem, delta.at[1, here_c], delta.at[0, pl.ds(there, depth_c)],
                    sign * distance, whole, from_whole,
                )
            )
            skip = 1 if distance == 1 else 0
            if depth_c > skip:
                shown = skip if sign == -1 else 0
                rest_hops.append(
                    time_hop(
                        8 + sem,
                        delta.at[1, pl.ds(own_c + shown, depth_c - skip)],
                        delta.at[0, pl.ds(there + shown, depth_c - skip)],
                        sign * distance, beyond, from_beyond,
                    )
                )

    first_slice = (n == 0).astype(jnp.float32)

    def sideways(center):
        lane = lax.broadcasted_iota(jnp.int32, center.shape, 1)
        return jnp.where(lane == height - 1, 0.0, pltpu.roll(center, height - 1, 1)) + jnp.where(
            lane == 0, 0.0, pltpu.roll(center, 1, 1)
        )

    def slope(buf, layer, own_layer, r, rows):
        center = buf[layer, pl.ds(PAD + r, rows)]
        behind = buf[layer, pl.ds(PAD - 1 + r, rows)]
        total = buf[layer - 1, pl.ds(PAD + r, rows)] + buf[layer + 1, pl.ds(PAD + r, rows)]
        total = total + buf[layer, pl.ds(PAD + 1 + r, rows)]
        total = total + sideways(center)
        at = pl.ds(r, rows)
        return kappa[own_layer, at] * total + inflow[own_layer, at] * behind - decay[own_layer, at] * center

    def rate(index, z, r, chunk=chunk):
        return slope(pads.at[index], z + 1, own + z, r, chunk)

    def plain_rate(index, z, r, speed):
        buf = pads.at[index]
        center = buf[z + 1, pl.ds(PAD + r, chunk)]
        behind = buf[z + 1, pl.ds(PAD - 1 + r, chunk)]
        total = buf[z, pl.ds(PAD + r, chunk)] + buf[z + 2, pl.ds(PAD + r, chunk)]
        total = total + (behind + buf[z + 1, pl.ds(PAD + 1 + r, chunk)])
        total = total + sideways(center) - 6.0 * center
        return kappa[own + z, pl.ds(r, chunk)] * total - speed * (center - behind)

    def place(buf, layer, r, value):
        rows = value.shape[0]
        buf[layer, pl.ds(PAD + r, rows)] = value
        if r == 0:
            buf[layer, pl.ds(PAD + width, 1)] = value[:1]
        if r + rows == width:
            buf[layer, pl.ds(PAD - 1, 1)] = value[rows - 1 :]

    def fill(index, z, r, value):
        place(pads.at[index], z + 1, r, value)

    def each(lo, hi, body, unroll=1):
        def turn(z, carry):
            for r in range(0, width, chunk):
                body(z, r, chunk)
            return carry

        lax.fori_loop(lo, hi, turn, 0, unroll=unroll)

    def edges(body, needs=None, gives=None):
        count = PIECES if gives is None else len(gives)
        rows = width // count
        for k in range(count):
            if needs is not None:
                arrive(needs[k : k + 1])
            body(0, k * rows, rows)
            body(depth - 1, k * rows, rows)
            if gives is not None:
                gives[k][0].start()
                gives[k][1].start()

    def interior(body):
        each(1, depth - 1, body, 2)

    def combine(coefficients, first, z, r, chunk):
        at = pl.ds(r, chunk)
        total = (first_slice * float(coefficients[0])) * fields[0, z, at] if first is None else first
        for node in range(1, NODES):
            total = total + float(coefficients[node]) * fields[node, z, at]
        return total

    def weigh(z, r, chunk):
        fill(0, z, r, combine(slice_length * WEIGHTS, None, z, r, chunk))

    def foresee(z, r, chunk):
        fill(FIRST, z, r, combine(slice_length * INTEGRALS[0], None, z, r, chunk))

    for load in loads:
        load.wait()
    edges(weigh)
    pl.semaphore_wait(barrier, met)
    for pieces in (weighted_halo, end_halo):
        for down, up in pieces:
            down.start()
            up.start()
    shift_hop.start()
    edges(foresee, None, first_halo)
    for transfer in rim_hops:
        transfer.start()
    for transfer in start_hops:
        transfer.start()
    interior(weigh)
    advect = shift[...].astype(jnp.float32) / slice_length

    def look_up(layer, r, chunk):
        at = pl.ds(r, chunk)
        labels = label[layer, at]
        total = jnp.zeros((chunk, height), jnp.float32)
        for region in range(table.shape[0]):
            total = total + jnp.where(labels == region, table[region], 0.0)
        kappa[layer, at] = total
        inflow[layer, at] = total + advect
        decay[layer, at] = 6.0 * total + advect

    def prepare(z, r, chunk):
        fill(1, z, r, fields[last, z, pl.ds(r, chunk)])
        look_up(own + z, r, chunk)

    each(0, depth, prepare)

    for index in range(EXCHANGES):

        @pl.when(jnp.logical_not(within[-1]))
        def _(index=index):
            pads[index, 0, inner] = jnp.zeros((width, height), jnp.float32)

        @pl.when(jnp.logical_not(within[1]))
        def _(index=index):
            pads[index, depth + 1, inner] = jnp.zeros((width, height), jnp.float32)

    def restrict(target, layer_of):
        def turn(zc, carry):
            for r in range(0, width, chunk):
                total = layer_of(BLOCK_Z * zc, r)
                for k in range(1, BLOCK_Z):
                    total = total + layer_of(BLOCK_Z * zc + k, r)
                fold[pl.ds(r, chunk)] = total
            total = fold[pl.ds(0, rows_c, stride=BLOCK_X)]
            for k in range(1, BLOCK_X):
                total = total + fold[pl.ds(k, rows_c, stride=BLOCK_X)]
            target[zc] = total * (1.0 / (BLOCK_Z * BLOCK_X))
            return carry

        lax.fori_loop(0, depth_c, turn, 0)

    def block_sums(index, layer_of):
        for zc in range(depth_c):
            inside = [z for z in range(BLOCK_Z * zc, BLOCK_Z * (zc + 1)) if 0 < z < depth - 1]
            for r in range(0, width, chunk):
                total = layer_of(inside[0], r)
                for z in inside[1:]:
                    total = total + layer_of(z, r)
                sums[index, zc, pl.ds(r, chunk)] = total

    def close(index, target, layer_of):
        for zc in range(depth_c):
            for r in range(0, width, chunk):
                total = sums[index, zc, pl.ds(r, chunk)]
                if zc == 0:
                    total = total + layer_of(0, r)
                if zc == depth_c - 1:
                    total = total + layer_of(depth - 1, r)
                fold[pl.ds(r, chunk)] = total
            total = fold[pl.ds(0, rows_c, stride=BLOCK_X)]
            for k in range(1, BLOCK_X):
                total = total + fold[pl.ds(k, rows_c, stride=BLOCK_X)]
            target[zc] = total * (1.0 / (BLOCK_Z * BLOCK_X))

    def gain_layer(z, r):
        at = pl.ds(r, chunk)
        return first_slice * fields[0, z, at] - fields[last, z, at] + slice_length * rate(0, z, r)

    def lift_layer(z, r):
        weight = slice_length * float(WEIGHTS[0])
        return fields[last, z, pl.ds(r, chunk)] + weight * plain_rate(1, z, r, advect_next)

    restrict(kappa_c.at[own_layers], lambda z, r: kappa[own + z, pl.ds(r, chunk)])
    edge_hops[0].start()
    edge_hops[1].start()
    block_sums(0, gain_layer)
    shift_hop.wait_recv()
    advect_next = shift_next[...].astype(jnp.float32) / slice_length
    block_sums(1, lift_layer)
    arrive(weighted_halo)
    close(0, gain.at[own_layers], gain_layer)
    edge_hops[2].start()
    edge_hops[3].start()

    def chain(wider):
        for transfer in lift_hops + edge_hops + [body_hop] + slab_hops + [front_hop]:
            transfer.wait_recv()
        for zc in range(-1, depth_c + 1) if wider else range(depth_c):
            center = delta[0, own_c + zc]
            under, over = delta[0, own_c + zc - 1], delta[0, own_c + zc + 1]
            behind = pltpu.roll(center, 1, 0)
            across = behind + pltpu.roll(center, rows_c - 1, 0)
            lateral = sideways(center)
            spreading = kappa_c[zc + 1] * (
                (under + over - 2.0 * center) * (1.0 / (BLOCK_Z * BLOCK_Z))
                + (across - 2.0 * center) * (1.0 / (BLOCK_X * BLOCK_X))
                + (lateral - 2.0 * center)
            )
            flow = (1.0 / BLOCK_X) * advect * (center - behind)
            value = center + slice_length * (spreading - flow) + (gain[zc + 1] + moved[zc + 1])
            if 0 <= zc < depth_c:
                delta[1, own_c + zc] = value
            if wider:
                front[zc + 1] = value
        for transfer in [front_hop] if wider else slab_hops + [body_hop]:
            transfer.start()

    def spread_ends():
        for transfer in rest_hops + wide_hops:
            transfer.start()

    pl.when(n == 0)(lambda: chain(False))

    arrive(end_halo)
    close(1, lift, lift_layer)
    for transfer in lift_hops:
        transfer.start()

    @pl.when(jnp.logical_not(has_prev))
    def _():
        def turn(z, carry):
            start[z] = fields[0, z]
            return carry

        lax.fori_loop(0, depth, turn, 0)
        rim[...] = jnp.zeros_like(rim)

    for end, there in enumerate((within[-1], within[1])):

        @pl.when(has_prev & jnp.logical_not(there))
        def _(end=end):
            rim[end] = jnp.zeros((width, height), jnp.float32)

    begin_weight = slice_length * float(INTEGRALS[0, 0])

    def combine_start(z, r, chunk):
        fill(2, z, r, combine(slice_length * INTEGRALS[0], begin_weight * start[z, pl.ds(r, chunk)], z, r, chunk))

    def open_layers(which):
        for k in which:
            start_hops[k].wait_recv()
            low, count = spans[k]
            for z in range(low, low + count):
                for r in range(0, width, chunk):
                    combine_start(z, r, chunk)

    rim_hops[0].wait_recv()
    rim_hops[1].wait_recv()
    arrive(first_halo)
    for end, layer in ((0, 0), (1, depth + 1)):
        for r in range(0, width, chunk):
            at = pl.ds(PAD + r, chunk)
            pads[2, layer, at] = pads[FIRST, layer, at] + begin_weight * rim[end, pl.ds(r, chunk)]
    open_layers((0, 1))

    def fine_step(sweep, step, needs):
        old = fields if sweep == 0 else mids
        new = mids if sweep == 0 else None
        offset = 0 if sweep == 0 else -1
        index = 2 + sweep * STEPS + step
        final = sweep == FINE_SWEEPS - 1
        more = not (final and step == STEPS - 1)

        def advance(z, r, chunk):
            at = pl.ds(r, chunk)
            if step == 0:
                before = start[z, at]
            else:
                before = out[step, z, at] if final else new[step - 1, z, at]
            value = before + rate(index, z, r, chunk)
            if final:
                out[step + 1, z, at] = value
            else:
                new[step, z, at] = value
            if not more:
                return
            weights = slice_length * INTEGRALS[(step + 1) % STEPS]
            if step < STEPS - 1:
                total = slice_length * float(GAPS[step + 1]) * value
                weights[step + 1] -= slice_length * GAPS[step + 1]
                source, shown, known = old, offset, {}
            else:
                total, source, shown, known = None, new, -1, {STEPS: value}
            for node in range(NODES):
                if node == 0:
                    part = start[z, at]
                else:
                    part = known[node] if node in known else source[node + shown, z, at]
                term = float(weights[node]) * part
                total = term if total is None else total + term
            fill(index + 1, z, r, total)

        following = halo(index + 1) if more else None
        edges(advance, needs, following)
        return following, lambda: interior(advance)

    def drain(count):
        for group in drains[:count]:
            for transfer in group:
                transfer.wait_send()
        del drains[:count]

    pair = None
    for stage in range(REACH - 2):
        turns = [slice_at for slice_at, slot in SLOTS.items() if slot == stage]
        for slice_at in turns:
            pl.when(n == slice_at)(lambda wider=slice_at % 2 == 0: chain(wider))
        pair, rest = fine_step(stage // STEPS, stage % STEPS, pair)
        if stage < half:
            for transfer in label_parts[stage]:
                transfer.start()
        for slice_at in turns + ([0] if stage == 0 else []):
            pl.when(n == slice_at)(spread_ends)
        if stage == 0:
            open_layers(range(2, len(start_hops)))
        rest()
        if stage == half:
            for first, second in zip(label_hops, label_forwards):
                first.wait_recv()
                second.start()
        drain(len(drains) - 1)

    for transfer in label_forwards:
        transfer.wait_recv()
    for distance in range(1, near + 1):
        for sign in (1, -1):
            low = own + sign * distance * depth
            there = within[sign * distance]

            @pl.when(there)
            def _(low=low):
                each(low, low + depth, look_up)

            @pl.when(jnp.logical_not(there))
            def _(low=low):
                def turn(z, carry):
                    kappa[z] = jnp.zeros((width, height), jnp.float32)
                    inflow[z] = jnp.zeros((width, height), jnp.float32)
                    decay[z] = jnp.zeros((width, height), jnp.float32)
                    return carry

                lax.fori_loop(low, low + depth, turn, 0)

    pl.when((n >= LATE_SLICE) & (side == 1))(lambda: chain(False))
    if slices > LATE_SLICE + 1:
        pl.when((n >= LATE_SLICE) & (side == 0))(lambda: chain(True))
    pl.when(n >= LATE_SLICE)(spread_ends)
    pair, rest = fine_step(FINE_SWEEPS - 1, STEPS - 2, pair)
    rest()

    drain(len(drains) - 1)
    for transfer in label_hops + label_forwards + lift_hops + edge_hops + rim_hops + start_hops:
        transfer.wait_send()
    for transfer in [shift_hop, front_hop, body_hop] + slab_hops + rest_hops + wide_hops:
        transfer.wait_send()
    for transfer in wide_hops + rest_hops:
        transfer.wait_recv()

    def mix(early, late, begin, finish):
        return (slice_length * float(early)) * begin + (slice_length * float(late)) * finish

    def widen(c, carry):
        for field in range(2):
            for k in range(BLOCK_X):
                spread[field, c, pl.ds(k, rows_c, stride=BLOCK_X)] = delta[field, c]
        for r in range(0, width, chunk):
            at = pl.ds(r, chunk)
            begin, finish = spread[0, c, at], spread[1, c, at]
            place(base, c + 1, r, mix(EARLY[0], LATE[0], begin, finish))
            for row in range(1, STEPS):
                gap, weight = float(GAPS[row]), float(TIMES[row])
                plan[row - 1, c, at] = mix(
                    EARLY[row] - gap * (1.0 - weight), LATE[row] - gap * weight, begin, finish
                )
        return carry

    lax.fori_loop(0, layers_c, widen, 0)
    base[0, inner] = jnp.zeros((width, height), jnp.float32)
    base[layers_c + 1, inner] = jnp.zeros((width, height), jnp.float32)

    def open_step(c, carry):
        for r in range(0, width, chunk):
            at, inside = pl.ds(r, chunk), pl.ds(PAD + r, chunk)
            center = base[c + 1, inside]
            behind = base[c + 1, pl.ds(PAD - 1 + r, chunk)]
            level = base[c + 1, pl.ds(PAD + 1 + r, chunk)] + sideways(center)
            initial, following = spread[0, c, at], plan[0, c, at]
            for k in range(BLOCK_Z):
                layer = BLOCK_Z * c + k
                under = base[c, inside] if k == 0 else center
                over = base[c + 2, inside] if k == BLOCK_Z - 1 else center
                total = level + (under + over)
                value = initial + (kappa[layer, at] * total + inflow[layer, at] * behind - decay[layer, at] * center)
                nodes[0, layer, at] = value
                place(grid.at[0], layer, r, float(GAPS[1]) * slice_length * value + following)
        return carry

    def wide_each(margin, body, apart):
        if not apart:

            def through(i, carry):
                for r in range(0, width, chunk):
                    body(own - margin + i, None, r)
                return carry

            lax.fori_loop(0, depth + 2 * margin, through, 0, unroll=4)
            return

        def outer(i, carry):
            layer = own - margin + i + jnp.where(i >= margin, depth, 0)
            for r in range(0, width, chunk):
                body(layer, None, r)
            return carry

        def middle(z, carry):
            for r in range(0, width, chunk):
                body(own + z, z, r)
            return carry

        if margin > 0:
            lax.fori_loop(0, 2 * margin, outer, 0, unroll=min(4, 2 * margin))
        lax.fori_loop(0, depth, middle, 0, unroll=4)

    def wide_step(stage):
        sweep, step = stage // STEPS, stage % STEPS
        source, target = grid.at[(stage - 1) % 2], grid.at[stage % 2]
        margin = REACH - 1 - stage
        final = sweep == FINE_SWEEPS - 1
        more = stage < REACH - 1

        def advance(layer, z, r):
            at, c = pl.ds(r, chunk), layer // BLOCK_Z
            if step == 0 or final:
                initial = spread[0, c, at]
            if step == 0:
                before = initial
            else:
                before = latest[layer, at] if final else nodes[step - 1, layer, at]
            value = before + slope(source, layer, layer, r, chunk)
            if final:
                if more:
                    latest[layer, at] = value
                if z is not None:
                    out[step + 1, z, at] = out[step + 1, z, at] + value
                    if step == 0:
                        out[0, z, at] = start[z, at] + initial
            else:
                nodes[step, layer, at] = value
            if not more:
                return
            if not final and step < STEPS - 1:
                total = slice_length * float(GAPS[step + 1]) * value + plan[step, c, at]
            else:
                weights = slice_length * INTEGRALS[(step + 1) % STEPS]
                known = {}
                if final:
                    total = slice_length * float(GAPS[step + 1]) * value + float(weights[0]) * initial
                    weights[step + 1] -= slice_length * GAPS[step + 1]
                else:
                    total = float(weights[0]) * spread[0, c, at]
                    known = {STEPS: value}
                for node in range(1, NODES):
                    part = known[node] if node in known else nodes[node - 1, layer, at]
                    total = total + float(weights[node]) * part
            place(target, layer, r, total)

        wide_each(margin, advance, final)

    lax.fori_loop(0, layers_c, open_step, 0)
    for stage in range(1, STEPS):
        wide_step(stage)
    pair, rest = fine_step(FINE_SWEEPS - 1, STEPS - 1, pair)
    rest()
    drain(len(drains))
    for stage in range(STEPS, REACH):
        wide_step(stage)


def shards(node_fields, region_label, sheet_shift, diffusivity):
    fields = node_fields[0]
    nodes, depth, width, height = fields.shape
    depth_c, rows_c = depth // BLOCK_Z, width // BLOCK_X
    near = -(-REACH // depth)
    layers, layers_c = (2 * near + 1) * depth, (2 * near + 1) * depth_c
    f32 = jnp.float32
    fine, wide = (depth, width, height), (layers, width, height)
    coarse = (depth_c, rows_c, height)
    ringed = (depth_c + 2, rows_c, height)
    padded = width + 2 * PAD
    vmem, hbm = (pl.BlockSpec(memory_space=space) for space in (pltpu.VMEM, pltpu.HBM))
    result = pl.pallas_call(
        kernel,
        out_shape=jax.ShapeDtypeStruct(fields.shape, f32),
        in_specs=[hbm] * 4,
        out_specs=vmem,
        scratch_shapes=[
            pltpu.VMEM(fields.shape, f32),
            pltpu.VMEM(wide, jnp.int32),
            pltpu.VMEM(sheet_shift.shape, jnp.int32),
            pltpu.SMEM(diffusivity.shape, f32),
            pltpu.VMEM(wide, f32),
            pltpu.VMEM(wide, f32),
            pltpu.VMEM(wide, f32),
            pltpu.VMEM(ringed, f32),
            pltpu.VMEM(fine, f32),
            pltpu.VMEM((2, width, height), f32),
            pltpu.VMEM(ringed, f32),
            pltpu.VMEM(sheet_shift.shape, jnp.int32),
            pltpu.VMEM((EXCHANGES, depth + 2, padded, height), f32),
            pltpu.VMEM((STEPS,) + fine, f32),
            pltpu.VMEM(ringed, f32),
            pltpu.VMEM(coarse, f32),
            pltpu.VMEM((2, layers_c, rows_c, height), f32),
            pltpu.VMEM(ringed, f32),
            pltpu.VMEM((2, depth_c, width, height), f32),
            pltpu.VMEM((width, height), f32),
            pltpu.VMEM((2, layers_c, width, height), f32),
            pltpu.VMEM((STEPS - 1, layers_c, width, height), f32),
            pltpu.VMEM((layers_c + 2, padded, height), f32),
            pltpu.VMEM((2, layers, padded, height), f32),
            pltpu.VMEM((STEPS,) + wide, f32),
            pltpu.VMEM(wide, f32),
            pltpu.SemaphoreType.DMA((2 * len(OPENING) + 4,)),
            pltpu.SemaphoreType.DMA((2 * len(OPENING) + 4 * PIECES,)),
            pltpu.SemaphoreType.DMA((8 + 4 * near,)),
            pltpu.SemaphoreType.DMA((8 + 4 * near,)),
            pltpu.SemaphoreType.DMA((3,)),
            pltpu.SemaphoreType.DMA((3,)),
            pltpu.SemaphoreType.DMA((2 * near,)),
            pltpu.SemaphoreType.DMA((2 * near,)),
            pltpu.SemaphoreType.DMA((4,)),
            pltpu.SemaphoreType.DMA((4,)),
            pltpu.SemaphoreType.DMA((4 * near,)),
            pltpu.SemaphoreType.DMA((4 * near,)),
            pltpu.SemaphoreType.DMA((4,)),
        ],
        compiler_params=pltpu.CompilerParams(
            collective_id=0, has_side_effects=True, vmem_limit_bytes=48 * 1024 * 1024,
        ),
    )(*(pltpu.with_memory_space_constraint(x, pltpu.HBM) for x in (fields, region_label, sheet_shift, diffusivity)))
    return result[None]


def solution(mesh):
    in_specs = (P("tm", None, "space", None, None), P("space", None, None), P("tm", None), P())
    out_specs = P("tm", None, "space", None, None)
    return jax.shard_map(shards, mesh=mesh, in_specs=in_specs, out_specs=out_specs, check_vma=False)
```

```python
import math

import jax
import jax.numpy as jnp
import numpy as np
from jax import lax
from jax.experimental import pallas as pl
from jax.experimental.pallas import tpu as pltpu
from jax.sharding import PartitionSpec as P

NODES = 5
FINE_SWEEPS = 2
BLOCK_Z = 4
BLOCK_X = 2
PAD = 8
PIECES = 4
MESH = pl.DeviceIdType.MESH

slice_length = 1.0


def node_tables():
    radius = math.sqrt(3.0 / 7.0)
    points = [0.0, (1.0 - radius) / 2.0, 0.5, (1.0 + radius) / 2.0, 1.0]
    integrals = np.zeros((4, 5))
    for column in range(5):
        coeffs = [1.0]
        divisor = 1.0
        for other in range(5):
            if other != column:
                anchor = points[other]
                product = [0.0] * (len(coeffs) + 1)
                for degree in range(len(coeffs)):
                    product[degree + 1] = product[degree + 1] + coeffs[degree]
                    product[degree] = product[degree] - anchor * coeffs[degree]
                coeffs = product
                divisor = divisor * (points[column] - anchor)
        for row in range(4):
            bottom = points[row]
            summit = points[row + 1]
            amount = 0.0
            for degree in range(len(coeffs)):
                amount = amount + coeffs[degree] / (degree + 1) * (
                    summit ** (degree + 1) - bottom ** (degree + 1)
                )
            integrals[row, column] = amount / divisor
    return (np.array(points), integrals)


TIMES, INTEGRALS = node_tables()
WEIGHTS = INTEGRALS.sum(axis=0)
STEPS = NODES - 1
REACH = FINE_SWEEPS * STEPS
EXCHANGES = 3 + REACH
FIRST = EXCHANGES - 1
OPENING = {0: 0, 1: 1, FIRST: 2}
GAPS = TIMES[1:] - TIMES[:-1]
LATE = (INTEGRALS * TIMES).sum(axis=1)
EARLY = INTEGRALS.sum(axis=1) - LATE
SLOTS = {1: 1, 2: 3, 3: 4, 4: 7, 5: 9, 6: 11}
LATE_SLICE = 7


class Transfer:
    def __init__(self, src, dst, send_sem, recv_sem, device, sends, receives):
        self.copy = pltpu.make_async_remote_copy(
            src_ref=src,
            dst_ref=dst,
            send_sem=send_sem,
            recv_sem=recv_sem,
            device_id=device,
            device_id_type=MESH,
        )
        self.sends, self.receives = sends, receives

    def start(self):
        pl.when(self.sends)(self.copy.start)

    def wait_recv(self):
        pl.when(self.receives)(self.copy.wait_recv)

    def wait_send(self):
        pl.when(self.sends)(self.copy.wait_send)


def kernel(
    fields_in, label_in, shift_in, table_in, out, fields, label, shift, table,
    kappa, inflow, decay, kappa_c, start, rim, moved, shift_next, pads, mids, gain, lift, delta, front, sums, fold,
    spread, plan, base, grid, nodes, latest,
    halo_send, halo_recv, time_send, time_recv, start_send, start_recv, wide_send, wide_recv, edge_send, edge_recv,
    label_send, label_recv, load_sem,
):
    n, s = lax.axis_index("tm"), lax.axis_index("space")
    slices, slabs = lax.axis_size("tm"), lax.axis_size("space")
    depth, width, height = fields.shape[1:]
    rows_c = width // BLOCK_X
    depth_c = depth // BLOCK_Z
    near = -(-REACH // depth)
    own, own_c = near * depth, near * depth_c
    layers, layers_c = (2 * near + 1) * depth, (2 * near + 1) * depth_c
    chunk = min(64, width)
    piece = width // PIECES
    last = NODES - 1
    has_prev, has_next = n > 0, n < slices - 1
    inner = pl.ds(PAD, width)
    here_c = pl.ds(own_c, depth_c)

    loads = [
        pltpu.make_async_copy(fields_in, fields, load_sem.at[0]),
        pltpu.make_async_copy(label_in, label.at[pl.ds(own, depth)], load_sem.at[1]),
        pltpu.make_async_copy(shift_in, shift, load_sem.at[2]),
        pltpu.make_async_copy(table_in, table, load_sem.at[3]),
    ]
    for load in loads:
        load.start()

    within = {
        distance: (s + distance >= 0) & (s + distance < slabs)
        for distance in range(-near, near + 1)
    }
    for distance in range(1, near + 1):
        for sign in (1, -1):

            @pl.when(jnp.logical_not(within[sign * distance]))
            def _(distance=distance, sign=sign):
                there = own_c + sign * distance * depth_c
                delta[:, pl.ds(there, depth_c)] = jnp.zeros((2, depth_c, rows_c, height), jnp.float32)
                if distance == 1:
                    edge = depth_c + 1 if sign == 1 else 0
                    for ref in (gain, moved, kappa_c):
                        ref[edge] = jnp.zeros((rows_c, height), jnp.float32)

    @pl.when(jnp.logical_not(has_prev))
    def _():
        moved[...] = jnp.zeros_like(moved)
        delta[0] = jnp.zeros((layers_c, rows_c, height), jnp.float32)

    barrier = pltpu.get_barrier_semaphore()
    met = jnp.int32(0)
    for dn in (-1, 0, 1):
        for ds in range(-near, near + 1):
            if dn == 0 and ds == 0:
                continue
            there = (n + dn >= 0) & (n + dn < slices) & within[ds]

            @pl.when(there)
            def _(dn=dn, ds=ds):
                pl.semaphore_signal(
                    barrier, inc=1, device_id={"tm": n + dn, "space": s + ds}, device_id_type=MESH
                )

            met = met + there.astype(jnp.int32)

    drains = []

    def halo(index, source=None):
        buf = pads.at[index]
        if index in OPENING:
            count, gone, come = 1, 2 * OPENING[index], 2 * OPENING[index]
        else:
            count = PIECES
            gone = 2 * (len(OPENING) + index % 2)
            come = 2 * (len(OPENING) + (index % 2) * PIECES)
        share = width // count

        def pair(start, rows, sem):
            here = pl.ds(PAD + start, rows)
            if source is None:
                low, high = buf.at[1, here], buf.at[depth, here]
            else:
                low, high = (source.at[z, pl.ds(start, rows)] for z in (0, depth - 1))
            up = Transfer(
                high, buf.at[0, here], halo_send.at[gone], halo_recv.at[sem + 1],
                {"space": s + 1}, within[1], within[-1],
            )
            down = Transfer(
                low, buf.at[depth + 1, here], halo_send.at[gone + 1], halo_recv.at[sem],
                {"space": s - 1}, within[-1], within[1],
            )
            return down, up

        drains.append(list(pair(0, width, come)))
        return [pair(k * share, share, come + 2 * k) for k in range(count)]

    def arrive(pieces):
        for down, up in pieces:
            down.wait_recv()
            up.wait_recv()

    side = lax.rem(n, 2)
    beyond = (side == 0) & has_prev
    always = n >= 0

    def time_hop(index, src, dst, ds=0, sends=always, receives=always):
        goes = has_next & sends if ds == 0 else has_next & sends & within[ds]
        comes = has_prev & receives if ds == 0 else has_prev & receives & within[-ds]
        to = {"tm": n + 1} if ds == 0 else {"tm": n + 1, "space": s + ds}
        return Transfer(src, dst, time_send.at[index], time_recv.at[index], to, goes, comes)

    shift_hop = Transfer(
        shift_in, shift_next, time_send.at[0], time_recv.at[0], {"tm": n - 1}, has_prev, has_next
    )
    weighted_halo = halo(0)
    end_halo = halo(1, fields_in.at[last])
    first_halo = halo(FIRST)
    rim_hops = [
        time_hop(6, fields_in.at[last, depth - 1], rim.at[0], 1),
        time_hop(7, fields_in.at[last, 0], rim.at[1], -1),
    ]
    rim_depth = min(2, depth // 2)
    spans = [(0, rim_depth), (depth - rim_depth, rim_depth), (rim_depth, depth - 2 * rim_depth)]
    start_hops = [
        Transfer(
            fields_in.at[last, pl.ds(low, count)], start.at[pl.ds(low, count)],
            start_send.at[k], start_recv.at[k], {"tm": n + 1}, has_next, has_prev,
        )
        for k, (low, count) in enumerate(spans)
        if count
    ]
    half = depth // 2
    label_parts = [[] for _ in range(half)]
    label_hops, label_forwards = [], []
    for distance in range(1, near + 1):
        for sign in (1, -1):
            sem = 2 * (distance - 1) + (sign + 1) // 2
            to, sends, receives = {"space": s + sign * distance}, within[sign * distance], within[-sign * distance]
            low = side * half
            there = own - sign * distance * depth + low
            sems = label_send.at[sem], label_recv.at[sem]
            for i in range(half):
                label_parts[i].append(
                    Transfer(label_in.at[low + i], label.at[there + i], *sems, to, sends, receives)
                )
            there = pl.ds(there, half)
            label_hops.append(
                Transfer(label_in.at[pl.ds(low, half)], label.at[there], *sems, to, sends, receives)
            )
            label_forwards.append(
                Transfer(
                    label.at[there], label.at[there],
                    label_send.at[2 * near + sem], label_recv.at[2 * near + sem],
                    {"tm": n + 1 - 2 * side}, receives, receives,
                )
            )

    own_layers = pl.ds(1, depth_c)
    whole = jnp.logical_not(beyond)
    from_beyond = (side == 1) & (n > 1)
    from_whole = jnp.logical_not(from_beyond)
    lift_hops = [
        time_hop(2, lift, moved.at[own_layers]),
        time_hop(4, lift.at[depth_c - 1], moved.at[0], 1, side == 1, beyond),
        time_hop(5, lift.at[0], moved.at[depth_c + 1], -1, side == 1, beyond),
    ]
    edge_hops = []
    for k, ref in enumerate((kappa_c, gain)):
        edge_hops.append(
            Transfer(
                ref.at[depth_c], ref.at[0], edge_send.at[2 * k], edge_recv.at[2 * k],
                {"space": s + 1}, beyond & within[1], beyond & within[-1],
            )
        )
        edge_hops.append(
            Transfer(
                ref.at[1], ref.at[depth_c + 1], edge_send.at[2 * k + 1], edge_recv.at[2 * k + 1],
                {"space": s - 1}, beyond & within[-1], beyond & within[1],
            )
        )
    front_hop = time_hop(
        1, front, delta.at[0, pl.ds(own_c - 1, depth_c + 2)], 0, beyond, from_beyond
    )
    body_hop = time_hop(3, delta.at[1, here_c], delta.at[0, here_c], 0, whole, from_whole)
    wide_hops, rest_hops, slab_hops = [], [], []
    for distance in range(1, near + 1):
        for sign in (1, -1):
            sem = 2 * (distance - 1) + (sign + 1) // 2
            there = own_c - sign * distance * depth_c
            wide_hops.append(
                Transfer(
                    delta.at[1, here_c], delta.at[1, pl.ds(there, depth_c)],
                    wide_send.at[sem], wide_recv.at[sem],
                    {"space": s + sign * distance}, within[sign * distance], within[-sign * distance],
                )
            )
            slab_hops.append(
                time_hop(
                    8 + 2 * near + sem, delta.at[1, here_c], delta.at[0, pl.ds(there, depth_c)],
                    sign * distance, whole, from_whole,
                )
            )
            skip = 1 if distance == 1 else 0
            if depth_c > skip:
                shown = skip if sign == -1 else 0
                rest_hops.append(
                    time_hop(
                        8 + sem,
                        delta.at[1, pl.ds(own_c + shown, depth_c - skip)],
                        delta.at[0, pl.ds(there + shown, depth_c - skip)],
                        sign * distance, beyond, from_beyond,
                    )
                )

    first_slice = (n == 0).astype(jnp.float32)

    def sideways(center):
        lane = lax.broadcasted_iota(jnp.int32, center.shape, 1)
        return jnp.where(lane == height - 1, 0.0, pltpu.roll(center, height - 1, 1)) + jnp.where(
            lane == 0, 0.0, pltpu.roll(center, 1, 1)
        )

    def slope(buf, layer, own_layer, r, rows):
        center = buf[layer, pl.ds(PAD + r, rows)]
        behind = buf[layer, pl.ds(PAD - 1 + r, rows)]
        total = buf[layer - 1, pl.ds(PAD + r, rows)] + buf[layer + 1, pl.ds(PAD + r, rows)]
        total = total + buf[layer, pl.ds(PAD + 1 + r, rows)]
        total = total + sideways(center)
        at = pl.ds(r, rows)
        return kappa[own_layer, at] * total + inflow[own_layer, at] * behind - decay[own_layer, at] * center

    def rate(index, z, r, chunk=chunk):
        return slope(pads.at[index], z + 1, own + z, r, chunk)

    def plain_rate(index, z, r, speed):
        buf = pads.at[index]
        center = buf[z + 1, pl.ds(PAD + r, chunk)]
        behind = buf[z + 1, pl.ds(PAD - 1 + r, chunk)]
        total = buf[z, pl.ds(PAD + r, chunk)] + buf[z + 2, pl.ds(PAD + r, chunk)]
        total = total + (behind + buf[z + 1, pl.ds(PAD + 1 + r, chunk)])
        total = total + sideways(center) - 6.0 * center
        return kappa[own + z, pl.ds(r, chunk)] * total - speed * (center - behind)

    def place(buf, layer, r, value):
        rows = value.shape[0]
        buf[layer, pl.ds(PAD + r, rows)] = value
        if r == 0:
            buf[layer, pl.ds(PAD + width, 1)] = value[:1]
        if r + rows == width:
            buf[layer, pl.ds(PAD - 1, 1)] = value[rows - 1 :]

    def fill(index, z, r, value):
        place(pads.at[index], z + 1, r, value)

    def each(lo, hi, body, unroll=1):
        def turn(z, carry):
            for r in range(0, width, chunk):
                body(z, r, chunk)
            return carry

        lax.fori_loop(lo, hi, turn, 0, unroll=unroll)

    def edges(body, needs=None, gives=None):
        count = PIECES if gives is None else len(gives)
        rows = width // count
        for k in range(count):
            if needs is not None:
                arrive(needs[k : k + 1])
            body(0, k * rows, rows)
            body(depth - 1, k * rows, rows)
            if gives is not None:
                gives[k][0].start()
                gives[k][1].start()

    def interior(body):
        each(1, depth - 1, body, 2)

    def combine(coefficients, first, z, r, chunk):
        at = pl.ds(r, chunk)
        total = (first_slice * float(coefficients[0])) * fields[0, z, at] if first is None else first
        for node in range(1, NODES):
            total = total + float(coefficients[node]) * fields[node, z, at]
        return total

    def weigh(z, r, chunk):
        fill(0, z, r, combine(slice_length * WEIGHTS, None, z, r, chunk))

    def foresee(z, r, chunk):
        fill(FIRST, z, r, combine(slice_length * INTEGRALS[0], None, z, r, chunk))

    for load in loads:
        load.wait()
    edges(weigh)
    pl.semaphore_wait(barrier, met)
    for pieces in (weighted_halo, end_halo):
        for down, up in pieces:
            down.start()
            up.start()
    shift_hop.start()
    edges(foresee, None, first_halo)
    for transfer in rim_hops:
        transfer.start()
    for transfer in start_hops:
        transfer.start()
    interior(weigh)
    advect = shift[...].astype(jnp.float32) / slice_length

    def look_up(layer, r, chunk):
        at = pl.ds(r, chunk)
        labels = label[layer, at]
        total = jnp.zeros((chunk, height), jnp.float32)
        for region in range(table.shape[0]):
            total = total + jnp.where(labels == region, table[region], 0.0)
        kappa[layer, at] = total
        inflow[layer, at] = total + advect
        decay[layer, at] = 6.0 * total + advect

    def prepare(z, r, chunk):
        fill(1, z, r, fields[last, z, pl.ds(r, chunk)])
        look_up(own + z, r, chunk)

    each(0, depth, prepare)

    for index in range(EXCHANGES):

        @pl.when(jnp.logical_not(within[-1]))
        def _(index=index):
            pads[index, 0, inner] = jnp.zeros((width, height), jnp.float32)

        @pl.when(jnp.logical_not(within[1]))
        def _(index=index):
            pads[index, depth + 1, inner] = jnp.zeros((width, height), jnp.float32)

    def restrict(target, layer_of):
        def turn(zc, carry):
            for r in range(0, width, chunk):
                total = layer_of(BLOCK_Z * zc, r)
                for k in range(1, BLOCK_Z):
                    total = total + layer_of(BLOCK_Z * zc + k, r)
                fold[pl.ds(r, chunk)] = total
            total = fold[pl.ds(0, rows_c, stride=BLOCK_X)]
            for k in range(1, BLOCK_X):
                total = total + fold[pl.ds(k, rows_c, stride=BLOCK_X)]
            target[zc] = total * (1.0 / (BLOCK_Z * BLOCK_X))
            return carry

        lax.fori_loop(0, depth_c, turn, 0)

    def block_sums(index, layer_of):
        for zc in range(depth_c):
            inside = [z for z in range(BLOCK_Z * zc, BLOCK_Z * (zc + 1)) if 0 < z < depth - 1]
            for r in range(0, width, chunk):
                total = layer_of(inside[0], r)
                for z in inside[1:]:
                    total = total + layer_of(z, r)
                sums[index, zc, pl.ds(r, chunk)] = total

    def close(index, target, layer_of):
        for zc in range(depth_c):
            for r in range(0, width, chunk):
                total = sums[index, zc, pl.ds(r, chunk)]
                if zc == 0:
                    total = total + layer_of(0, r)
                if zc == depth_c - 1:
                    total = total + layer_of(depth - 1, r)
                fold[pl.ds(r, chunk)] = total
            total = fold[pl.ds(0, rows_c, stride=BLOCK_X)]
            for k in range(1, BLOCK_X):
                total = total + fold[pl.ds(k, rows_c, stride=BLOCK_X)]
            target[zc] = total * (1.0 / (BLOCK_Z * BLOCK_X))

    def gain_layer(z, r):
        at = pl.ds(r, chunk)
        return first_slice * fields[0, z, at] - fields[last, z, at] + slice_length * rate(0, z, r)

    def lift_layer(z, r):
        weight = slice_length * float(WEIGHTS[0])
        return fields[last, z, pl.ds(r, chunk)] + weight * plain_rate(1, z, r, advect_next)

    restrict(kappa_c.at[own_layers], lambda z, r: kappa[own + z, pl.ds(r, chunk)])
    edge_hops[0].start()
    edge_hops[1].start()
    block_sums(0, gain_layer)
    shift_hop.wait_recv()
    advect_next = shift_next[...].astype(jnp.float32) / slice_length
    block_sums(1, lift_layer)
    arrive(weighted_halo)
    close(0, gain.at[own_layers], gain_layer)
    edge_hops[2].start()
    edge_hops[3].start()

    def chain(wider):
        for transfer in lift_hops + edge_hops + [body_hop] + slab_hops + [front_hop]:
            transfer.wait_recv()
        for zc in range(-1, depth_c + 1) if wider else range(depth_c):
            center = delta[0, own_c + zc]
            under, over = delta[0, own_c + zc - 1], delta[0, own_c + zc + 1]
            behind = pltpu.roll(center, 1, 0)
            across = behind + pltpu.roll(center, rows_c - 1, 0)
            lateral = sideways(center)
            spreading = kappa_c[zc + 1] * (
                (under + over - 2.0 * center) * (1.0 / (BLOCK_Z * BLOCK_Z))
                + (across - 2.0 * center) * (1.0 / (BLOCK_X * BLOCK_X))
                + (lateral - 2.0 * center)
            )
            flow = (1.0 / BLOCK_X) * advect * (center - behind)
            value = center + slice_length * (spreading - flow) + (gain[zc + 1] + moved[zc + 1])
            if 0 <= zc < depth_c:
                delta[1, own_c + zc] = value
            if wider:
                front[zc + 1] = value
        for transfer in [front_hop] if wider else slab_hops + [body_hop]:
            transfer.start()

    def spread_ends():
        for transfer in rest_hops + wide_hops:
            transfer.start()

    pl.when(n == 0)(lambda: chain(False))

    arrive(end_halo)
    close(1, lift, lift_layer)
    for transfer in lift_hops:
        transfer.start()

    @pl.when(jnp.logical_not(has_prev))
    def _():
        def turn(z, carry):
            start[z] = fields[0, z]
            return carry

        lax.fori_loop(0, depth, turn, 0)
        rim[...] = jnp.zeros_like(rim)

    for end, there in enumerate((within[-1], within[1])):

        @pl.when(has_prev & jnp.logical_not(there))
        def _(end=end):
            rim[end] = jnp.zeros((width, height), jnp.float32)

    begin_weight = slice_length * float(INTEGRALS[0, 0])

    def combine_start(z, r, chunk):
        fill(2, z, r, combine(slice_length * INTEGRALS[0], begin_weight * start[z, pl.ds(r, chunk)], z, r, chunk))

    def open_layers(which):
        for k in which:
            start_hops[k].wait_recv()
            low, count = spans[k]
            for z in range(low, low + count):
                for r in range(0, width, chunk):
                    combine_start(z, r, chunk)

    rim_hops[0].wait_recv()
    rim_hops[1].wait_recv()
    arrive(first_halo)
    for end, layer in ((0, 0), (1, depth + 1)):
        for r in range(0, width, chunk):
            at = pl.ds(PAD + r, chunk)
            pads[2, layer, at] = pads[FIRST, layer, at] + begin_weight * rim[end, pl.ds(r, chunk)]
    open_layers((0, 1))

    def fine_step(sweep, step, needs):
        old = fields if sweep == 0 else mids
        new = mids if sweep == 0 else None
        offset = 0 if sweep == 0 else -1
        index = 2 + sweep * STEPS + step
        final = sweep == FINE_SWEEPS - 1
        more = not (final and step == STEPS - 1)

        def advance(z, r, chunk):
            at = pl.ds(r, chunk)
            if step == 0:
                before = start[z, at]
            else:
                before = out[step, z, at] if final else new[step - 1, z, at]
            value = before + rate(index, z, r, chunk)
            if final:
                out[step + 1, z, at] = value
            else:
                new[step, z, at] = value
            if not more:
                return
            weights = slice_length * INTEGRALS[(step + 1) % STEPS]
            if step < STEPS - 1:
                total = slice_length * float(GAPS[step + 1]) * value
                weights[step + 1] -= slice_length * GAPS[step + 1]
                source, shown, known = old, offset, {}
            else:
                total, source, shown, known = None, new, -1, {STEPS: value}
            for node in range(NODES):
                if node == 0:
                    part = start[z, at]
                else:
                    part = known[node] if node in known else source[node + shown, z, at]
                term = float(weights[node]) * part
                total = term if total is None else total + term
            fill(index + 1, z, r, total)

        if not more:
            return None, lambda: (arrive(needs), each(0, depth, advance, 4))
        following = halo(index + 1)
        edges(advance, needs, following)
        return following, lambda: interior(advance)

    def drain(count):
        for group in drains[:count]:
            for transfer in group:
                transfer.wait_send()
        del drains[:count]

    pair = None
    for stage in range(REACH - 2):
        early = [slice_at for slice_at, slot in SLOTS.items() if slot == 2 * stage]
        late = [slice_at for slice_at, slot in SLOTS.items() if slot == 2 * stage + 1]
        for slice_at in early:
            pl.when(n == slice_at)(lambda wider=slice_at % 2 == 0: chain(wider))
        pair, rest = fine_step(stage // STEPS, stage % STEPS, pair)
        for slice_at in late:
            pl.when(n == slice_at)(lambda wider=slice_at % 2 == 0: chain(wider))
        if stage < half:
            for transfer in label_parts[stage]:
                transfer.start()
        for slice_at in early + late + ([0] if stage == 0 else []):
            pl.when(n == slice_at)(spread_ends)
        if stage == 0:
            open_layers(range(2, len(start_hops)))
        rest()
        if stage == half:
            for first, second in zip(label_hops, label_forwards):
                first.wait_recv()
                second.start()
        drain(len(drains) - 1)

    for transfer in label_forwards:
        transfer.wait_recv()
    for distance in range(1, near + 1):
        for sign in (1, -1):
            low = own + sign * distance * depth
            there = within[sign * distance]

            @pl.when(there)
            def _(low=low):
                each(low, low + depth, look_up)

            @pl.when(jnp.logical_not(there))
            def _(low=low):
                def turn(z, carry):
                    kappa[z] = jnp.zeros((width, height), jnp.float32)
                    inflow[z] = jnp.zeros((width, height), jnp.float32)
                    decay[z] = jnp.zeros((width, height), jnp.float32)
                    return carry

                lax.fori_loop(low, low + depth, turn, 0)

    pair, rest = fine_step(FINE_SWEEPS - 1, STEPS - 2, pair)
    pl.when((n >= LATE_SLICE) & (side == 1))(lambda: chain(False))
    if slices > LATE_SLICE + 1:
        pl.when((n >= LATE_SLICE) & (side == 0))(lambda: chain(True))
    pl.when(n >= LATE_SLICE)(spread_ends)
    rest()

    drain(len(drains) - 1)
    for transfer in label_hops + label_forwards + lift_hops + edge_hops + rim_hops + start_hops:
        transfer.wait_send()
    for transfer in [shift_hop, front_hop, body_hop] + slab_hops + rest_hops + wide_hops:
        transfer.wait_send()
    for transfer in wide_hops + rest_hops:
        transfer.wait_recv()

    def mix(early, late, begin, finish):
        return (slice_length * float(early)) * begin + (slice_length * float(late)) * finish

    def widen(c, carry):
        for field in range(2):
            for k in range(BLOCK_X):
                spread[field, c, pl.ds(k, rows_c, stride=BLOCK_X)] = delta[field, c]
        for r in range(0, width, chunk):
            at = pl.ds(r, chunk)
            begin, finish = spread[0, c, at], spread[1, c, at]
            place(base, c + 1, r, mix(EARLY[0], LATE[0], begin, finish))
            for row in range(1, STEPS):
                gap, weight = float(GAPS[row]), float(TIMES[row])
                plan[row - 1, c, at] = mix(
                    EARLY[row] - gap * (1.0 - weight), LATE[row] - gap * weight, begin, finish
                )
        return carry

    lax.fori_loop(0, layers_c, widen, 0)
    base[0, inner] = jnp.zeros((width, height), jnp.float32)
    base[layers_c + 1, inner] = jnp.zeros((width, height), jnp.float32)

    def open_step(c, carry):
        for r in range(0, width, chunk):
            at, inside = pl.ds(r, chunk), pl.ds(PAD + r, chunk)
            center = base[c + 1, inside]
            behind = base[c + 1, pl.ds(PAD - 1 + r, chunk)]
            level = base[c + 1, pl.ds(PAD + 1 + r, chunk)] + sideways(center)
            initial, following = spread[0, c, at], plan[0, c, at]
            for k in range(BLOCK_Z):
                layer = BLOCK_Z * c + k
                under = base[c, inside] if k == 0 else center
                over = base[c + 2, inside] if k == BLOCK_Z - 1 else center
                total = level + (under + over)
                value = initial + (kappa[layer, at] * total + inflow[layer, at] * behind - decay[layer, at] * center)
                nodes[0, layer, at] = value
                place(grid.at[0], layer, r, float(GAPS[1]) * slice_length * value + following)
        return carry

    def wide_each(margin, body, apart):
        if not apart:

            def through(i, carry):
                for r in range(0, width, chunk):
                    body(own - margin + i, None, r)
                return carry

            lax.fori_loop(0, depth + 2 * margin, through, 0, unroll=4)
            return

        def outer(i, carry):
            layer = own - margin + i + jnp.where(i >= margin, depth, 0)
            for r in range(0, width, chunk):
                body(layer, None, r)
            return carry

        def middle(z, carry):
            for r in range(0, width, chunk):
                body(own + z, z, r)
            return carry

        if margin > 0:
            lax.fori_loop(0, 2 * margin, outer, 0, unroll=min(4, 2 * margin))
        lax.fori_loop(0, depth, middle, 0, unroll=4)

    def wide_step(stage):
        sweep, step = stage // STEPS, stage % STEPS
        source, target = grid.at[(stage - 1) % 2], grid.at[stage % 2]
        margin = REACH - 1 - stage
        final = sweep == FINE_SWEEPS - 1
        more = stage < REACH - 1

        def advance(layer, z, r):
            at, c = pl.ds(r, chunk), layer // BLOCK_Z
            if step == 0 or final:
                initial = spread[0, c, at]
            if step == 0:
                before = initial
            else:
                before = latest[layer, at] if final else nodes[step - 1, layer, at]
            value = before + slope(source, layer, layer, r, chunk)
            if final:
                if more:
                    latest[layer, at] = value
                if z is not None:
                    out[step + 1, z, at] = out[step + 1, z, at] + value
                    if step == 0:
                        out[0, z, at] = start[z, at] + initial
            else:
                nodes[step, layer, at] = value
            if not more:
                return
            if not final and step < STEPS - 1:
                total = slice_length * float(GAPS[step + 1]) * value + plan[step, c, at]
            else:
                weights = slice_length * INTEGRALS[(step + 1) % STEPS]
                known = {}
                if final:
                    total = slice_length * float(GAPS[step + 1]) * value + float(weights[0]) * initial
                    weights[step + 1] -= slice_length * GAPS[step + 1]
                else:
                    total = float(weights[0]) * spread[0, c, at]
                    known = {STEPS: value}
                for node in range(1, NODES):
                    part = known[node] if node in known else nodes[node - 1, layer, at]
                    total = total + float(weights[node]) * part
            place(target, layer, r, total)

        wide_each(margin, advance, final)

    lax.fori_loop(0, layers_c, open_step, 0)
    for stage in range(1, STEPS):
        wide_step(stage)
    pair, rest = fine_step(FINE_SWEEPS - 1, STEPS - 1, pair)
    rest()
    drain(len(drains))
    for stage in range(STEPS, REACH):
        wide_step(stage)


def shards(node_fields, region_label, sheet_shift, diffusivity):
    fields = node_fields[0]
    nodes, depth, width, height = fields.shape
    depth_c, rows_c = depth // BLOCK_Z, width // BLOCK_X
    near = -(-REACH // depth)
    layers, layers_c = (2 * near + 1) * depth, (2 * near + 1) * depth_c
    f32 = jnp.float32
    fine, wide = (depth, width, height), (layers, width, height)
    coarse = (depth_c, rows_c, height)
    ringed = (depth_c + 2, rows_c, height)
    padded = width + 2 * PAD
    vmem, hbm = (pl.BlockSpec(memory_space=space) for space in (pltpu.VMEM, pltpu.HBM))
    result = pl.pallas_call(
        kernel,
        out_shape=jax.ShapeDtypeStruct(fields.shape, f32),
        in_specs=[hbm] * 4,
        out_specs=vmem,
        scratch_shapes=[
            pltpu.VMEM(fields.shape, f32),
            pltpu.VMEM(wide, jnp.int32),
            pltpu.VMEM(sheet_shift.shape, jnp.int32),
            pltpu.SMEM(diffusivity.shape, f32),
            pltpu.VMEM(wide, f32),
            pltpu.VMEM(wide, f32),
            pltpu.VMEM(wide, f32),
            pltpu.VMEM(ringed, f32),
            pltpu.VMEM(fine, f32),
            pltpu.VMEM((2, width, height), f32),
            pltpu.VMEM(ringed, f32),
            pltpu.VMEM(sheet_shift.shape, jnp.int32),
            pltpu.VMEM((EXCHANGES, depth + 2, padded, height), f32),
            pltpu.VMEM((STEPS,) + fine, f32),
            pltpu.VMEM(ringed, f32),
            pltpu.VMEM(coarse, f32),
            pltpu.VMEM((2, layers_c, rows_c, height), f32),
            pltpu.VMEM(ringed, f32),
            pltpu.VMEM((2, depth_c, width, height), f32),
            pltpu.VMEM((width, height), f32),
            pltpu.VMEM((2, layers_c, width, height), f32),
            pltpu.VMEM((STEPS - 1, layers_c, width, height), f32),
            pltpu.VMEM((layers_c + 2, padded, height), f32),
            pltpu.VMEM((2, layers, padded, height), f32),
            pltpu.VMEM((STEPS,) + wide, f32),
            pltpu.VMEM(wide, f32),
            pltpu.SemaphoreType.DMA((2 * len(OPENING) + 4,)),
            pltpu.SemaphoreType.DMA((2 * len(OPENING) + 4 * PIECES,)),
            pltpu.SemaphoreType.DMA((8 + 4 * near,)),
            pltpu.SemaphoreType.DMA((8 + 4 * near,)),
            pltpu.SemaphoreType.DMA((3,)),
            pltpu.SemaphoreType.DMA((3,)),
            pltpu.SemaphoreType.DMA((2 * near,)),
            pltpu.SemaphoreType.DMA((2 * near,)),
            pltpu.SemaphoreType.DMA((4,)),
            pltpu.SemaphoreType.DMA((4,)),
            pltpu.SemaphoreType.DMA((4 * near,)),
            pltpu.SemaphoreType.DMA((4 * near,)),
            pltpu.SemaphoreType.DMA((4,)),
        ],
        compiler_params=pltpu.CompilerParams(
            collective_id=0, has_side_effects=True, vmem_limit_bytes=48 * 1024 * 1024,
        ),
    )(*(pltpu.with_memory_space_constraint(x, pltpu.HBM) for x in (fields, region_label, sheet_shift, diffusivity)))
    return result[None]


def solution(mesh):
    in_specs = (P("tm", None, "space", None, None), P("space", None, None), P("tm", None), P())
    out_specs = P("tm", None, "space", None, None)
    return jax.shard_map(shards, mesh=mesh, in_specs=in_specs, out_specs=out_specs, check_vma=False)
```

```python
import math

import jax
import jax.numpy as jnp
import numpy as np
from jax import lax
from jax.experimental import pallas as pl
from jax.experimental.pallas import tpu as pltpu
from jax.sharding import PartitionSpec as P

NODES = 5
FINE_SWEEPS = 2
BLOCK_Z = 4
BLOCK_X = 2
PAD = 8
PIECES = 4
MESH = pl.DeviceIdType.MESH

slice_length = 1.0


def node_tables():
    radius = math.sqrt(3.0 / 7.0)
    points = [0.0, (1.0 - radius) / 2.0, 0.5, (1.0 + radius) / 2.0, 1.0]
    integrals = np.zeros((4, 5))
    for column in range(5):
        coeffs = [1.0]
        divisor = 1.0
        for other in range(5):
            if other != column:
                anchor = points[other]
                product = [0.0] * (len(coeffs) + 1)
                for degree in range(len(coeffs)):
                    product[degree + 1] = product[degree + 1] + coeffs[degree]
                    product[degree] = product[degree] - anchor * coeffs[degree]
                coeffs = product
                divisor = divisor * (points[column] - anchor)
        for row in range(4):
            bottom = points[row]
            summit = points[row + 1]
            amount = 0.0
            for degree in range(len(coeffs)):
                amount = amount + coeffs[degree] / (degree + 1) * (
                    summit ** (degree + 1) - bottom ** (degree + 1)
                )
            integrals[row, column] = amount / divisor
    return (np.array(points), integrals)


TIMES, INTEGRALS = node_tables()
WEIGHTS = INTEGRALS.sum(axis=0)
STEPS = NODES - 1
REACH = FINE_SWEEPS * STEPS
EXCHANGES = 3 + REACH
FIRST = EXCHANGES - 1
OPENING = {0: 0, 1: 1, FIRST: 2}
GAPS = TIMES[1:] - TIMES[:-1]
LATE = (INTEGRALS * TIMES).sum(axis=1)
EARLY = INTEGRALS.sum(axis=1) - LATE
SLOTS = {1: 1, 2: 3, 3: 4, 4: 7, 5: 9, 6: 11}
LATE_SLICE = 7


class Transfer:
    def __init__(self, src, dst, send_sem, recv_sem, device, sends, receives):
        self.copy = pltpu.make_async_remote_copy(
            src_ref=src,
            dst_ref=dst,
            send_sem=send_sem,
            recv_sem=recv_sem,
            device_id=device,
            device_id_type=MESH,
        )
        self.sends, self.receives = sends, receives

    def start(self):
        pl.when(self.sends)(self.copy.start)

    def wait_recv(self):
        pl.when(self.receives)(self.copy.wait_recv)

    def wait_send(self):
        pl.when(self.sends)(self.copy.wait_send)


def kernel(
    fields_in, label_in, shift_in, table_in, out, fields, label, shift, table,
    kappa, inflow, decay, kappa_c, start, rim, moved, shift_next, pads, mids, gain, lift, delta, front, sums, fold,
    spread, plan, base, grid, nodes, latest,
    halo_send, halo_recv, time_send, time_recv, start_send, start_recv, wide_send, wide_recv, edge_send, edge_recv,
    label_send, label_recv, load_sem,
):
    n, s = lax.axis_index("tm"), lax.axis_index("space")
    slices, slabs = lax.axis_size("tm"), lax.axis_size("space")
    depth, width, height = fields.shape[1:]
    rows_c = width // BLOCK_X
    depth_c = depth // BLOCK_Z
    near = -(-REACH // depth)
    own, own_c = near * depth, near * depth_c
    layers, layers_c = (2 * near + 1) * depth, (2 * near + 1) * depth_c
    chunk = min(64, width)
    piece = width // PIECES
    last = NODES - 1
    has_prev, has_next = n > 0, n < slices - 1
    inner = pl.ds(PAD, width)
    here_c = pl.ds(own_c, depth_c)

    loads = [
        pltpu.make_async_copy(fields_in, fields, load_sem.at[0]),
        pltpu.make_async_copy(label_in, label.at[pl.ds(own, depth)], load_sem.at[1]),
        pltpu.make_async_copy(shift_in, shift, load_sem.at[2]),
        pltpu.make_async_copy(table_in, table, load_sem.at[3]),
    ]
    for load in loads:
        load.start()

    within = {
        distance: (s + distance >= 0) & (s + distance < slabs)
        for distance in range(-near, near + 1)
    }
    for distance in range(1, near + 1):
        for sign in (1, -1):

            @pl.when(jnp.logical_not(within[sign * distance]))
            def _(distance=distance, sign=sign):
                there = own_c + sign * distance * depth_c
                delta[:, pl.ds(there, depth_c)] = jnp.zeros((2, depth_c, rows_c, height), jnp.float32)
                if distance == 1:
                    edge = depth_c + 1 if sign == 1 else 0
                    for ref in (gain, moved, kappa_c):
                        ref[edge] = jnp.zeros((rows_c, height), jnp.float32)

    @pl.when(jnp.logical_not(has_prev))
    def _():
        moved[...] = jnp.zeros_like(moved)
        delta[0] = jnp.zeros((layers_c, rows_c, height), jnp.float32)

    barrier = pltpu.get_barrier_semaphore()
    met = jnp.int32(0)
    for dn in (-1, 0, 1):
        for ds in range(-near, near + 1):
            if dn == 0 and ds == 0:
                continue
            there = (n + dn >= 0) & (n + dn < slices) & within[ds]

            @pl.when(there)
            def _(dn=dn, ds=ds):
                pl.semaphore_signal(
                    barrier, inc=1, device_id={"tm": n + dn, "space": s + ds}, device_id_type=MESH
                )

            met = met + there.astype(jnp.int32)

    drains = []

    def halo(index, source=None):
        buf = pads.at[index]
        if index in OPENING:
            count, gone, come = 1, 2 * OPENING[index], 2 * OPENING[index]
        else:
            count = PIECES
            gone = 2 * (len(OPENING) + index % 2)
            come = 2 * (len(OPENING) + (index % 2) * PIECES)
        share = width // count

        def pair(start, rows, sem):
            here = pl.ds(PAD + start, rows)
            if source is None:
                low, high = buf.at[1, here], buf.at[depth, here]
            else:
                low, high = (source.at[z, pl.ds(start, rows)] for z in (0, depth - 1))
            up = Transfer(
                high, buf.at[0, here], halo_send.at[gone], halo_recv.at[sem + 1],
                {"space": s + 1}, within[1], within[-1],
            )
            down = Transfer(
                low, buf.at[depth + 1, here], halo_send.at[gone + 1], halo_recv.at[sem],
                {"space": s - 1}, within[-1], within[1],
            )
            return down, up

        drains.append(list(pair(0, width, come)))
        return [pair(k * share, share, come + 2 * k) for k in range(count)]

    def arrive(pieces):
        for down, up in pieces:
            down.wait_recv()
            up.wait_recv()

    side = lax.rem(n, 2)
    beyond = (side == 0) & has_prev
    always = n >= 0

    def time_hop(index, src, dst, ds=0, sends=always, receives=always):
        goes = has_next & sends if ds == 0 else has_next & sends & within[ds]
        comes = has_prev & receives if ds == 0 else has_prev & receives & within[-ds]
        to = {"tm": n + 1} if ds == 0 else {"tm": n + 1, "space": s + ds}
        return Transfer(src, dst, time_send.at[index], time_recv.at[index], to, goes, comes)

    shift_hop = Transfer(
        shift_in, shift_next, time_send.at[0], time_recv.at[0], {"tm": n - 1}, has_prev, has_next
    )
    weighted_halo = halo(0)
    end_halo = halo(1, fields_in.at[last])
    first_halo = halo(FIRST)
    rim_hops = [
        time_hop(6, fields_in.at[last, depth - 1], rim.at[0], 1),
        time_hop(7, fields_in.at[last, 0], rim.at[1], -1),
    ]
    rim_depth = min(2, depth // 2)
    spans = [(0, rim_depth), (depth - rim_depth, rim_depth), (rim_depth, depth - 2 * rim_depth)]
    start_hops = [
        Transfer(
            fields_in.at[last, pl.ds(low, count)], start.at[pl.ds(low, count)],
            start_send.at[k], start_recv.at[k], {"tm": n + 1}, has_next, has_prev,
        )
        for k, (low, count) in enumerate(spans)
        if count
    ]
    half = depth // 2
    label_parts = [[] for _ in range(half)]
    label_hops, label_forwards = [], []
    for distance in range(1, near + 1):
        for sign in (1, -1):
            sem = 2 * (distance - 1) + (sign + 1) // 2
            to, sends, receives = {"space": s + sign * distance}, within[sign * distance], within[-sign * distance]
            low = side * half
            there = own - sign * distance * depth + low
            sems = label_send.at[sem], label_recv.at[sem]
            for i in range(half):
                label_parts[i].append(
                    Transfer(label_in.at[low + i], label.at[there + i], *sems, to, sends, receives)
                )
            there = pl.ds(there, half)
            label_hops.append(
                Transfer(label_in.at[pl.ds(low, half)], label.at[there], *sems, to, sends, receives)
            )
            label_forwards.append(
                Transfer(
                    label.at[there], label.at[there],
                    label_send.at[2 * near + sem], label_recv.at[2 * near + sem],
                    {"tm": n + 1 - 2 * side}, receives, receives,
                )
            )

    own_layers = pl.ds(1, depth_c)
    whole = jnp.logical_not(beyond)
    from_beyond = (side == 1) & (n > 1)
    from_whole = jnp.logical_not(from_beyond)
    lift_hops = [
        time_hop(2, lift, moved.at[own_layers]),
        time_hop(4, lift.at[depth_c - 1], moved.at[0], 1, side == 1, beyond),
        time_hop(5, lift.at[0], moved.at[depth_c + 1], -1, side == 1, beyond),
    ]
    edge_hops = []
    for k, ref in enumerate((kappa_c, gain)):
        edge_hops.append(
            Transfer(
                ref.at[depth_c], ref.at[0], edge_send.at[2 * k], edge_recv.at[2 * k],
                {"space": s + 1}, beyond & within[1], beyond & within[-1],
            )
        )
        edge_hops.append(
            Transfer(
                ref.at[1], ref.at[depth_c + 1], edge_send.at[2 * k + 1], edge_recv.at[2 * k + 1],
                {"space": s - 1}, beyond & within[-1], beyond & within[1],
            )
        )
    front_hop = time_hop(
        1, front, delta.at[0, pl.ds(own_c - 1, depth_c + 2)], 0, beyond, from_beyond
    )
    body_hop = time_hop(3, delta.at[1, here_c], delta.at[0, here_c], 0, whole, from_whole)
    wide_hops, rest_hops, slab_hops = [], [], []
    for distance in range(1, near + 1):
        for sign in (1, -1):
            sem = 2 * (distance - 1) + (sign + 1) // 2
            there = own_c - sign * distance * depth_c
            wide_hops.append(
                Transfer(
                    delta.at[1, here_c], delta.at[1, pl.ds(there, depth_c)],
                    wide_send.at[sem], wide_recv.at[sem],
                    {"space": s + sign * distance}, within[sign * distance], within[-sign * distance],
                )
            )
            slab_hops.append(
                time_hop(
                    8 + 2 * near + sem, delta.at[1, here_c], delta.at[0, pl.ds(there, depth_c)],
                    sign * distance, whole, from_whole,
                )
            )
            skip = 1 if distance == 1 else 0
            if depth_c > skip:
                shown = skip if sign == -1 else 0
                rest_hops.append(
                    time_hop(
                        8 + sem,
                        delta.at[1, pl.ds(own_c + shown, depth_c - skip)],
                        delta.at[0, pl.ds(there + shown, depth_c - skip)],
                        sign * distance, beyond, from_beyond,
                    )
                )

    first_slice = (n == 0).astype(jnp.float32)

    def sideways(center):
        lane = lax.broadcasted_iota(jnp.int32, center.shape, 1)
        return jnp.where(lane == height - 1, 0.0, pltpu.roll(center, height - 1, 1)) + jnp.where(
            lane == 0, 0.0, pltpu.roll(center, 1, 1)
        )

    def slope(buf, layer, own_layer, r, rows):
        center = buf[layer, pl.ds(PAD + r, rows)]
        behind = buf[layer, pl.ds(PAD - 1 + r, rows)]
        total = buf[layer - 1, pl.ds(PAD + r, rows)] + buf[layer + 1, pl.ds(PAD + r, rows)]
        total = total + buf[layer, pl.ds(PAD + 1 + r, rows)]
        total = total + sideways(center)
        at = pl.ds(r, rows)
        return kappa[own_layer, at] * total + inflow[own_layer, at] * behind - decay[own_layer, at] * center

    def rate(index, z, r, chunk=chunk):
        return slope(pads.at[index], z + 1, own + z, r, chunk)

    def plain_rate(index, z, r, speed):
        buf = pads.at[index]
        center = buf[z + 1, pl.ds(PAD + r, chunk)]
        behind = buf[z + 1, pl.ds(PAD - 1 + r, chunk)]
        total = buf[z, pl.ds(PAD + r, chunk)] + buf[z + 2, pl.ds(PAD + r, chunk)]
        total = total + (behind + buf[z + 1, pl.ds(PAD + 1 + r, chunk)])
        total = total + sideways(center) - 6.0 * center
        return kappa[own + z, pl.ds(r, chunk)] * total - speed * (center - behind)

    def place(buf, layer, r, value):
        rows = value.shape[0]
        buf[layer, pl.ds(PAD + r, rows)] = value
        if r == 0:
            buf[layer, pl.ds(PAD + width, 1)] = value[:1]
        if r + rows == width:
            buf[layer, pl.ds(PAD - 1, 1)] = value[rows - 1 :]

    def fill(index, z, r, value):
        place(pads.at[index], z + 1, r, value)

    def each(lo, hi, body, unroll=1):
        def turn(z, carry):
            for r in range(0, width, chunk):
                body(z, r, chunk)
            return carry

        lax.fori_loop(lo, hi, turn, 0, unroll=unroll)

    def edges(body, needs=None, gives=None):
        count = PIECES if gives is None else len(gives)
        rows = width // count
        for k in range(count):
            if needs is not None:
                arrive(needs[k : k + 1])
            body(0, k * rows, rows)
            body(depth - 1, k * rows, rows)
            if gives is not None:
                gives[k][0].start()
                gives[k][1].start()

    def interior(body):
        each(1, depth - 1, body, 2)

    def combine(coefficients, first, z, r, chunk):
        at = pl.ds(r, chunk)
        total = (first_slice * float(coefficients[0])) * fields[0, z, at] if first is None else first
        for node in range(1, NODES):
            total = total + float(coefficients[node]) * fields[node, z, at]
        return total

    def weigh(z, r, chunk):
        fill(0, z, r, combine(slice_length * WEIGHTS, None, z, r, chunk))

    def foresee(z, r, chunk):
        fill(FIRST, z, r, combine(slice_length * INTEGRALS[0], None, z, r, chunk))

    for load in loads:
        load.wait()
    edges(weigh)
    pl.semaphore_wait(barrier, met)
    for pieces in (weighted_halo, end_halo):
        for down, up in pieces:
            down.start()
            up.start()
    shift_hop.start()
    edges(foresee, None, first_halo)
    for transfer in rim_hops:
        transfer.start()
    for transfer in start_hops:
        transfer.start()
    interior(weigh)
    advect = shift[...].astype(jnp.float32) / slice_length

    def look_up(layer, r, chunk):
        at = pl.ds(r, chunk)
        labels = label[layer, at]
        total = jnp.zeros((chunk, height), jnp.float32)
        for region in range(table.shape[0]):
            total = total + jnp.where(labels == region, table[region], 0.0)
        kappa[layer, at] = total
        inflow[layer, at] = total + advect
        decay[layer, at] = 6.0 * total + advect

    def prepare(z, r, chunk):
        fill(1, z, r, fields[last, z, pl.ds(r, chunk)])
        look_up(own + z, r, chunk)

    each(0, depth, prepare)

    for index in range(EXCHANGES):

        @pl.when(jnp.logical_not(within[-1]))
        def _(index=index):
            pads[index, 0, inner] = jnp.zeros((width, height), jnp.float32)

        @pl.when(jnp.logical_not(within[1]))
        def _(index=index):
            pads[index, depth + 1, inner] = jnp.zeros((width, height), jnp.float32)

    def restrict(target, layer_of):
        def turn(zc, carry):
            for r in range(0, width, chunk):
                total = layer_of(BLOCK_Z * zc, r)
                for k in range(1, BLOCK_Z):
                    total = total + layer_of(BLOCK_Z * zc + k, r)
                fold[pl.ds(r, chunk)] = total
            total = fold[pl.ds(0, rows_c, stride=BLOCK_X)]
            for k in range(1, BLOCK_X):
                total = total + fold[pl.ds(k, rows_c, stride=BLOCK_X)]
            target[zc] = total * (1.0 / (BLOCK_Z * BLOCK_X))
            return carry

        lax.fori_loop(0, depth_c, turn, 0)

    def block_sums(index, layer_of):
        for zc in range(depth_c):
            inside = [z for z in range(BLOCK_Z * zc, BLOCK_Z * (zc + 1)) if 0 < z < depth - 1]
            for r in range(0, width, chunk):
                total = layer_of(inside[0], r)
                for z in inside[1:]:
                    total = total + layer_of(z, r)
                sums[index, zc, pl.ds(r, chunk)] = total

    def close(index, target, layer_of):
        for zc in range(depth_c):
            for r in range(0, width, chunk):
                total = sums[index, zc, pl.ds(r, chunk)]
                if zc == 0:
                    total = total + layer_of(0, r)
                if zc == depth_c - 1:
                    total = total + layer_of(depth - 1, r)
                fold[pl.ds(r, chunk)] = total
            total = fold[pl.ds(0, rows_c, stride=BLOCK_X)]
            for k in range(1, BLOCK_X):
                total = total + fold[pl.ds(k, rows_c, stride=BLOCK_X)]
            target[zc] = total * (1.0 / (BLOCK_Z * BLOCK_X))

    def gain_layer(z, r):
        at = pl.ds(r, chunk)
        return first_slice * fields[0, z, at] - fields[last, z, at] + slice_length * rate(0, z, r)

    def lift_layer(z, r):
        weight = slice_length * float(WEIGHTS[0])
        return fields[last, z, pl.ds(r, chunk)] + weight * plain_rate(1, z, r, advect_next)

    restrict(kappa_c.at[own_layers], lambda z, r: kappa[own + z, pl.ds(r, chunk)])
    edge_hops[0].start()
    edge_hops[1].start()
    block_sums(0, gain_layer)
    shift_hop.wait_recv()
    advect_next = shift_next[...].astype(jnp.float32) / slice_length
    block_sums(1, lift_layer)
    arrive(weighted_halo)
    close(0, gain.at[own_layers], gain_layer)
    edge_hops[2].start()
    edge_hops[3].start()

    def chain(wider):
        for transfer in lift_hops + edge_hops + [body_hop] + slab_hops + [front_hop]:
            transfer.wait_recv()
        for zc in range(-1, depth_c + 1) if wider else range(depth_c):
            center = delta[0, own_c + zc]
            under, over = delta[0, own_c + zc - 1], delta[0, own_c + zc + 1]
            behind = pltpu.roll(center, 1, 0)
            across = behind + pltpu.roll(center, rows_c - 1, 0)
            lateral = sideways(center)
            spreading = kappa_c[zc + 1] * (
                (under + over - 2.0 * center) * (1.0 / (BLOCK_Z * BLOCK_Z))
                + (across - 2.0 * center) * (1.0 / (BLOCK_X * BLOCK_X))
                + (lateral - 2.0 * center)
            )
            flow = (1.0 / BLOCK_X) * advect * (center - behind)
            value = center + slice_length * (spreading - flow) + (gain[zc + 1] + moved[zc + 1])
            if 0 <= zc < depth_c:
                delta[1, own_c + zc] = value
            if wider:
                front[zc + 1] = value
        for transfer in [front_hop] if wider else slab_hops + [body_hop]:
            transfer.start()

    def spread_ends():
        for transfer in rest_hops + wide_hops:
            transfer.start()

    pl.when(n == 0)(lambda: chain(False))

    arrive(end_halo)
    close(1, lift, lift_layer)
    for transfer in lift_hops:
        transfer.start()

    @pl.when(jnp.logical_not(has_prev))
    def _():
        def turn(z, carry):
            start[z] = fields[0, z]
            return carry

        lax.fori_loop(0, depth, turn, 0)
        rim[...] = jnp.zeros_like(rim)

    for end, there in enumerate((within[-1], within[1])):

        @pl.when(has_prev & jnp.logical_not(there))
        def _(end=end):
            rim[end] = jnp.zeros((width, height), jnp.float32)

    begin_weight = slice_length * float(INTEGRALS[0, 0])

    def combine_start(z, r, chunk):
        fill(2, z, r, combine(slice_length * INTEGRALS[0], begin_weight * start[z, pl.ds(r, chunk)], z, r, chunk))

    def open_layers(which):
        for k in which:
            start_hops[k].wait_recv()
            low, count = spans[k]
            for z in range(low, low + count):
                for r in range(0, width, chunk):
                    combine_start(z, r, chunk)

    rim_hops[0].wait_recv()
    rim_hops[1].wait_recv()
    arrive(first_halo)
    for end, layer in ((0, 0), (1, depth + 1)):
        for r in range(0, width, chunk):
            at = pl.ds(PAD + r, chunk)
            pads[2, layer, at] = pads[FIRST, layer, at] + begin_weight * rim[end, pl.ds(r, chunk)]
    open_layers((0, 1))

    def fine_step(sweep, step, needs):
        old = fields if sweep == 0 else mids
        new = mids if sweep == 0 else None
        offset = 0 if sweep == 0 else -1
        index = 2 + sweep * STEPS + step
        final = sweep == FINE_SWEEPS - 1
        more = not (final and step == STEPS - 1)

        def advance(z, r, chunk):
            at = pl.ds(r, chunk)
            if step == 0:
                before = start[z, at]
            else:
                before = out[step, z, at] if final else new[step - 1, z, at]
            value = before + rate(index, z, r, chunk)
            if final:
                out[step + 1, z, at] = value
            else:
                new[step, z, at] = value
            if not more:
                return
            weights = slice_length * INTEGRALS[(step + 1) % STEPS]
            if step < STEPS - 1:
                total = slice_length * float(GAPS[step + 1]) * value
                weights[step + 1] -= slice_length * GAPS[step + 1]
                source, shown, known = old, offset, {}
            else:
                total, source, shown, known = None, new, -1, {STEPS: value}
            for node in range(NODES):
                if node == 0:
                    part = start[z, at]
                else:
                    part = known[node] if node in known else source[node + shown, z, at]
                term = float(weights[node]) * part
                total = term if total is None else total + term
            fill(index + 1, z, r, total)

        if not more:
            return None, lambda: (arrive(needs), each(0, depth, advance, 4))
        following = halo(index + 1)
        edges(advance, needs, following)
        return following, lambda: interior(advance)

    def drain(count):
        for group in drains[:count]:
            for transfer in group:
                transfer.wait_send()
        del drains[:count]

    pair = None
    for stage in range(REACH - 2):
        early = [slice_at for slice_at, slot in SLOTS.items() if slot == 2 * stage]
        late = [slice_at for slice_at, slot in SLOTS.items() if slot == 2 * stage + 1]
        for slice_at in early:
            pl.when(n == slice_at)(lambda wider=slice_at % 2 == 0: chain(wider))
        pair, rest = fine_step(stage // STEPS, stage % STEPS, pair)
        for slice_at in late:
            pl.when(n == slice_at)(lambda wider=slice_at % 2 == 0: chain(wider))
        if stage < half:
            for transfer in label_parts[stage]:
                transfer.start()
        for slice_at in early + late + ([0] if stage == 0 else []):
            pl.when(n == slice_at)(spread_ends)
        if stage == 0:
            open_layers(range(2, len(start_hops)))
        rest()
        if stage == half:
            for first, second in zip(label_hops, label_forwards):
                first.wait_recv()
                second.start()
        drain(len(drains) - 1)

    for transfer in label_forwards:
        transfer.wait_recv()
    for distance in range(1, near + 1):
        for sign in (1, -1):
            low = own + sign * distance * depth
            there = within[sign * distance]

            @pl.when(there)
            def _(low=low):
                each(low, low + depth, look_up)

            @pl.when(jnp.logical_not(there))
            def _(low=low):
                def turn(z, carry):
                    kappa[z] = jnp.zeros((width, height), jnp.float32)
                    inflow[z] = jnp.zeros((width, height), jnp.float32)
                    decay[z] = jnp.zeros((width, height), jnp.float32)
                    return carry

                lax.fori_loop(low, low + depth, turn, 0)

    pair, rest = fine_step(FINE_SWEEPS - 1, STEPS - 2, pair)
    pl.when((n >= LATE_SLICE) & (side == 1))(lambda: chain(False))
    if slices > LATE_SLICE + 1:
        pl.when((n >= LATE_SLICE) & (side == 0))(lambda: chain(True))
    pl.when(n >= LATE_SLICE)(spread_ends)
    rest()

    drain(len(drains) - 1)
    for transfer in label_hops + label_forwards + lift_hops + edge_hops + rim_hops + start_hops:
        transfer.wait_send()
    for transfer in [shift_hop, front_hop, body_hop] + slab_hops + rest_hops + wide_hops:
        transfer.wait_send()
    for transfer in wide_hops + rest_hops:
        transfer.wait_recv()

    def mix(early, late, begin, finish):
        return (slice_length * float(early)) * begin + (slice_length * float(late)) * finish

    def widen(c, carry):
        for field in range(2):
            for k in range(BLOCK_X):
                spread[field, c, pl.ds(k, rows_c, stride=BLOCK_X)] = delta[field, c]
        for r in range(0, width, chunk):
            at = pl.ds(r, chunk)
            begin, finish = spread[0, c, at], spread[1, c, at]
            place(base, c + 1, r, mix(EARLY[0], LATE[0], begin, finish))
            for row in range(1, STEPS):
                gap, weight = float(GAPS[row]), float(TIMES[row])
                plan[row - 1, c, at] = mix(
                    EARLY[row] - gap * (1.0 - weight), LATE[row] - gap * weight, begin, finish
                )
        return carry

    lax.fori_loop(0, layers_c, widen, 0)
    base[0, inner] = jnp.zeros((width, height), jnp.float32)
    base[layers_c + 1, inner] = jnp.zeros((width, height), jnp.float32)

    def open_step(c, carry):
        for r in range(0, width, 32):
            at, inside = pl.ds(r, 32), pl.ds(PAD + r, 32)
            center = base[c + 1, inside]
            behind = base[c + 1, pl.ds(PAD - 1 + r, 32)]
            level = base[c + 1, pl.ds(PAD + 1 + r, 32)] + sideways(center)
            initial, following = spread[0, c, at], plan[0, c, at]
            for k in range(BLOCK_Z):
                layer = BLOCK_Z * c + k
                under = base[c, inside] if k == 0 else center
                over = base[c + 2, inside] if k == BLOCK_Z - 1 else center
                total = level + (under + over)
                value = initial + (kappa[layer, at] * total + inflow[layer, at] * behind - decay[layer, at] * center)
                nodes[0, layer, at] = value
                place(grid.at[0], layer, r, float(GAPS[1]) * slice_length * value + following)
        return carry

    def wide_each(margin, body, apart):
        if not apart:

            def through(i, carry):
                for r in range(0, width, chunk):
                    body(own - margin + i, None, r)
                return carry

            lax.fori_loop(0, depth + 2 * margin, through, 0, unroll=(depth + 2 * margin) // 2)
            return

        def outer(i, carry):
            layer = own - margin + i + jnp.where(i >= margin, depth, 0)
            for r in range(0, width, chunk):
                body(layer, None, r)
            return carry

        def middle(z, carry):
            for r in range(0, width, chunk):
                body(own + z, z, r)
            return carry

        if margin > 0:
            lax.fori_loop(0, 2 * margin, outer, 0, unroll=min(8, 2 * margin))
        lax.fori_loop(0, depth, middle, 0, unroll=min(8, depth))

    def wide_step(stage):
        sweep, step = stage // STEPS, stage % STEPS
        source, target = grid.at[(stage - 1) % 2], grid.at[stage % 2]
        margin = REACH - 1 - stage
        final = sweep == FINE_SWEEPS - 1
        more = stage < REACH - 1

        def advance(layer, z, r):
            at, c = pl.ds(r, chunk), layer // BLOCK_Z
            if step == 0 or final:
                initial = spread[0, c, at]
            if step == 0:
                before = initial
            else:
                before = latest[layer, at] if final else nodes[step - 1, layer, at]
            value = before + slope(source, layer, layer, r, chunk)
            if final:
                if more:
                    latest[layer, at] = value
                if z is not None:
                    out[step + 1, z, at] = out[step + 1, z, at] + value
                    if step == 0:
                        out[0, z, at] = start[z, at] + initial
            else:
                nodes[step, layer, at] = value
            if not more:
                return
            if not final and step < STEPS - 1:
                total = slice_length * float(GAPS[step + 1]) * value + plan[step, c, at]
            else:
                weights = slice_length * INTEGRALS[(step + 1) % STEPS]
                known = {}
                if final:
                    total = slice_length * float(GAPS[step + 1]) * value + float(weights[0]) * initial
                    weights[step + 1] -= slice_length * GAPS[step + 1]
                else:
                    total = float(weights[0]) * spread[0, c, at]
                    known = {STEPS: value}
                for node in range(1, NODES):
                    part = known[node] if node in known else nodes[node - 1, layer, at]
                    total = total + float(weights[node]) * part
            place(target, layer, r, total)

        wide_each(margin, advance, final)

    lax.fori_loop(0, layers_c, open_step, 0)
    for stage in range(1, STEPS):
        wide_step(stage)
    pair, rest = fine_step(FINE_SWEEPS - 1, STEPS - 1, pair)
    rest()
    drain(len(drains))
    for stage in range(STEPS, REACH):
        wide_step(stage)


def shards(node_fields, region_label, sheet_shift, diffusivity):
    fields = node_fields[0]
    nodes, depth, width, height = fields.shape
    depth_c, rows_c = depth // BLOCK_Z, width // BLOCK_X
    near = -(-REACH // depth)
    layers, layers_c = (2 * near + 1) * depth, (2 * near + 1) * depth_c
    f32 = jnp.float32
    fine, wide = (depth, width, height), (layers, width, height)
    coarse = (depth_c, rows_c, height)
    ringed = (depth_c + 2, rows_c, height)
    padded = width + 2 * PAD
    vmem, hbm = (pl.BlockSpec(memory_space=space) for space in (pltpu.VMEM, pltpu.HBM))
    result = pl.pallas_call(
        kernel,
        out_shape=jax.ShapeDtypeStruct(fields.shape, f32),
        in_specs=[hbm] * 4,
        out_specs=vmem,
        scratch_shapes=[
            pltpu.VMEM(fields.shape, f32),
            pltpu.VMEM(wide, jnp.int32),
            pltpu.VMEM(sheet_shift.shape, jnp.int32),
            pltpu.SMEM(diffusivity.shape, f32),
            pltpu.VMEM(wide, f32),
            pltpu.VMEM(wide, f32),
            pltpu.VMEM(wide, f32),
            pltpu.VMEM(ringed, f32),
            pltpu.VMEM(fine, f32),
            pltpu.VMEM((2, width, height), f32),
            pltpu.VMEM(ringed, f32),
            pltpu.VMEM(sheet_shift.shape, jnp.int32),
            pltpu.VMEM((EXCHANGES, depth + 2, padded, height), f32),
            pltpu.VMEM((STEPS,) + fine, f32),
            pltpu.VMEM(ringed, f32),
            pltpu.VMEM(coarse, f32),
            pltpu.VMEM((2, layers_c, rows_c, height), f32),
            pltpu.VMEM(ringed, f32),
            pltpu.VMEM((2, depth_c, width, height), f32),
            pltpu.VMEM((width, height), f32),
            pltpu.VMEM((2, layers_c, width, height), f32),
            pltpu.VMEM((STEPS - 1, layers_c, width, height), f32),
            pltpu.VMEM((layers_c + 2, padded, height), f32),
            pltpu.VMEM((2, layers, padded, height), f32),
            pltpu.VMEM((STEPS,) + wide, f32),
            pltpu.VMEM(wide, f32),
            pltpu.SemaphoreType.DMA((2 * len(OPENING) + 4,)),
            pltpu.SemaphoreType.DMA((2 * len(OPENING) + 4 * PIECES,)),
            pltpu.SemaphoreType.DMA((8 + 4 * near,)),
            pltpu.SemaphoreType.DMA((8 + 4 * near,)),
            pltpu.SemaphoreType.DMA((3,)),
            pltpu.SemaphoreType.DMA((3,)),
            pltpu.SemaphoreType.DMA((2 * near,)),
            pltpu.SemaphoreType.DMA((2 * near,)),
            pltpu.SemaphoreType.DMA((4,)),
            pltpu.SemaphoreType.DMA((4,)),
            pltpu.SemaphoreType.DMA((4 * near,)),
            pltpu.SemaphoreType.DMA((4 * near,)),
            pltpu.SemaphoreType.DMA((4,)),
        ],
        compiler_params=pltpu.CompilerParams(
            collective_id=0, has_side_effects=True, vmem_limit_bytes=48 * 1024 * 1024,
        ),
    )(*(pltpu.with_memory_space_constraint(x, pltpu.HBM) for x in (fields, region_label, sheet_shift, diffusivity)))
    return result[None]


def solution(mesh):
    in_specs = (P("tm", None, "space", None, None), P("space", None, None), P("tm", None), P())
    out_specs = P("tm", None, "space", None, None)
    return jax.shard_map(shards, mesh=mesh, in_specs=in_specs, out_specs=out_specs, check_vma=False)
```

```python
import math

import jax
import jax.numpy as jnp
import numpy as np
from jax import lax
from jax.experimental import pallas as pl
from jax.experimental.pallas import tpu as pltpu
from jax.sharding import PartitionSpec as P

NODES = 5
FINE_SWEEPS = 2
BLOCK_Z = 4
BLOCK_X = 2
PAD = 8
PIECES = 4
MESH = pl.DeviceIdType.MESH

slice_length = 1.0


def node_tables():
    radius = math.sqrt(3.0 / 7.0)
    points = [0.0, (1.0 - radius) / 2.0, 0.5, (1.0 + radius) / 2.0, 1.0]
    integrals = np.zeros((4, 5))
    for column in range(5):
        coeffs = [1.0]
        divisor = 1.0
        for other in range(5):
            if other != column:
                anchor = points[other]
                product = [0.0] * (len(coeffs) + 1)
                for degree in range(len(coeffs)):
                    product[degree + 1] = product[degree + 1] + coeffs[degree]
                    product[degree] = product[degree] - anchor * coeffs[degree]
                coeffs = product
                divisor = divisor * (points[column] - anchor)
        for row in range(4):
            bottom = points[row]
            summit = points[row + 1]
            amount = 0.0
            for degree in range(len(coeffs)):
                amount = amount + coeffs[degree] / (degree + 1) * (
                    summit ** (degree + 1) - bottom ** (degree + 1)
                )
            integrals[row, column] = amount / divisor
    return (np.array(points), integrals)


TIMES, INTEGRALS = node_tables()
WEIGHTS = INTEGRALS.sum(axis=0)
STEPS = NODES - 1
REACH = FINE_SWEEPS * STEPS
EXCHANGES = 3 + REACH
FIRST = EXCHANGES - 1
OPENING = {0: 0, 1: 1, FIRST: 2}
GAPS = TIMES[1:] - TIMES[:-1]
LATE = (INTEGRALS * TIMES).sum(axis=1)
EARLY = INTEGRALS.sum(axis=1) - LATE
SLOTS = {1: 1, 2: 3, 3: 4, 4: 7, 5: 9, 6: 11}
LATE_SLICE = 7


class Transfer:
    def __init__(self, src, dst, send_sem, recv_sem, device, sends, receives):
        self.copy = pltpu.make_async_remote_copy(
            src_ref=src,
            dst_ref=dst,
            send_sem=send_sem,
            recv_sem=recv_sem,
            device_id=device,
            device_id_type=MESH,
        )
        self.sends, self.receives = sends, receives

    def start(self):
        pl.when(self.sends)(self.copy.start)

    def wait_recv(self):
        pl.when(self.receives)(self.copy.wait_recv)

    def wait_send(self):
        pl.when(self.sends)(self.copy.wait_send)


def kernel(
    fields_in, label_in, shift_in, table_in, out, fields, label, shift, table,
    kappa, inflow, decay, kappa_c, start, rim, moved, shift_next, pads, mids, gain, lift, delta, front, sums, fold,
    spread, plan, base, grid, nodes, latest,
    halo_send, halo_recv, time_send, time_recv, start_send, start_recv, wide_send, wide_recv, edge_send, edge_recv,
    label_send, label_recv, load_sem,
):
    n, s = lax.axis_index("tm"), lax.axis_index("space")
    slices, slabs = lax.axis_size("tm"), lax.axis_size("space")
    depth, width, height = fields.shape[1:]
    rows_c = width // BLOCK_X
    depth_c = depth // BLOCK_Z
    near = -(-REACH // depth)
    own, own_c = near * depth, near * depth_c
    layers, layers_c = (2 * near + 1) * depth, (2 * near + 1) * depth_c
    chunk = min(64, width)
    piece = width // PIECES
    last = NODES - 1
    has_prev, has_next = n > 0, n < slices - 1
    inner = pl.ds(PAD, width)
    here_c = pl.ds(own_c, depth_c)

    loads = [
        pltpu.make_async_copy(fields_in, fields, load_sem.at[0]),
        pltpu.make_async_copy(label_in, label.at[pl.ds(own, depth)], load_sem.at[1]),
        pltpu.make_async_copy(shift_in, shift, load_sem.at[2]),
        pltpu.make_async_copy(table_in, table, load_sem.at[3]),
    ]
    for load in loads:
        load.start()

    within = {
        distance: (s + distance >= 0) & (s + distance < slabs)
        for distance in range(-near, near + 1)
    }
    for distance in range(1, near + 1):
        for sign in (1, -1):

            @pl.when(jnp.logical_not(within[sign * distance]))
            def _(distance=distance, sign=sign):
                there = own_c + sign * distance * depth_c
                delta[:, pl.ds(there, depth_c)] = jnp.zeros((2, depth_c, rows_c, height), jnp.float32)
                if distance == 1:
                    edge = depth_c + 1 if sign == 1 else 0
                    for ref in (gain, moved, kappa_c):
                        ref[edge] = jnp.zeros((rows_c, height), jnp.float32)

    @pl.when(jnp.logical_not(has_prev))
    def _():
        moved[...] = jnp.zeros_like(moved)
        delta[0] = jnp.zeros((layers_c, rows_c, height), jnp.float32)

    barrier = pltpu.get_barrier_semaphore()
    met = jnp.int32(0)
    for dn in (-1, 0, 1):
        for ds in range(-near, near + 1):
            if dn == 0 and ds == 0:
                continue
            there = (n + dn >= 0) & (n + dn < slices) & within[ds]

            @pl.when(there)
            def _(dn=dn, ds=ds):
                pl.semaphore_signal(
                    barrier, inc=1, device_id={"tm": n + dn, "space": s + ds}, device_id_type=MESH
                )

            met = met + there.astype(jnp.int32)

    drains = []

    def halo(index, source=None):
        buf = pads.at[index]
        if index in OPENING:
            count, gone, come = 1, 2 * OPENING[index], 2 * OPENING[index]
        else:
            count = PIECES
            gone = 2 * (len(OPENING) + index % 2)
            come = 2 * (len(OPENING) + (index % 2) * PIECES)
        share = width // count

        def pair(start, rows, sem):
            here = pl.ds(PAD + start, rows)
            if source is None:
                low, high = buf.at[1, here], buf.at[depth, here]
            else:
                low, high = (source.at[z, pl.ds(start, rows)] for z in (0, depth - 1))
            up = Transfer(
                high, buf.at[0, here], halo_send.at[gone], halo_recv.at[sem + 1],
                {"space": s + 1}, within[1], within[-1],
            )
            down = Transfer(
                low, buf.at[depth + 1, here], halo_send.at[gone + 1], halo_recv.at[sem],
                {"space": s - 1}, within[-1], within[1],
            )
            return down, up

        drains.append(list(pair(0, width, come)))
        return [pair(k * share, share, come + 2 * k) for k in range(count)]

    def arrive(pieces):
        for down, up in pieces:
            down.wait_recv()
            up.wait_recv()

    side = lax.rem(n, 2)
    beyond = (side == 0) & has_prev
    always = n >= 0

    def time_hop(index, src, dst, ds=0, sends=always, receives=always):
        goes = has_next & sends if ds == 0 else has_next & sends & within[ds]
        comes = has_prev & receives if ds == 0 else has_prev & receives & within[-ds]
        to = {"tm": n + 1} if ds == 0 else {"tm": n + 1, "space": s + ds}
        return Transfer(src, dst, time_send.at[index], time_recv.at[index], to, goes, comes)

    shift_hop = Transfer(
        shift_in, shift_next, time_send.at[0], time_recv.at[0], {"tm": n - 1}, has_prev, has_next
    )
    weighted_halo = halo(0)
    end_halo = halo(1, fields_in.at[last])
    first_halo = halo(FIRST)
    rim_hops = [
        time_hop(6, fields_in.at[last, depth - 1], rim.at[0], 1),
        time_hop(7, fields_in.at[last, 0], rim.at[1], -1),
    ]
    rim_depth = min(2, depth // 2)
    spans = [(0, rim_depth), (depth - rim_depth, rim_depth), (rim_depth, depth - 2 * rim_depth)]
    start_hops = [
        Transfer(
            fields_in.at[last, pl.ds(low, count)], start.at[pl.ds(low, count)],
            start_send.at[k], start_recv.at[k], {"tm": n + 1}, has_next, has_prev,
        )
        for k, (low, count) in enumerate(spans)
        if count
    ]
    half = depth // 2
    label_parts = [[] for _ in range(half)]
    label_hops, label_forwards = [], []
    for distance in range(1, near + 1):
        for sign in (1, -1):
            sem = 2 * (distance - 1) + (sign + 1) // 2
            to, sends, receives = {"space": s + sign * distance}, within[sign * distance], within[-sign * distance]
            low = side * half
            there = own - sign * distance * depth + low
            sems = label_send.at[sem], label_recv.at[sem]
            for i in range(half):
                label_parts[i].append(
                    Transfer(label_in.at[low + i], label.at[there + i], *sems, to, sends, receives)
                )
            there = pl.ds(there, half)
            label_hops.append(
                Transfer(label_in.at[pl.ds(low, half)], label.at[there], *sems, to, sends, receives)
            )
            label_forwards.append(
                Transfer(
                    label.at[there], label.at[there],
                    label_send.at[2 * near + sem], label_recv.at[2 * near + sem],
                    {"tm": n + 1 - 2 * side}, receives, receives,
                )
            )

    own_layers = pl.ds(1, depth_c)
    whole = jnp.logical_not(beyond)
    from_beyond = (side == 1) & (n > 1)
    from_whole = jnp.logical_not(from_beyond)
    lift_hops = [
        time_hop(2, lift, moved.at[own_layers]),
        time_hop(4, lift.at[depth_c - 1], moved.at[0], 1, side == 1, beyond),
        time_hop(5, lift.at[0], moved.at[depth_c + 1], -1, side == 1, beyond),
    ]
    edge_hops = []
    for k, ref in enumerate((kappa_c, gain)):
        edge_hops.append(
            Transfer(
                ref.at[depth_c], ref.at[0], edge_send.at[2 * k], edge_recv.at[2 * k],
                {"space": s + 1}, beyond & within[1], beyond & within[-1],
            )
        )
        edge_hops.append(
            Transfer(
                ref.at[1], ref.at[depth_c + 1], edge_send.at[2 * k + 1], edge_recv.at[2 * k + 1],
                {"space": s - 1}, beyond & within[-1], beyond & within[1],
            )
        )
    front_hop = time_hop(
        1, front, delta.at[0, pl.ds(own_c - 1, depth_c + 2)], 0, beyond, from_beyond
    )
    body_hop = time_hop(3, delta.at[1, here_c], delta.at[0, here_c], 0, whole, from_whole)
    wide_hops, rest_hops, slab_hops = [], [], []
    for distance in range(1, near + 1):
        for sign in (1, -1):
            sem = 2 * (distance - 1) + (sign + 1) // 2
            there = own_c - sign * distance * depth_c
            wide_hops.append(
                Transfer(
                    delta.at[1, here_c], delta.at[1, pl.ds(there, depth_c)],
                    wide_send.at[sem], wide_recv.at[sem],
                    {"space": s + sign * distance}, within[sign * distance], within[-sign * distance],
                )
            )
            slab_hops.append(
                time_hop(
                    8 + 2 * near + sem, delta.at[1, here_c], delta.at[0, pl.ds(there, depth_c)],
                    sign * distance, whole, from_whole,
                )
            )
            skip = 1 if distance == 1 else 0
            if depth_c > skip:
                shown = skip if sign == -1 else 0
                rest_hops.append(
                    time_hop(
                        8 + sem,
                        delta.at[1, pl.ds(own_c + shown, depth_c - skip)],
                        delta.at[0, pl.ds(there + shown, depth_c - skip)],
                        sign * distance, beyond, from_beyond,
                    )
                )

    first_slice = (n == 0).astype(jnp.float32)

    def sideways(center):
        lane = lax.broadcasted_iota(jnp.int32, center.shape, 1)
        return jnp.where(lane == height - 1, 0.0, pltpu.roll(center, height - 1, 1)) + jnp.where(
            lane == 0, 0.0, pltpu.roll(center, 1, 1)
        )

    def slope(buf, layer, own_layer, r, rows):
        center = buf[layer, pl.ds(PAD + r, rows)]
        behind = buf[layer, pl.ds(PAD - 1 + r, rows)]
        total = buf[layer - 1, pl.ds(PAD + r, rows)] + buf[layer + 1, pl.ds(PAD + r, rows)]
        total = total + buf[layer, pl.ds(PAD + 1 + r, rows)]
        total = total + sideways(center)
        at = pl.ds(r, rows)
        return kappa[own_layer, at] * total + inflow[own_layer, at] * behind - decay[own_layer, at] * center

    def rate(index, z, r, chunk=chunk):
        return slope(pads.at[index], z + 1, own + z, r, chunk)

    def plain_rate(index, z, r, speed):
        buf = pads.at[index]
        center = buf[z + 1, pl.ds(PAD + r, chunk)]
        behind = buf[z + 1, pl.ds(PAD - 1 + r, chunk)]
        total = buf[z, pl.ds(PAD + r, chunk)] + buf[z + 2, pl.ds(PAD + r, chunk)]
        total = total + (behind + buf[z + 1, pl.ds(PAD + 1 + r, chunk)])
        total = total + sideways(center) - 6.0 * center
        return kappa[own + z, pl.ds(r, chunk)] * total - speed * (center - behind)

    def place(buf, layer, r, value):
        rows = value.shape[0]
        buf[layer, pl.ds(PAD + r, rows)] = value
        if r == 0:
            buf[layer, pl.ds(PAD + width, 1)] = value[:1]
        if r + rows == width:
            buf[layer, pl.ds(PAD - 1, 1)] = value[rows - 1 :]

    def fill(index, z, r, value):
        place(pads.at[index], z + 1, r, value)

    def each(lo, hi, body, unroll=1):
        def turn(z, carry):
            for r in range(0, width, chunk):
                body(z, r, chunk)
            return carry

        lax.fori_loop(lo, hi, turn, 0, unroll=unroll)

    def edges(body, needs=None, gives=None):
        count = PIECES if gives is None else len(gives)
        rows = width // count
        for k in range(count):
            if needs is not None:
                arrive(needs[k : k + 1])
            body(0, k * rows, rows)
            body(depth - 1, k * rows, rows)
            if gives is not None:
                gives[k][0].start()
                gives[k][1].start()

    def interior(body):
        each(1, depth - 1, body, 2)

    def combine(coefficients, first, z, r, chunk):
        at = pl.ds(r, chunk)
        total = (first_slice * float(coefficients[0])) * fields[0, z, at] if first is None else first
        for node in range(1, NODES):
            total = total + float(coefficients[node]) * fields[node, z, at]
        return total

    def weigh(z, r, chunk):
        fill(0, z, r, combine(slice_length * WEIGHTS, None, z, r, chunk))

    def foresee(z, r, chunk):
        fill(FIRST, z, r, combine(slice_length * INTEGRALS[0], None, z, r, chunk))

    for load in loads:
        load.wait()
    edges(weigh)
    pl.semaphore_wait(barrier, met)
    for pieces in (weighted_halo, end_halo):
        for down, up in pieces:
            down.start()
            up.start()
    shift_hop.start()
    edges(foresee, None, first_halo)
    for transfer in rim_hops:
        transfer.start()
    for transfer in start_hops:
        transfer.start()
    interior(weigh)
    advect = shift[...].astype(jnp.float32) / slice_length

    def look_up(layer, r, chunk):
        at = pl.ds(r, chunk)
        labels = label[layer, at]
        total = jnp.zeros((chunk, height), jnp.float32)
        for region in range(table.shape[0]):
            total = total + jnp.where(labels == region, table[region], 0.0)
        kappa[layer, at] = total
        inflow[layer, at] = total + advect
        decay[layer, at] = 6.0 * total + advect

    def prepare(z, r, chunk):
        fill(1, z, r, fields[last, z, pl.ds(r, chunk)])
        look_up(own + z, r, chunk)

    each(0, depth, prepare)

    for index in range(EXCHANGES):

        @pl.when(jnp.logical_not(within[-1]))
        def _(index=index):
            pads[index, 0, inner] = jnp.zeros((width, height), jnp.float32)

        @pl.when(jnp.logical_not(within[1]))
        def _(index=index):
            pads[index, depth + 1, inner] = jnp.zeros((width, height), jnp.float32)

    def restrict(target, layer_of):
        def turn(zc, carry):
            for r in range(0, width, chunk):
                total = layer_of(BLOCK_Z * zc, r)
                for k in range(1, BLOCK_Z):
                    total = total + layer_of(BLOCK_Z * zc + k, r)
                fold[pl.ds(r, chunk)] = total
            total = fold[pl.ds(0, rows_c, stride=BLOCK_X)]
            for k in range(1, BLOCK_X):
                total = total + fold[pl.ds(k, rows_c, stride=BLOCK_X)]
            target[zc] = total * (1.0 / (BLOCK_Z * BLOCK_X))
            return carry

        lax.fori_loop(0, depth_c, turn, 0)

    def block_sums(index, layer_of):
        for zc in range(depth_c):
            inside = [z for z in range(BLOCK_Z * zc, BLOCK_Z * (zc + 1)) if 0 < z < depth - 1]
            for r in range(0, width, chunk):
                total = layer_of(inside[0], r)
                for z in inside[1:]:
                    total = total + layer_of(z, r)
                sums[index, zc, pl.ds(r, chunk)] = total

    def close(index, target, layer_of):
        for zc in range(depth_c):
            for r in range(0, width, chunk):
                total = sums[index, zc, pl.ds(r, chunk)]
                if zc == 0:
                    total = total + layer_of(0, r)
                if zc == depth_c - 1:
                    total = total + layer_of(depth - 1, r)
                fold[pl.ds(r, chunk)] = total
            total = fold[pl.ds(0, rows_c, stride=BLOCK_X)]
            for k in range(1, BLOCK_X):
                total = total + fold[pl.ds(k, rows_c, stride=BLOCK_X)]
            target[zc] = total * (1.0 / (BLOCK_Z * BLOCK_X))

    def gain_layer(z, r):
        at = pl.ds(r, chunk)
        return first_slice * fields[0, z, at] - fields[last, z, at] + slice_length * rate(0, z, r)

    def lift_layer(z, r):
        weight = slice_length * float(WEIGHTS[0])
        return fields[last, z, pl.ds(r, chunk)] + weight * plain_rate(1, z, r, advect_next)

    restrict(kappa_c.at[own_layers], lambda z, r: kappa[own + z, pl.ds(r, chunk)])
    edge_hops[0].start()
    edge_hops[1].start()
    block_sums(0, gain_layer)
    shift_hop.wait_recv()
    advect_next = shift_next[...].astype(jnp.float32) / slice_length
    block_sums(1, lift_layer)
    arrive(weighted_halo)
    close(0, gain.at[own_layers], gain_layer)
    edge_hops[2].start()
    edge_hops[3].start()

    def chain(wider):
        for transfer in lift_hops + edge_hops + [body_hop] + slab_hops + [front_hop]:
            transfer.wait_recv()
        for zc in range(-1, depth_c + 1) if wider else range(depth_c):
            center = delta[0, own_c + zc]
            under, over = delta[0, own_c + zc - 1], delta[0, own_c + zc + 1]
            behind = pltpu.roll(center, 1, 0)
            across = behind + pltpu.roll(center, rows_c - 1, 0)
            lateral = sideways(center)
            spreading = kappa_c[zc + 1] * (
                (under + over - 2.0 * center) * (1.0 / (BLOCK_Z * BLOCK_Z))
                + (across - 2.0 * center) * (1.0 / (BLOCK_X * BLOCK_X))
                + (lateral - 2.0 * center)
            )
            flow = (1.0 / BLOCK_X) * advect * (center - behind)
            value = center + slice_length * (spreading - flow) + (gain[zc + 1] + moved[zc + 1])
            if 0 <= zc < depth_c:
                delta[1, own_c + zc] = value
            if wider:
                front[zc + 1] = value
        for transfer in [front_hop] if wider else slab_hops + [body_hop]:
            transfer.start()

    def spread_ends():
        for transfer in rest_hops + wide_hops:
            transfer.start()

    pl.when(n == 0)(lambda: chain(False))

    arrive(end_halo)
    close(1, lift, lift_layer)
    for transfer in lift_hops:
        transfer.start()

    @pl.when(jnp.logical_not(has_prev))
    def _():
        def turn(z, carry):
            start[z] = fields[0, z]
            return carry

        lax.fori_loop(0, depth, turn, 0)
        rim[...] = jnp.zeros_like(rim)

    for end, there in enumerate((within[-1], within[1])):

        @pl.when(has_prev & jnp.logical_not(there))
        def _(end=end):
            rim[end] = jnp.zeros((width, height), jnp.float32)

    begin_weight = slice_length * float(INTEGRALS[0, 0])

    def combine_start(z, r, chunk):
        fill(2, z, r, combine(slice_length * INTEGRALS[0], begin_weight * start[z, pl.ds(r, chunk)], z, r, chunk))

    def open_layers(which):
        for k in which:
            start_hops[k].wait_recv()
            low, count = spans[k]
            for z in range(low, low + count):
                for r in range(0, width, chunk):
                    combine_start(z, r, chunk)

    rim_hops[0].wait_recv()
    rim_hops[1].wait_recv()
    arrive(first_halo)
    for end, layer in ((0, 0), (1, depth + 1)):
        for r in range(0, width, chunk):
            at = pl.ds(PAD + r, chunk)
            pads[2, layer, at] = pads[FIRST, layer, at] + begin_weight * rim[end, pl.ds(r, chunk)]
    open_layers((0, 1))

    def fine_step(sweep, step, needs):
        old = fields if sweep == 0 else mids
        new = mids if sweep == 0 else None
        offset = 0 if sweep == 0 else -1
        index = 2 + sweep * STEPS + step
        final = sweep == FINE_SWEEPS - 1
        more = not (final and step == STEPS - 1)

        def advance(z, r, chunk):
            at = pl.ds(r, chunk)
            if step == 0:
                before = start[z, at]
            else:
                before = out[step, z, at] if final else new[step - 1, z, at]
            value = before + rate(index, z, r, chunk)
            if final:
                out[step + 1, z, at] = value
            else:
                new[step, z, at] = value
            if not more:
                return
            weights = slice_length * INTEGRALS[(step + 1) % STEPS]
            if step < STEPS - 1:
                total = slice_length * float(GAPS[step + 1]) * value
                weights[step + 1] -= slice_length * GAPS[step + 1]
                source, shown, known = old, offset, {}
            else:
                total, source, shown, known = None, new, -1, {STEPS: value}
            for node in range(NODES):
                if node == 0:
                    part = start[z, at]
                else:
                    part = known[node] if node in known else source[node + shown, z, at]
                term = float(weights[node]) * part
                total = term if total is None else total + term
            fill(index + 1, z, r, total)

        if not more:
            return None, lambda: (arrive(needs), each(0, depth, advance, min(8, depth)))
        following = halo(index + 1)
        edges(advance, needs, following)
        return following, lambda: interior(advance)

    def drain(count):
        for group in drains[:count]:
            for transfer in group:
                transfer.wait_send()
        del drains[:count]

    pair = None
    for stage in range(REACH - 2):
        early = [slice_at for slice_at, slot in SLOTS.items() if slot == 2 * stage]
        late = [slice_at for slice_at, slot in SLOTS.items() if slot == 2 * stage + 1]
        for slice_at in early:
            pl.when(n == slice_at)(lambda wider=slice_at % 2 == 0: chain(wider))
        pair, rest = fine_step(stage // STEPS, stage % STEPS, pair)
        for slice_at in late:
            pl.when(n == slice_at)(lambda wider=slice_at % 2 == 0: chain(wider))
        if stage < half:
            for transfer in label_parts[stage]:
                transfer.start()
        for slice_at in early + late + ([0] if stage == 0 else []):
            pl.when(n == slice_at)(spread_ends)
        if stage == 0:
            open_layers(range(2, len(start_hops)))
        rest()
        if stage == half:
            for first, second in zip(label_hops, label_forwards):
                first.wait_recv()
                second.start()
        drain(len(drains) - 1)

    for transfer in label_forwards:
        transfer.wait_recv()
    for distance in range(1, near + 1):
        for sign in (1, -1):
            low = own + sign * distance * depth
            there = within[sign * distance]

            @pl.when(there)
            def _(low=low):
                each(low, low + depth, look_up)

            @pl.when(jnp.logical_not(there))
            def _(low=low):
                def turn(z, carry):
                    kappa[z] = jnp.zeros((width, height), jnp.float32)
                    inflow[z] = jnp.zeros((width, height), jnp.float32)
                    decay[z] = jnp.zeros((width, height), jnp.float32)
                    return carry

                lax.fori_loop(low, low + depth, turn, 0)

    pair, rest = fine_step(FINE_SWEEPS - 1, STEPS - 2, pair)
    pl.when((n >= LATE_SLICE) & (side == 1))(lambda: chain(False))
    if slices > LATE_SLICE + 1:
        pl.when((n >= LATE_SLICE) & (side == 0))(lambda: chain(True))
    pl.when(n >= LATE_SLICE)(spread_ends)
    rest()

    drain(len(drains) - 1)
    for transfer in label_hops + label_forwards + lift_hops + edge_hops + rim_hops + start_hops:
        transfer.wait_send()
    for transfer in [shift_hop, front_hop, body_hop] + slab_hops + rest_hops + wide_hops:
        transfer.wait_send()
    for transfer in wide_hops + rest_hops:
        transfer.wait_recv()

    def mix(early, late, begin, finish):
        return (slice_length * float(early)) * begin + (slice_length * float(late)) * finish

    def widen(c, carry):
        for field in range(2):
            for k in range(BLOCK_X):
                spread[field, c, pl.ds(k, rows_c, stride=BLOCK_X)] = delta[field, c]
        for r in range(0, width, chunk):
            at = pl.ds(r, chunk)
            begin, finish = spread[0, c, at], spread[1, c, at]
            place(base, c + 1, r, mix(EARLY[0], LATE[0], begin, finish))
            for row in range(1, STEPS):
                gap, weight = float(GAPS[row]), float(TIMES[row])
                plan[row - 1, c, at] = mix(
                    EARLY[row] - gap * (1.0 - weight), LATE[row] - gap * weight, begin, finish
                )
        return carry

    lax.fori_loop(0, layers_c, widen, 0)
    base[0, inner] = jnp.zeros((width, height), jnp.float32)
    base[layers_c + 1, inner] = jnp.zeros((width, height), jnp.float32)

    def open_step(c, carry):
        for r in range(0, width, 32):
            at, inside = pl.ds(r, 32), pl.ds(PAD + r, 32)
            center = base[c + 1, inside]
            behind = base[c + 1, pl.ds(PAD - 1 + r, 32)]
            level = base[c + 1, pl.ds(PAD + 1 + r, 32)] + sideways(center)
            initial, following = spread[0, c, at], plan[0, c, at]
            for k in range(BLOCK_Z):
                layer = BLOCK_Z * c + k
                under = base[c, inside] if k == 0 else center
                over = base[c + 2, inside] if k == BLOCK_Z - 1 else center
                total = level + (under + over)
                value = initial + (kappa[layer, at] * total + inflow[layer, at] * behind - decay[layer, at] * center)
                nodes[0, layer, at] = value
                place(grid.at[0], layer, r, float(GAPS[1]) * slice_length * value + following)
        return carry

    def wide_each(margin, body, apart):
        if not apart:

            def through(i, carry):
                for r in range(0, width, chunk):
                    body(own - margin + i, None, r)
                return carry

            lax.fori_loop(0, depth + 2 * margin, through, 0, unroll=(depth + 2 * margin) // 2)
            return

        def outer(i, carry):
            layer = own - margin + i + jnp.where(i >= margin, depth, 0)
            for r in range(0, width, chunk):
                body(layer, None, r)
            return carry

        def middle(z, carry):
            for r in range(0, width, chunk):
                body(own + z, z, r)
            return carry

        if margin > 0:
            lax.fori_loop(0, 2 * margin, outer, 0, unroll=min(8, 2 * margin))
        lax.fori_loop(0, depth, middle, 0, unroll=min(8, depth))

    def wide_step(stage):
        sweep, step = stage // STEPS, stage % STEPS
        source, target = grid.at[(stage - 1) % 2], grid.at[stage % 2]
        margin = REACH - 1 - stage
        final = sweep == FINE_SWEEPS - 1
        more = stage < REACH - 1

        def advance(layer, z, r):
            at, c = pl.ds(r, chunk), layer // BLOCK_Z
            if step == 0 or final:
                initial = spread[0, c, at]
            if step == 0:
                before = initial
            else:
                before = latest[layer, at] if final else nodes[step - 1, layer, at]
            value = before + slope(source, layer, layer, r, chunk)
            if final:
                if more:
                    latest[layer, at] = value
                if z is not None:
                    out[step + 1, z, at] = out[step + 1, z, at] + value
                    if step == 0:
                        out[0, z, at] = start[z, at] + initial
            else:
                nodes[step, layer, at] = value
            if not more:
                return
            if not final and step < STEPS - 1:
                total = slice_length * float(GAPS[step + 1]) * value + plan[step, c, at]
            else:
                weights = slice_length * INTEGRALS[(step + 1) % STEPS]
                known = {}
                if final:
                    total = slice_length * float(GAPS[step + 1]) * value + float(weights[0]) * initial
                    weights[step + 1] -= slice_length * GAPS[step + 1]
                else:
                    total = float(weights[0]) * spread[0, c, at]
                    known = {STEPS: value}
                for node in range(1, NODES):
                    part = known[node] if node in known else nodes[node - 1, layer, at]
                    total = total + float(weights[node]) * part
            place(target, layer, r, total)

        wide_each(margin, advance, final)

    lax.fori_loop(0, layers_c, open_step, 0, unroll=3)
    for stage in range(1, STEPS):
        wide_step(stage)
    pair, rest = fine_step(FINE_SWEEPS - 1, STEPS - 1, pair)
    rest()
    drain(len(drains))
    for stage in range(STEPS, REACH):
        wide_step(stage)


def shards(node_fields, region_label, sheet_shift, diffusivity):
    fields = node_fields[0]
    nodes, depth, width, height = fields.shape
    depth_c, rows_c = depth // BLOCK_Z, width // BLOCK_X
    near = -(-REACH // depth)
    layers, layers_c = (2 * near + 1) * depth, (2 * near + 1) * depth_c
    f32 = jnp.float32
    fine, wide = (depth, width, height), (layers, width, height)
    coarse = (depth_c, rows_c, height)
    ringed = (depth_c + 2, rows_c, height)
    padded = width + 2 * PAD
    vmem, hbm = (pl.BlockSpec(memory_space=space) for space in (pltpu.VMEM, pltpu.HBM))
    result = pl.pallas_call(
        kernel,
        out_shape=jax.ShapeDtypeStruct(fields.shape, f32),
        in_specs=[hbm] * 4,
        out_specs=vmem,
        scratch_shapes=[
            pltpu.VMEM(fields.shape, f32),
            pltpu.VMEM(wide, jnp.int32),
            pltpu.VMEM(sheet_shift.shape, jnp.int32),
            pltpu.SMEM(diffusivity.shape, f32),
            pltpu.VMEM(wide, f32),
            pltpu.VMEM(wide, f32),
            pltpu.VMEM(wide, f32),
            pltpu.VMEM(ringed, f32),
            pltpu.VMEM(fine, f32),
            pltpu.VMEM((2, width, height), f32),
            pltpu.VMEM(ringed, f32),
            pltpu.VMEM(sheet_shift.shape, jnp.int32),
            pltpu.VMEM((EXCHANGES, depth + 2, padded, height), f32),
            pltpu.VMEM((STEPS,) + fine, f32),
            pltpu.VMEM(ringed, f32),
            pltpu.VMEM(coarse, f32),
            pltpu.VMEM((2, layers_c, rows_c, height), f32),
            pltpu.VMEM(ringed, f32),
            pltpu.VMEM((2, depth_c, width, height), f32),
            pltpu.VMEM((width, height), f32),
            pltpu.VMEM((2, layers_c, width, height), f32),
            pltpu.VMEM((STEPS - 1, layers_c, width, height), f32),
            pltpu.VMEM((layers_c + 2, padded, height), f32),
            pltpu.VMEM((2, layers, padded, height), f32),
            pltpu.VMEM((STEPS,) + wide, f32),
            pltpu.VMEM(wide, f32),
            pltpu.SemaphoreType.DMA((2 * len(OPENING) + 4,)),
            pltpu.SemaphoreType.DMA((2 * len(OPENING) + 4 * PIECES,)),
            pltpu.SemaphoreType.DMA((8 + 4 * near,)),
            pltpu.SemaphoreType.DMA((8 + 4 * near,)),
            pltpu.SemaphoreType.DMA((3,)),
            pltpu.SemaphoreType.DMA((3,)),
            pltpu.SemaphoreType.DMA((2 * near,)),
            pltpu.SemaphoreType.DMA((2 * near,)),
            pltpu.SemaphoreType.DMA((4,)),
            pltpu.SemaphoreType.DMA((4,)),
            pltpu.SemaphoreType.DMA((4 * near,)),
            pltpu.SemaphoreType.DMA((4 * near,)),
            pltpu.SemaphoreType.DMA((4,)),
        ],
        compiler_params=pltpu.CompilerParams(
            collective_id=0, has_side_effects=True, vmem_limit_bytes=48 * 1024 * 1024,
        ),
    )(*(pltpu.with_memory_space_constraint(x, pltpu.HBM) for x in (fields, region_label, sheet_shift, diffusivity)))
    return result[None]


def solution(mesh):
    in_specs = (P("tm", None, "space", None, None), P("space", None, None), P("tm", None), P())
    out_specs = P("tm", None, "space", None, None)
    return jax.shard_map(shards, mesh=mesh, in_specs=in_specs, out_specs=out_specs, check_vma=False)
```
